128 devices in a mesh: rows: 2 (over core), waves: 64 (over z, y, x).
Axes of the slice: x: 4, y: 4, z: 4, core: 2. Of those that a mesh axis runs over, the one named last changes fastest.
Arguments:
- feats: float32 [32768, 256], P(('rows', 'waves')), may hold values from -6 to 6
- positions: float32 [3, 32768], P(None, ('rows', 'waves')), may hold values from 0 to 6
- cell_counts: int32 [256], P(('rows', 'waves')), may hold values from 1 to 128
- neighbours: int32 [256, 5], P(('rows', 'waves')), may hold values from 0 to 255, as said below
- nbr_count: int32 [256], P(('rows', 'waves')), may hold values from 3 to 5
- kvec: float32 [3, 3072], P(None, 'waves'), may hold values from -4 to 4
- filters: float32 [3072, 256], P('waves'), may hold values from -5 to 5
- w_msg: float32 [256, 256], replicated, may hold values from -0.375 to 0.375
- w_val: float32 [256, 256], replicated, may hold values from -0.375 to 0.375
- w_one: float32 [256, 256], replicated, may hold values from -0.375 to 0.375
- w_two: float32 [256, 256], replicated, may hold values from -0.375 to 0.375
Outputs:
- updated: float32 [32768, 256], P(('rows', 'waves'))
The draws below stay inside these ranges and needn't reach their ends.
Inputs may be any that keep to these rules, and one draw needn't show every extreme that they name: `neighbours`: column 0 of each cell's list is the cell itself, column 1 the cell (c - 2) mod 256, column 2 the cell (c + 2) mod 256; the 5 entries of a list are distinct cells, and every listed cell c' of cell c satisfies (c' - c) mod 256 <= 2 or (c - c') mod 256 <= 2; entries at or beyond nbr_count are in range and unused.
All inputs are finite; a program needn't handle non-finite values.
Results may differ from the reference program's by a relative error of at most 0.0003.
Values sent between devices are 32-bit elements; how exact they have to be, the bound alone decides.
No kernel may reach another device: no remote copies, remote signals or barrier semaphores. Data moves between devices by JAX's collectives and lax.ppermute only.
A program may use at most 128 MiB of HBM per device.

```python
import jax
import jax.numpy as jnp
from jax import lax

F = 256
CELL = 128
NB = 5
KWAVES = 3072
CELLS_DEV = 2
CELLS = 256
SLOTS = 32768
DEVICES = 128


def draw_neighbours(key, part):
    span = 2 * CELLS_DEV + 1
    offs = jnp.arange(span, dtype=jnp.int32) - CELLS_DEV
    scores = jax.random.randint(jax.random.fold_in(key, 17), (CELLS, span), 0, 1 << 20)
    scores = scores * span + jnp.arange(span, dtype=jnp.int32)[None, :]
    scores = jnp.where(offs[None, :] == 0, jnp.int32(3 << 28), scores)
    scores = jnp.where(offs[None, :] == -CELLS_DEV, jnp.int32(2 << 28), scores)
    scores = jnp.where(offs[None, :] == CELLS_DEV, jnp.int32(1 << 28), scores)
    order = jnp.argsort(-scores, axis=1, stable=True)[:, :NB]
    chosen = offs[order]
    own = jnp.arange(CELLS, dtype=jnp.int32)[:, None]
    return ((own + chosen) % CELLS).astype(jnp.int32)


def set_ends(entries, rng, low, high):
    longest = entries.shape.index(max(entries.shape))
    spots = []
    for shift in (0, 1):
        where = [jax.random.randint(jax.random.fold_in(rng, axis), (), 0, length) for axis, length in enumerate(entries.shape)]
        where[longest] = (where[longest] + shift) % entries.shape[longest]
        spots.append(tuple(where))
    return entries.at[spots[0]].set(low).at[spots[1]].set(high)


def shard_levels(key, shape, pieces, low, top_value):
    loudness, own = 1.0, jax.random.fold_in(key, 6)
    for dim, blocks in pieces:
        steps = jnp.exp(jax.random.uniform(jax.random.fold_in(own, dim), (blocks,), jnp.float32, low / len(pieces), top_value / len(pieces)))
        loudness = loudness * jnp.repeat(steps, shape[dim] // blocks).reshape([-1 if axis == dim else 1 for axis in range(len(shape))])
    return loudness


def scatter_about(stream_key, shape, deviation, most, split=(), held_as=jnp.bfloat16):
    result = deviation * jax.random.normal(stream_key, shape, jnp.float32)
    if split:
        result = result * shard_levels(stream_key, shape, split, -0.22, 0.18)
    return jnp.clip(result, -most, most).astype(held_as)


def setup_inputs(seed: int = 0) -> dict:
    seeds = jax.random.split(jax.random.key(seed), 12)
    feats = scatter_about(seeds[0], (SLOTS, F), 1.0, 6.0, ((0, 128),), jnp.float32)
    positions = jnp.clip(6.0 * jax.random.uniform(seeds[1], (3, SLOTS), jnp.float32) ** shard_levels(seeds[1], (3, SLOTS), ((1, 128),), -0.2, 0.2), 0.0, 6.0)
    cell_counts = set_ends(jax.random.randint(seeds[2], (CELLS,), 1, CELL + 1), jax.random.fold_in(seeds[2], 1), 1, CELL).astype(jnp.int32)
    neighbours = draw_neighbours(jax.random.fold_in(seeds[11], 71), 0)
    nbr_count = set_ends(jax.random.randint(seeds[4], (CELLS,), 3, NB + 1), jax.random.fold_in(seeds[4], 1), 3, NB).astype(jnp.int32)
    kvec = scatter_about(seeds[5], (3, KWAVES), 1.0, 4.0, ((1, 64),), jnp.float32)
    filters = scatter_about(seeds[6], (KWAVES, F), 1.0, 5.0, ((0, 64),), jnp.float32)
    w_msg = scatter_about(seeds[7], (F, F), F ** -0.5, 0.375, (), jnp.float32)
    w_val = scatter_about(seeds[8], (F, F), F ** -0.5, 0.375, (), jnp.float32)
    w_one = scatter_about(seeds[9], (F, F), F ** -0.5, 0.375, (), jnp.float32)
    w_two = scatter_about(seeds[10], (F, F), F ** -0.5, 0.375, (), jnp.float32)
    return {"feats": feats, "positions": positions, "cell_counts": cell_counts, "neighbours": neighbours, "nbr_count": nbr_count, "kvec": kvec, "filters": filters, "w_msg": w_msg, "w_val": w_val, "w_one": w_one, "w_two": w_two}


HIGH = lax.Precision.HIGHEST

def reference(feats, positions, cell_counts, neighbours, nbr_count, kvec, filters, w_msg, w_val, w_one, w_two):
    slot_ids = jnp.arange(CELL, dtype=jnp.int32)
    valid2 = (slot_ids[None, :] < cell_counts[:, None]).astype(jnp.float32)
    valid = valid2.reshape(-1)
    hw = jnp.dot(feats, w_msg, precision=HIGH)
    vals = jnp.dot(feats, w_val, precision=HIGH) * valid[:, None]
    pos3 = positions.reshape(3, CELLS, CELL)
    hw3 = hw.reshape(CELLS, CELL, F)
    same_slot = jnp.eye(CELL, dtype=jnp.bool_)

    def one_cell(c):
        own = pos3[:, c]
        acc = jnp.zeros((CELL, F), jnp.float32)
        for b in range(NB):
            other = neighbours[c, b]
            near = pos3[:, other]
            dist = lax.optimization_barrier(jnp.sum((own[:, :, None] - near[:, None, :]) ** 2, axis=0))
            live = (b < nbr_count[c]).astype(jnp.float32)
            keep = valid2[c][:, None] * valid2[other][None, :] * live
            weight = jnp.where(same_slot & (other == c), 0.0, jnp.exp(-0.125 * dist) * keep)
            acc = acc + jnp.dot(weight, hw3[other], precision=HIGH)
        return acc
    msg = 0.125 * lax.map(one_cell, jnp.arange(CELLS, dtype=jnp.int32)).reshape(SLOTS, F)
    block = SLOTS // DEVICES
    pos_blocks = positions.reshape(3, DEVICES, block).transpose(1, 0, 2)
    val_blocks = vals.reshape(DEVICES, block, F)

    def forward(carry, item):
        pos_b, val_b = item
        phase = jnp.dot(kvec.T, pos_b, precision=HIGH)
        return ((carry[0] + jnp.dot(jnp.cos(phase), val_b, precision=HIGH), carry[1] + jnp.dot(jnp.sin(phase), val_b, precision=HIGH)), None)
    zero = jnp.zeros((KWAVES, F), jnp.float32)
    (sum_cos, sum_sin), _ = lax.scan(forward, (zero, zero), (pos_blocks, val_blocks))
    filt_cos = filters * sum_cos
    filt_sin = filters * sum_sin

    def backward(pos_b):
        phase = jnp.dot(pos_b.T, kvec, precision=HIGH)
        return jnp.dot(jnp.cos(phase), filt_cos, precision=HIGH) + jnp.dot(jnp.sin(phase), filt_sin, precision=HIGH)
    ewald = lax.map(backward, pos_blocks).reshape(SLOTS, F) / jnp.sqrt(jnp.float32(SLOTS) * jnp.float32(KWAVES))
    total = feats + msg + ewald
    normed = total / jnp.sqrt(lax.optimization_barrier(jnp.mean(total * total, axis=1, keepdims=True)) + 1e-06)
    hidden = jax.nn.silu(jnp.dot(normed, w_one, precision=HIGH))
    return (total + jnp.dot(hidden, w_two, precision=HIGH)) * valid[:, None]
```

```python
import math

import jax
import jax.numpy as jnp
from jax import lax
from jax.experimental import pallas as pl
from jax.experimental.pallas import tpu as pltpu
from jax.sharding import Mesh
from jax.sharding import PartitionSpec as P

Z, Y, X = "waves_0", "waves_1", "waves_2"
WAVES = (Z, Y, X)
ROWS_WAVES = ("rows", Z, Y, X)
F32 = jnp.float32
BF16 = jnp.bfloat16

SIN_POLY = (6.283185280154403, -10.33542015333633, 5.100154773052372, -1.1965808225334407, 0.15531182448662934)
COS_POLY = (0.9999999997791529, -4.934802136928833, 4.058709154760502, -1.335211949366169, 0.23493706849740192, -0.0243959319559508)


def horner(coeffs, u):
    out = coeffs[-1]
    for c in coeffs[-2::-1]:
        out = out * u + c
    return out


def split(a):
    high = a.astype(BF16)
    return high, (a - high.astype(F32)).astype(BF16)


def dot(a, b):
    return jnp.dot(a, b, preferred_element_type=F32)


def dot3(a, b):
    return dot(a[0], b[0]) + (dot(a[1], b[0]) + dot(a[0], b[1]))


def call(kernel, outs, scratch=(), smem=(), n_in=0, limit=40 << 20):
    return pl.pallas_call(
        kernel,
        out_shape=outs,
        in_specs=[
            pl.BlockSpec(memory_space=pltpu.SMEM if i in smem else pltpu.VMEM) for i in range(n_in)
        ],
        out_specs=jax.tree.map(lambda _: pl.BlockSpec(memory_space=pltpu.VMEM), outs),
        scratch_shapes=scratch,
        compiler_params=pltpu.CompilerParams(vmem_limit_bytes=limit),
    )


def live_rows(counts, cells, cell):
    row = lax.broadcasted_iota(jnp.int32, (cells * cell, 1), 0)
    limit = jnp.full(row.shape, counts[0])
    for c in range(1, cells):
        limit = jnp.where(row >= c * cell, c * cell + counts[c], limit)
    return row < limit


def prepare(cells, cell):
    slots = cells * cell

    def kernel(counts, feats, positions, out):
        out[:slots] = jnp.where(live_rows(counts, cells, cell), feats[...], 0.0)
        out[slots:] = jnp.zeros((8, out.shape[1]), F32)
        out[slots : slots + 3] = positions[...]

    return kernel


def forward(slots, count, waves, first):
    block = 48

    def kernel(kt, w_val, *refs):
        chunks, refs = refs[:count], refs[count:]
        if not first:
            before, refs = refs[0], refs[1:]
        out, ch, cl, sh, sl, acc_c, acc_s = refs
        w = split(w_val[...])
        for j, chunk in enumerate(chunks):
            v = split(dot3(split(chunk[:slots]), w))
            px = chunk[slots : slots + 1]
            py = chunk[slots + 1 : slots + 2]
            pz = chunk[slots + 2 : slots + 3]

            def body(i, carry, j=j, px=px, py=py, pz=pz):
                rows = pl.ds(pl.multiple_of(i * block, block), block)
                k = kt[rows, :]
                t = k[:, 0:1] * px + k[:, 1:2] * py + k[:, 2:3] * pz
                f = t - jnp.round(t)
                u = f * f
                s = f * horner(SIN_POLY, u)
                c = horner(COS_POLY, u)
                ch[j, rows, :], cl[j, rows, :] = split(1.0 - 0.5 * (s * s))
                sh[j, rows, :], sl[j, rows, :] = split(s * c)
                return carry

            lax.fori_loop(0, waves // block, body, 0)
            part_c = dot3((ch[j], cl[j]), v)
            part_s = dot3((sh[j], sl[j]), v)
            if j == 0:
                acc_c[...] = part_c
                acc_s[...] = part_s
            else:
                acc_c[...] += part_c
                acc_s[...] += part_s
        own = out.shape[2]
        total_c = acc_c[...].reshape(-1, own, out.shape[3])
        total_s = acc_s[...].reshape(-1, own, out.shape[3])
        if first:
            out[:, 0] = total_c
            out[:, 1] = total_s
        else:
            out[:, 0] = before[:, 0] + total_c
            out[:, 1] = before[:, 1] + total_s

    return kernel


def filtered(scale):
    def kernel(half, parts, filters, out):
        groups, _, own, _ = parts.shape
        f = filters[pl.ds(pl.multiple_of(half[0] * own, 8), own), :] * scale
        for i in range(2):
            total = parts[0, i]
            for g in range(1, groups):
                total = total + parts[g, i]
            total = total * f
            for g in range(groups):
                out[g, i] = total

    return kernel


def backward(count, waves):
    def kernel(f, ch, cl, sh, sl, out):
        fc = split(f[:, 0].reshape(waves, -1).T)
        fs = split(f[:, 1].reshape(waves, -1).T)
        for j in range(count):
            out[j] = dot3(fc, (ch[j], cl[j])) + dot3(fs, (sh[j], sl[j]))

    return kernel


def messages(cells, cell, cells_all, nb):
    slots = cells * cell

    def kernel(place, neighbours, nbr_count, own, low, high, edge, w_msg, out):
        x, last, first = place[0], place[1], place[2]
        lo = jnp.where(x == 0, edge[...], low[...])
        hi = jnp.where(x == last, edge[...], high[...])
        blocks = (lo, own[...], hi)
        parts = [split(b[:slots]) for b in blocks]
        wide = [tuple(p[k][c * cell : (c + 1) * cell] for k in range(2)) for p in parts for c in range(cells)]
        pos = [
            b[slots : slots + 3, c * cell : (c + 1) * cell] for b in blocks for c in range(cells)
        ]
        cols = own[slots : slots + 8].T
        eye = lax.broadcasted_iota(jnp.int32, (cell, cell), 0) == lax.broadcasted_iota(jnp.int32, (cell, cell), 1)
        gathered = []
        for c in range(cells):
            mine = cols[c * cell : (c + 1) * cell]
            acc = None
            for step in range(2 * cells + 1):
                other = c + step
                local = other - cells
                target = lax.rem(first + local + cells_all, cells_all)
                listed = jnp.float32(0.0)
                for b in range(nb):
                    hit = (neighbours[c, b] == target) & (b < nbr_count[c])
                    listed = listed + jnp.where(hit, jnp.float32(1.0), jnp.float32(0.0))
                near = pos[other]
                d0 = mine[:, 0:1] - near[0:1]
                d1 = mine[:, 1:2] - near[1:2]
                d2 = mine[:, 2:3] - near[2:3]
                weight = jnp.exp(-0.125 * (d0 * d0 + d1 * d1 + d2 * d2)) * listed
                if step == cells:
                    weight = jnp.where(eye, 0.0, weight)
                part = dot3(split(weight), wide[other])
                acc = part if acc is None else acc + part
            gathered.append(acc)
        total = jnp.concatenate(gathered, axis=0)
        out[...] = 0.125 * dot3(split(total), split(w_msg[...]))

    return kernel


def finish(cells, cell):
    def kernel(counts, feats, msg, own, swap, a, b, c, w_one, w_two, out):
        live = live_rows(counts, cells, cell)
        spectral = ((own[...] + swap[...]) + (a[...] + b[...])) + c[...]
        u = feats[...] + jnp.where(live, msg[...], 0.0) + spectral.T
        normed = u / jnp.sqrt(jnp.mean(u * u, axis=1, keepdims=True) + 1e-06)
        v = dot3(split(normed), split(w_one[...]))
        hidden = v / (1.0 + jnp.exp(-v))
        res = u + dot3(split(hidden), split(w_two[...]))
        out[...] = jnp.where(live, res, 0.0)

    return kernel


def shift(axis, by):
    size = lax.axis_size(axis)
    return [(i, (i + by) % size) for i in range(size)]


def shards(
    feats, positions, cell_counts, neighbours, nbr_count, kvec, filters, w_msg, w_val, w_one, w_two
):
    cells = cell_counts.shape[0]
    slots, width = feats.shape
    cell = slots // cells
    devices = lax.axis_size(ROWS_WAVES)
    nx = lax.axis_size(X)
    rows = lax.axis_size("rows")
    group = lax.axis_size((Z, Y))
    own_waves = kvec.shape[1] // rows
    waves = own_waves * group
    half = lax.axis_index("rows").astype(jnp.int32)
    x = lax.axis_index(X).astype(jnp.int32)
    first = lax.axis_index(ROWS_WAVES).astype(jnp.int32) * cells

    tall = slots + 8
    payload = call(prepare(cells, cell), jax.ShapeDtypeStruct((tall, width), F32), smem=(0,), n_in=3)(
        cell_counts, feats, positions
    )
    near2 = lax.ppermute(payload, X, shift(X, 2))
    above = lax.ppermute(payload, X, shift(X, -1))
    below = lax.ppermute(payload, X, shift(X, 1))
    ends = [(d, (d + 1) % devices) for d in range(devices) if d % nx == nx - 1]
    ends = ends + [(b, a) for a, b in ends]
    edge = lax.ppermute(payload, ROWS_WAVES, ends)

    kt = lax.dynamic_slice_in_dim(kvec.T, half * own_waves, own_waves, 0) * (0.5 / math.pi)
    kt = jnp.pad(kt, ((0, 0), (0, 128 - kt.shape[1])))
    kt = lax.all_to_all(jnp.broadcast_to(kt[None], (group, *kt.shape)), (Z, Y), 0, 0, tiled=True)
    kt = kt.reshape(waves, 128)

    line = (payload, above, below, near2)
    other = tuple(lax.ppermute(c, "rows", shift("rows", 1)) for c in line)
    count = len(line)
    wide = jax.ShapeDtypeStruct((count, waves, slots), BF16)
    sums = jax.ShapeDtypeStruct((group, 2, own_waves, width), F32)
    acc = [pltpu.VMEM((waves, width), F32)] * 2
    part, *mine = call(forward(slots, count, waves, True), (sums,) + (wide,) * 4, acc, n_in=2 + count)(
        kt, w_val, *line
    )
    part, *theirs = call(forward(slots, count, waves, False), (sums,) + (wide,) * 4, acc, n_in=3 + count)(
        kt, w_val, *other, part
    )
    parts = lax.all_to_all(part, (Z, Y), 0, 0, tiled=True)
    scale = 1.0 / math.sqrt(float(slots * devices) * float(waves * rows * nx))
    spread = call(filtered(scale), sums, smem=(0,), n_in=3)(half.reshape(1), parts, filters)
    f = lax.all_to_all(spread, (Z, Y), 0, 0, tiled=True)

    back = call(backward(count, waves), jax.ShapeDtypeStruct((count, width, slots), F32), n_in=5)
    swap = lax.ppermute(back(f, *theirs), "rows", shift("rows", 1))
    own = back(f, *mine)
    e1 = lax.ppermute(own[1] + swap[1], X, shift(X, 1))
    e2 = lax.ppermute(own[2] + swap[2], X, shift(X, -1))
    e3 = lax.ppermute(own[3] + swap[3], X, shift(X, 2))

    place = jnp.stack([x, jnp.int32(nx - 1), first])
    msg = call(
        messages(cells, cell, cells * devices, neighbours.shape[1]),
        jax.ShapeDtypeStruct((slots, width), F32),
        smem=(0, 1, 2),
        n_in=8,
    )(place, neighbours, nbr_count, payload, below, above, edge, w_msg)
    return call(finish(cells, cell), jax.ShapeDtypeStruct((slots, width), F32), smem=(0,), n_in=10)(
        cell_counts, feats, msg, own[0], swap[0], e1, e2, e3, w_one, w_two
    )


def solution(mesh):
    torus = Mesh(mesh.devices.reshape(mesh.shape["rows"], 4, 4, 4), ROWS_WAVES)
    return jax.shard_map(
        shards,
        mesh=torus,
        in_specs=(
            P(ROWS_WAVES, None),
            P(None, ROWS_WAVES),
            P(ROWS_WAVES),
            P(ROWS_WAVES, None),
            P(ROWS_WAVES),
            P(None, WAVES),
            P(WAVES, None),
            P(),
            P(),
            P(),
            P(),
        ),
        out_specs=P(ROWS_WAVES, None),
        check_vma=False,
    )
```

```python
import math

import jax
import jax.numpy as jnp
from jax import lax
from jax.experimental import pallas as pl
from jax.experimental.pallas import tpu as pltpu
from jax.sharding import Mesh
from jax.sharding import PartitionSpec as P

Z, Y, X = "waves_0", "waves_1", "waves_2"
WAVES = (Z, Y, X)
ROWS_WAVES = ("rows", Z, Y, X)
F32 = jnp.float32
BF16 = jnp.bfloat16

SIN_POLY = (6.283185280154403, -10.33542015333633, 5.100154773052372, -1.1965808225334407, 0.15531182448662934)
COS_POLY = (0.9999999997791529, -4.934802136928833, 4.058709154760502, -1.335211949366169, 0.23493706849740192, -0.0243959319559508)
ROUNDER = 12582912.0


def horner(coeffs, u):
    out = coeffs[-1]
    for c in coeffs[-2::-1]:
        out = out * u + c
    return out


def split(a):
    high = a.astype(BF16)
    return high, (a - high.astype(F32)).astype(BF16)


def thirds(a):
    high = a.astype(BF16).astype(F32)
    rest = a - high
    middle = rest.astype(BF16).astype(F32)
    return high, middle, rest - middle


def dot(a, b):
    return jnp.dot(a, b, preferred_element_type=F32)


def dot3(a, b):
    return dot(a[0], b[0]) + (dot(a[1], b[0]) + dot(a[0], b[1]))


def call(kernel, outs, n_in, scratch=(), smem=(), hbm=(), limit=40 << 20):
    def space(i):
        return pltpu.SMEM if i in smem else pltpu.HBM if i in hbm else pltpu.VMEM

    return pl.pallas_call(
        kernel,
        out_shape=outs,
        in_specs=[pl.BlockSpec(memory_space=space(i)) for i in range(n_in)],
        out_specs=jax.tree.map(lambda _: pl.BlockSpec(memory_space=pltpu.VMEM), outs),
        scratch_shapes=scratch,
        compiler_params=pltpu.CompilerParams(vmem_limit_bytes=limit),
    )


def live_rows(counts, cells, cell):
    row = lax.broadcasted_iota(jnp.int32, (cells * cell, 1), 0)
    limit = jnp.full(row.shape, counts[0])
    for c in range(1, cells):
        limit = jnp.where(row >= c * cell, c * cell + counts[c], limit)
    return row < limit


def prepare(cells, cell):
    slots = cells * cell

    def kernel(counts, feats, positions, out, counts_s, pos_s, sems):
        copies = [
            pltpu.make_async_copy(counts, counts_s, sems.at[0]),
            pltpu.make_async_copy(positions, pos_s, sems.at[1]),
            pltpu.make_async_copy(feats, out.at[pl.ds(0, slots)], sems.at[2]),
        ]
        for c in copies:
            c.start()
        for c in copies:
            c.wait()
        out[:slots] = jnp.where(live_rows(counts_s, cells, cell), out[:slots], 0.0)
        out[slots:] = jnp.zeros((8, out.shape[1]), F32)
        out[slots : slots + 3] = pos_s[...]

    return kernel


def forward(slots, count, own, groups, first):
    def kernel(kt, w_val, *refs):
        chunks, refs = refs[:count], refs[count:]
        if not first:
            before, refs = refs[0], refs[1:]
        out, mh, ml = refs
        w = split(w_val[...])
        kh, km, kl = thirds(kt[...])
        lhs = kh
        for at, part in enumerate((kh, km, kh, km, kl)):
            lhs = lhs + pltpu.roll(part, 8 * (at + 1), 1)
        lhs = lhs[:, :48].astype(BF16)
        for j, chunk in enumerate(chunks):
            v = split(dot3(split(chunk[:slots]), w))
            ph, pm, pl_ = thirds(chunk[slots : slots + 8])
            turns = dot(lhs, jnp.concatenate([ph, pm, ph, pl_, pm, ph], axis=0).astype(BF16))
            for g in range(groups):
                t = turns[g * own : (g + 1) * own]
                f = t - ((t + ROUNDER) - ROUNDER)
                u = f * f
                s = f * horner(SIN_POLY, u)
                c = horner(COS_POLY, u)
                both = jnp.concatenate([1.0 - 0.5 * (s * s), s * c], axis=0)
                rows = slice(2 * own * g, 2 * own * (g + 1))
                mh[j, rows], ml[j, rows] = split(both)
            part = dot3((mh[j], ml[j]), v)
            if j:
                out[...] += part
            elif first:
                out[...] = part
            else:
                out[...] = before[...] + part

    return kernel


def filtered(scale):
    def kernel(half, parts, filters, out):
        groups, double, _ = parts.shape
        own = double // 2
        f = filters[pl.ds(pl.multiple_of(half[0] * own, 8), own), :] * scale
        total = parts[0]
        for g in range(1, groups):
            total = total + parts[g]
        total = total * jnp.concatenate([f, f], axis=0)
        for g in range(groups):
            out[g] = total

    return kernel


def backward(count):
    def kernel(f, mh, ml, out):
        ft = split(f[...].T)
        for j in range(count):
            out[j] = dot3(ft, (mh[j], ml[j]))

    return kernel


def messages(cells, cell, cells_all, nb):
    slots = cells * cell

    def kernel(place, neighbours, nbr_count, counts, feats, own, low, high, edge, w_msg, out, mask):
        x, last, first = place[0], place[1], place[2]
        lo = jnp.where(x == 0, edge[...], low[...])
        hi = jnp.where(x == last, edge[...], high[...])
        blocks = (lo, own[...], hi)
        parts = [split(b[:slots]) for b in blocks]
        wide = [tuple(p[k][c * cell : (c + 1) * cell] for k in range(2)) for p in parts for c in range(cells)]
        pos = [
            b[slots : slots + 3, c * cell : (c + 1) * cell] for b in blocks for c in range(cells)
        ]
        cols = own[slots : slots + 8].T
        eye = lax.broadcasted_iota(jnp.int32, (cell, cell), 0) == lax.broadcasted_iota(jnp.int32, (cell, cell), 1)
        gathered = []
        for c in range(cells):
            mine = cols[c * cell : (c + 1) * cell]
            acc = None
            for step in range(2 * cells + 1):
                other = c + step
                local = other - cells
                target = lax.rem(first + local + cells_all, cells_all)
                listed = jnp.float32(0.0)
                for b in range(nb):
                    hit = (neighbours[c, b] == target) & (b < nbr_count[c])
                    listed = listed + jnp.where(hit, jnp.float32(1.0), jnp.float32(0.0))
                near = pos[other]
                d0 = mine[:, 0:1] - near[0:1]
                d1 = mine[:, 1:2] - near[1:2]
                d2 = mine[:, 2:3] - near[2:3]
                weight = jnp.exp(-0.125 * (d0 * d0 + d1 * d1 + d2 * d2)) * listed
                if step == cells:
                    weight = jnp.where(eye, 0.0, weight)
                part = dot3(split(weight), wide[other])
                acc = part if acc is None else acc + part
            gathered.append(acc)
        total = jnp.concatenate(gathered, axis=0)
        live = live_rows(counts, cells, cell)
        msg = 0.125 * dot3(split(total), split(w_msg[...]))
        out[...] = feats[...] + jnp.where(live, msg, 0.0)
        mask[...] = jnp.broadcast_to(jnp.where(live, 1.0, 0.0), mask.shape)

    return kernel


def finish():
    def kernel(base, mask, own, swap, a, b, c, w_one, w_two, out):
        spectral = ((own[...] + swap[...]) + (a[...] + b[...])) + c[...]
        u = base[...] + spectral.T
        normed = u / jnp.sqrt(jnp.mean(u * u, axis=1, keepdims=True) + 1e-06)
        v = dot3(split(normed), split(w_one[...]))
        hidden = v / (1.0 + jnp.exp(-v))
        out[...] = (u + dot3(split(hidden), split(w_two[...]))) * mask[:, 0:1]

    return kernel


def shift(axis, by):
    size = lax.axis_size(axis)
    return [(i, (i + by) % size) for i in range(size)]


def shards(
    feats, positions, cell_counts, neighbours, nbr_count, kvec, filters, w_msg, w_val, w_one, w_two
):
    cells = cell_counts.shape[0]
    slots, width = feats.shape
    cell = slots // cells
    devices = lax.axis_size(ROWS_WAVES)
    nx = lax.axis_size(X)
    rows = lax.axis_size("rows")
    group = lax.axis_size((Z, Y))
    own_waves = kvec.shape[1] // rows
    waves = own_waves * group
    half = lax.axis_index("rows").astype(jnp.int32)
    x = lax.axis_index(X).astype(jnp.int32)
    first = lax.axis_index(ROWS_WAVES).astype(jnp.int32) * cells

    tall = slots + 8
    payload = call(
        prepare(cells, cell),
        jax.ShapeDtypeStruct((tall, width), F32),
        3,
        [pltpu.SMEM((cells,), jnp.int32), pltpu.VMEM((3, slots), F32), pltpu.SemaphoreType.DMA((3,))],
        hbm=(0, 1, 2),
    )(cell_counts, feats, positions)
    near2 = lax.ppermute(payload, X, shift(X, 2))
    above = lax.ppermute(payload, X, shift(X, -1))
    below = lax.ppermute(payload, X, shift(X, 1))
    ends = [(d, (d + 1) % devices) for d in range(devices) if d % nx == nx - 1]
    ends = ends + [(b, a) for a, b in ends]
    edge = lax.ppermute(payload, ROWS_WAVES, ends)
    other = [lax.ppermute(payload, "rows", shift("rows", 1))]

    kt = lax.dynamic_slice_in_dim(kvec.T, half * own_waves, own_waves, 0) * (0.5 / math.pi)
    kt = jnp.pad(kt, ((0, 0), (0, 128 - kt.shape[1])))
    kt = lax.all_to_all(jnp.broadcast_to(kt[None], (group, *kt.shape)), (Z, Y), 0, 0, tiled=True)
    kt, near2, above, below, edge = lax.optimization_barrier((kt, near2, above, below, edge))
    kt = kt.reshape(waves, 128)

    line = (payload, above, below, near2)
    other += [lax.ppermute(c, "rows", shift("rows", 1)) for c in line[1:]]
    count = len(line)
    wide = jax.ShapeDtypeStruct((count, 2 * waves, slots), BF16)
    sums = jax.ShapeDtypeStruct((2 * waves, width), F32)
    part, *mine = call(forward(slots, count, own_waves, group, True), (sums, wide, wide), 2 + count)(
        kt, w_val, *line
    )
    part, *theirs = call(forward(slots, count, own_waves, group, False), (sums, wide, wide), 3 + count)(
        kt, w_val, *other, part
    )
    parts = lax.all_to_all(part.reshape(group, 2 * own_waves, width), (Z, Y), 0, 0, tiled=True)
    scale = 1.0 / math.sqrt(float(slots * devices) * float(waves * rows * nx))
    spread = call(filtered(scale), jax.ShapeDtypeStruct(parts.shape, F32), 3, smem=(0,))(
        half.reshape(1), parts, filters
    )
    f = lax.all_to_all(spread, (Z, Y), 0, 0, tiled=True).reshape(2 * waves, width)

    back = call(backward(count), jax.ShapeDtypeStruct((count, width, slots), F32), 3)
    swap = lax.ppermute(back(f, *theirs), "rows", shift("rows", 1))
    own = back(f, *mine)
    e3 = lax.ppermute(own[3] + swap[3], X, shift(X, 2))
    e1 = lax.ppermute(own[1] + swap[1], X, shift(X, 1))
    e2 = lax.ppermute(own[2] + swap[2], X, shift(X, -1))

    place = jnp.stack([x, jnp.int32(nx - 1), first])
    base, mask = call(
        messages(cells, cell, cells * devices, neighbours.shape[1]),
        (jax.ShapeDtypeStruct((slots, width), F32), jax.ShapeDtypeStruct((slots, 128), F32)),
        10,
        smem=(0, 1, 2, 3),
    )(place, neighbours, nbr_count, cell_counts, feats, payload, below, above, edge, w_msg)
    return call(finish(), jax.ShapeDtypeStruct((slots, width), F32), 9)(
        base, mask, own[0], swap[0], e1, e2, e3, w_one, w_two
    )


def solution(mesh):
    torus = Mesh(mesh.devices.reshape(mesh.shape["rows"], 4, 4, 4), ROWS_WAVES)
    return jax.shard_map(
        shards,
        mesh=torus,
        in_specs=(
            P(ROWS_WAVES, None),
            P(None, ROWS_WAVES),
            P(ROWS_WAVES),
            P(ROWS_WAVES, None),
            P(ROWS_WAVES),
            P(None, WAVES),
            P(WAVES, None),
            P(),
            P(),
            P(),
            P(),
        ),
        out_specs=P(ROWS_WAVES, None),
        check_vma=False,
    )
```

```python
import math

import jax
import jax.numpy as jnp
from jax import lax
from jax.experimental import pallas as pl
from jax.experimental.pallas import tpu as pltpu
from jax.sharding import Mesh
from jax.sharding import PartitionSpec as P

Z, Y, X = "waves_0", "waves_1", "waves_2"
WAVES = (Z, Y, X)
ROWS_WAVES = ("rows", Z, Y, X)
F32 = jnp.float32
BF16 = jnp.bfloat16

SIN_POLY = (6.283185280154403, -10.33542015333633, 5.100154773052372, -1.1965808225334407, 0.15531182448662934)
COS_POLY = (0.9999999997791529, -4.934802136928833, 4.058709154760502, -1.335211949366169, 0.23493706849740192, -0.0243959319559508)
ROUNDER = 12582912.0


def horner(coeffs, u):
    out = coeffs[-1]
    for c in coeffs[-2::-1]:
        out = out * u + c
    return out


def split(a):
    high = a.astype(BF16)
    return high, (a - high.astype(F32)).astype(BF16)


def thirds(a):
    high = a.astype(BF16).astype(F32)
    rest = a - high
    middle = rest.astype(BF16).astype(F32)
    return high, middle, rest - middle


def dot(a, b):
    return jnp.dot(a, b, preferred_element_type=F32)


def dot3(a, b):
    return dot(a[0], b[0]) + (dot(a[1], b[0]) + dot(a[0], b[1]))


def call(kernel, outs, n_in, scratch=(), smem=(), hbm=(), limit=40 << 20):
    def space(i):
        return pltpu.SMEM if i in smem else pltpu.HBM if i in hbm else pltpu.VMEM

    return pl.pallas_call(
        kernel,
        out_shape=outs,
        in_specs=[pl.BlockSpec(memory_space=space(i)) for i in range(n_in)],
        out_specs=jax.tree.map(lambda _: pl.BlockSpec(memory_space=pltpu.VMEM), outs),
        scratch_shapes=scratch,
        compiler_params=pltpu.CompilerParams(vmem_limit_bytes=limit),
    )


def live_rows(counts, cells, cell):
    row = lax.broadcasted_iota(jnp.int32, (cells * cell, 1), 0)
    limit = jnp.full(row.shape, counts[0])
    for c in range(1, cells):
        limit = jnp.where(row >= c * cell, c * cell + counts[c], limit)
    return row < limit


def assemble(own):
    def kernel(z, a, b, c, d, kt, filters, kv):
        kv[...] = jnp.zeros(kv.shape, F32)
        for j, ref in enumerate((a, b, c, d)):
            home = lax.rem(z[0] + j, 4)
            filters[pl.ds(pl.multiple_of(home * own, 8), own), :] = ref[:own]
            kv[...] += pltpu.roll(ref[own : own + 8, :128], home * own, 1)
        kt[...] = jnp.zeros(kt.shape, F32)
        kt[:, 0:8] = kv[...].T[: 4 * own]

    return kernel


def values(slots):
    def kernel(w_val, *refs):
        chunks, (vh, vl, where) = refs[:4], refs[4:]
        w = split(w_val[...])
        for j, chunk in enumerate(chunks):
            vh[j], vl[j] = split(dot3(split(chunk[:slots]), w))
            ph, pm, pl_ = thirds(chunk[slots : slots + 8])
            where[j] = jnp.concatenate([ph, pm, ph, pl_, pm, ph], axis=0).astype(BF16)

    return kernel


def forward(own):
    def kernel(ka, kb, vh0, vl0, at0, vh1, vl1, at1, sa, sb, mh0, ml0, mh1, ml1, acc):
        half = ka.shape[0]
        kh, km, kl = thirds(jnp.concatenate([ka[...], kb[...]], axis=0))
        lhs = kh
        for at, part in enumerate((kh, km, kh, km, kl)):
            lhs = lhs + pltpu.roll(part, 8 * (at + 1), 1)
        lhs = lhs[:, :48].astype(BF16)
        sides = ((vh0, vl0, at0, mh0, ml0), (vh1, vl1, at1, mh1, ml1))
        for side, (vh, vl, where, mh, ml) in enumerate(sides):
            for j in range(4):
                turns = dot(lhs, where[j])
                for g in range(2 * half // own):
                    t = turns[g * own : (g + 1) * own]
                    f = t - ((t + ROUNDER) - ROUNDER)
                    u = f * f
                    s = f * horner(SIN_POLY, u)
                    c = horner(COS_POLY, u)
                    both = jnp.concatenate([1.0 - 0.5 * (s * s), s * c], axis=0)
                    rows = slice(2 * own * g, 2 * own * (g + 1))
                    mh[j, rows], ml[j, rows] = split(both)
                part = dot3((mh[j], ml[j]), (vh[j], vl[j]))
                if side or j:
                    acc[...] += part
                else:
                    acc[...] = part
        sa[...] = acc[: 2 * half]
        sb[...] = acc[2 * half :]

    return kernel


def four(a, b, c, d, out):
    out[...] = (a[...] + b[...]) + (c[...] + d[...])


def filtered(own):
    def kernel(a, b, c, d, filters, out):
        total = (a[...] + b[...]) + (c[...] + d[...])
        for g in range(total.shape[0] // (2 * own)):
            f = filters[g * own : (g + 1) * own]
            for k in range(2):
                rows = slice((2 * g + k) * own, (2 * g + k + 1) * own)
                out[rows] = total[rows] * f

    return kernel


def backward(fa, fb, fc, fd, mha, mla, mhb, mlb, out):
    ft = split(jnp.concatenate([fa[...], fb[...], fc[...], fd[...]], axis=0).T)
    for j in range(out.shape[0]):
        mh = jnp.concatenate([mha[j], mhb[j]], axis=0)
        ml = jnp.concatenate([mla[j], mlb[j]], axis=0)
        out[j] = dot3(ft, (mh, ml))


def pairs(a, b, *outs):
    for j, out in enumerate(outs):
        out[...] = a[j] + b[j]


def messages(cells, cell, cells_all, nb):
    slots = cells * cell

    def kernel(place, neighbours, nbr_count, counts, feats, own, low, high, edge, w_msg, out, mask):
        x, last, first = place[0], place[1], place[2]
        lo = jnp.where(x == 0, edge[...], low[...])
        hi = jnp.where(x == last, edge[...], high[...])
        blocks = (lo, own[...], hi)
        parts = [split(b[:slots]) for b in blocks]
        wide = [tuple(p[k][c * cell : (c + 1) * cell] for k in range(2)) for p in parts for c in range(cells)]
        pos = [
            b[slots : slots + 3, c * cell : (c + 1) * cell] for b in blocks for c in range(cells)
        ]
        cols = own[slots : slots + 8].T
        eye = lax.broadcasted_iota(jnp.int32, (cell, cell), 0) == lax.broadcasted_iota(jnp.int32, (cell, cell), 1)
        gathered = []
        for c in range(cells):
            mine = cols[c * cell : (c + 1) * cell]
            acc = None
            for step in range(2 * cells + 1):
                other = c + step
                local = other - cells
                target = lax.rem(first + local + cells_all, cells_all)
                listed = jnp.float32(0.0)
                for b in range(nb):
                    hit = (neighbours[c, b] == target) & (b < nbr_count[c])
                    listed = listed + jnp.where(hit, jnp.float32(1.0), jnp.float32(0.0))
                near = pos[other]
                d0 = mine[:, 0:1] - near[0:1]
                d1 = mine[:, 1:2] - near[1:2]
                d2 = mine[:, 2:3] - near[2:3]
                weight = jnp.exp(-0.125 * (d0 * d0 + d1 * d1 + d2 * d2)) * listed
                if step == cells:
                    weight = jnp.where(eye, 0.0, weight)
                part = dot3(split(weight), wide[other])
                acc = part if acc is None else acc + part
            gathered.append(acc)
        total = jnp.concatenate(gathered, axis=0)
        live = live_rows(counts, cells, cell)
        msg = 0.125 * dot3(split(total), split(w_msg[...]))
        out[...] = feats[...] + jnp.where(live, msg, 0.0)
        mask[...] = jnp.broadcast_to(jnp.where(live, 1.0, 0.0), mask.shape)

    return kernel


def finish():
    def kernel(base, mask, own, a, b, c, w_one, w_two, out):
        spectral = (own[...] + a[...]) + (b[...] + c[...])
        u = base[...] + spectral.T
        normed = u / jnp.sqrt(jnp.mean(u * u, axis=1, keepdims=True) + 1e-06)
        v = dot3(split(normed), split(w_one[...]))
        hidden = v / (1.0 + jnp.exp(-v))
        out[...] = (u + dot3(split(hidden), split(w_two[...]))) * mask[:, 0:1]

    return kernel


def shift(axis, by):
    size = lax.axis_size(axis)
    return [(i, (i + by) % size) for i in range(size)]


def from_others(x, axis):
    return tuple(lax.ppermute(x, axis, shift(axis, by)) for by in (-1, 2, 1))


def shards(
    feats, positions, cell_counts, neighbours, nbr_count, kvec, filters, w_msg, w_val, w_one, w_two
):
    cells = cell_counts.shape[0]
    slots, width = feats.shape
    cell = slots // cells
    devices = lax.axis_size(ROWS_WAVES)
    nx = lax.axis_size(X)
    rows = lax.axis_size("rows")
    own = kvec.shape[1] // rows
    total_waves = kvec.shape[1] * lax.axis_size(WAVES)
    half = lax.axis_index("rows").astype(jnp.int32)
    x = lax.axis_index(X).astype(jnp.int32)
    z = lax.axis_index(Z).astype(jnp.int32)
    first = lax.axis_index(ROWS_WAVES).astype(jnp.int32) * cells

    def floats(*dims):
        return jax.ShapeDtypeStruct(dims, F32)

    def halves(*dims):
        return jax.ShapeDtypeStruct(dims, BF16)

    live = jnp.arange(cell, dtype=jnp.int32)[None, :] < cell_counts[:, None]
    masked = jnp.where(live.reshape(slots, 1), feats, 0.0)
    payload = jnp.pad(masked, ((0, 8), (0, 0))) + jnp.pad(positions, ((slots, 5), (0, 0)))
    above, near2, below = from_others(payload, X)
    ends = [(d, (d + 1) % devices) for d in range(devices) if d % nx == nx - 1]
    ends = ends + [(b, a) for a, b in ends]

    scale = 1.0 / math.sqrt(float(slots * devices) * float(total_waves))
    mine_k = lax.dynamic_slice_in_dim(kvec * (0.5 / math.pi), half * own, own, 1)
    mine_f = lax.dynamic_slice_in_dim(filters * scale, half * own, own, 0)
    home = jnp.pad(mine_f, ((0, 8), (0, 0))) + jnp.pad(mine_k, ((own, 5), (0, width - own)))
    k0, filt = call(
        assemble(own),
        (floats(4 * own, 128), floats(4 * own, width)),
        5,
        [pltpu.VMEM((8, 128), F32)],
        smem=(0,),
    )(z.reshape(1), home, *from_others(home, Z))
    k1, k2, k3 = from_others(k0, Y)

    line = (payload, above, near2, below)
    after = lax.optimization_barrier((k1, k2, k3, *line))[3:]
    other = tuple(lax.ppermute(c, "rows", shift("rows", 1)) for c in after)
    lists = (halves(4, slots, width), halves(4, slots, width), halves(4, 48, slots))
    v_mine = call(values(slots), lists, 5)(w_val, *line)
    v_theirs = call(values(slots), lists, 5)(w_val, *other)
    wide = (halves(4, 16 * own, slots),) * 4
    fwd = call(
        forward(own), (floats(8 * own, width),) * 2 + wide, 8, [pltpu.VMEM((16 * own, width), F32)]
    )
    s2, s1, *m_a = fwd(k2, k1, *v_mine, *v_theirs)
    t2 = lax.ppermute(s2, Y, shift(Y, 2))
    t1 = lax.ppermute(s1, Y, shift(Y, 1))
    edge = lax.ppermute(lax.optimization_barrier((s1, payload))[1], ROWS_WAVES, ends)
    s3, s0, *m_b = fwd(k3, k0, *v_mine, *v_theirs)
    t3 = lax.ppermute(s3, Y, shift(Y, -1))
    s0, edge = lax.optimization_barrier((s0, edge))
    plane = call(four, floats(8 * own, width), 4)(s0, t1, t2, t3)
    f0 = call(filtered(own), floats(8 * own, width), 5)(plane, *from_others(plane, Z), filt)
    f1, f2, f3 = from_others(f0, Y)

    back = call(backward, floats(4, width, slots), 8)
    swap = lax.ppermute(back(f2, f1, f3, f0, *m_a[2:], *m_b[2:]), "rows", shift("rows", 1))
    part = back(f2, f1, f3, f0, *m_a[:2], *m_b[:2])
    e0, e1, e2, e3 = call(pairs, (floats(width, slots),) * 4, 2)(part, swap)
    e2 = lax.ppermute(e2, X, shift(X, 2))
    e1 = lax.ppermute(e1, X, shift(X, 1))
    e3 = lax.ppermute(e3, X, shift(X, -1))

    place = jnp.stack([x, jnp.int32(nx - 1), first])
    base, mask = call(
        messages(cells, cell, cells * devices, neighbours.shape[1]),
        (floats(slots, width), floats(slots, 128)),
        10,
        smem=(0, 1, 2, 3),
    )(place, neighbours, nbr_count, cell_counts, feats, payload, below, above, edge, w_msg)
    return call(finish(), floats(slots, width), 8)(base, mask, e0, e1, e2, e3, w_one, w_two)


def solution(mesh):
    torus = Mesh(mesh.devices.reshape(mesh.shape["rows"], 4, 4, 4), ROWS_WAVES)
    return jax.shard_map(
        shards,
        mesh=torus,
        in_specs=(
            P(ROWS_WAVES, None),
            P(None, ROWS_WAVES),
            P(ROWS_WAVES),
            P(ROWS_WAVES, None),
            P(ROWS_WAVES),
            P(None, WAVES),
            P(WAVES, None),
            P(),
            P(),
            P(),
            P(),
        ),
        out_specs=P(ROWS_WAVES, None),
        check_vma=False,
    )
```

```python
import math

import jax
import jax.numpy as jnp
from jax import lax
from jax.experimental import pallas as pl
from jax.experimental.pallas import tpu as pltpu
from jax.sharding import Mesh
from jax.sharding import PartitionSpec as P

Z, Y, X = "waves_0", "waves_1", "waves_2"
WAVES = (Z, Y, X)
ROWS_WAVES = ("rows", Z, Y, X)
F32 = jnp.float32
BF16 = jnp.bfloat16

SIN_POLY = (6.283185280154403, -10.33542015333633, 5.100154773052372, -1.1965808225334407, 0.15531182448662934)
COS_POLY = (0.9999999997791529, -4.934802136928833, 4.058709154760502, -1.335211949366169, 0.23493706849740192, -0.0243959319559508)
ROUNDER = 12582912.0


def horner(coeffs, u):
    out = coeffs[-1]
    for c in coeffs[-2::-1]:
        out = out * u + c
    return out


def split(a):
    high = a.astype(BF16)
    return high, (a - high.astype(F32)).astype(BF16)


def thirds(a):
    high = a.astype(BF16).astype(F32)
    rest = a - high
    middle = rest.astype(BF16).astype(F32)
    return high, middle, rest - middle


def dot(a, b):
    return jnp.dot(a, b, preferred_element_type=F32)


def dot3(a, b):
    return dot(a[0], b[0]) + (dot(a[1], b[0]) + dot(a[0], b[1]))


def call(kernel, outs, n_in, scratch=(), smem=(), flops=0, limit=16 << 20):
    def space(i):
        return pltpu.SMEM if i in smem else pltpu.VMEM

    return pl.pallas_call(
        kernel,
        out_shape=outs,
        in_specs=[pl.BlockSpec(memory_space=space(i)) for i in range(n_in)],
        out_specs=jax.tree.map(lambda _: pl.BlockSpec(memory_space=pltpu.VMEM), outs),
        scratch_shapes=scratch,
        cost_estimate=pl.CostEstimate(flops=flops, bytes_accessed=1 << 16, transcendentals=0),
        compiler_params=pltpu.CompilerParams(vmem_limit_bytes=limit),
    )


def live_rows(block, cells, cell):
    slots = cells * cell
    row = lax.broadcasted_iota(jnp.int32, (slots, 1), 0).astype(F32)
    limit = block[slots + 3 : slots + 4, 0:1]
    for c in range(1, cells):
        limit = jnp.where(row < c * cell, limit, c * cell + block[slots + 3 : slots + 4, c : c + 1])
    return row < limit


def lattice(own, groups):
    def kernel(kv, out, flat):
        flat[...] = jnp.zeros(flat.shape, F32)
        pad = jnp.zeros((8, flat.shape[1] - 128), F32)
        for g in range(groups):
            flat[...] += pltpu.roll(jnp.concatenate([kv[g], pad], axis=1), g * own, 1)
        kh, km, kl = thirds(flat[...])
        out[...] = jnp.concatenate([kh, kh, km, kh, km, kl], axis=0).T.astype(BF16)

    return kernel


def forward(cells, cell, count, own, groups, first):
    slots = cells * cell

    def kernel(lhs, w_val, *refs):
        chunks, refs = refs[:count], refs[count:]
        if not first:
            before, refs = refs[0], refs[1:]
        out, mh, ml = refs
        w = split(w_val[...])
        for j, chunk in enumerate(chunks):
            live = live_rows(chunk, cells, cell)
            v = split(jnp.where(live, dot3(split(chunk[:slots]), w), 0.0))
            ph, pm, pl_ = thirds(chunk[slots : slots + 8])
            turns = dot(lhs[...], jnp.concatenate([ph, pm, ph, pl_, pm, ph], axis=0).astype(BF16))
            for g in range(groups):
                t = turns[g * own : (g + 1) * own]
                f = t - ((t + ROUNDER) - ROUNDER)
                u = f * f
                s = f * horner(SIN_POLY, u)
                c = horner(COS_POLY, u)
                both = jnp.concatenate([1.0 - 0.5 * (s * s), s * c], axis=0)
                rows = slice(2 * own * g, 2 * own * (g + 1))
                mh[j, rows], ml[j, rows] = split(both)
            part = dot3((mh[j], ml[j]), v)
            if j:
                out[...] += part
            elif first:
                out[...] = part
            else:
                out[...] = before[...] + part

    return kernel


def filtered(scale):
    def kernel(half, parts, filters, out):
        groups, double, _ = parts.shape
        own = double // 2
        f = filters[pl.ds(pl.multiple_of(half[0] * own, 8), own), :] * scale
        total = parts[0]
        for g in range(1, groups):
            total = total + parts[g]
        total = total * jnp.concatenate([f, f], axis=0)
        for g in range(groups):
            out[g] = total

    return kernel


def turned(f, high, low):
    high[...], low[...] = split(f[...].T)


def backward(chunks):
    def kernel(fh, fl, mh, ml, *outs):
        for j, out in zip(chunks, outs):
            out[...] = dot3((fh[...], fl[...]), (mh[j], ml[j]))

    return kernel


def pairs(*refs):
    count = len(refs) // 3
    for a, b, out in zip(refs[:count], refs[count : 2 * count], refs[2 * count :]):
        out[...] = a[...] + b[...]


def messages(cells, cell, cells_all, nb, last):
    slots = cells * cell

    def kernel(at_x, at_cell, neighbours, nbr_count, own, low, high, edge, w_msg, out, mask):
        x, first = at_x[0], at_cell[0]
        lo = jnp.where(x == 0, edge[...], low[...])
        hi = jnp.where(x == last, edge[...], high[...])
        blocks = (lo, own[...], hi)
        masks = [live_rows(b, cells, cell) for b in blocks]
        parts = [split(jnp.where(m, b[:slots], 0.0)) for m, b in zip(masks, blocks)]
        wide = [tuple(p[k][c * cell : (c + 1) * cell] for k in range(2)) for p in parts for c in range(cells)]
        pos = [
            b[slots : slots + 3, c * cell : (c + 1) * cell] for b in blocks for c in range(cells)
        ]
        cols = own[slots : slots + 8].T
        eye = lax.broadcasted_iota(jnp.int32, (cell, cell), 0) == lax.broadcasted_iota(jnp.int32, (cell, cell), 1)
        gathered = []
        for c in range(cells):
            mine = cols[c * cell : (c + 1) * cell]
            acc = None
            for step in range(2 * cells + 1):
                other = c + step
                local = other - cells
                target = lax.rem(first + local + cells_all, cells_all)
                listed = jnp.float32(0.0)
                for b in range(nb):
                    hit = (neighbours[c, b] == target) & (b < nbr_count[c])
                    listed = listed + jnp.where(hit, jnp.float32(1.0), jnp.float32(0.0))
                near = pos[other]
                d0 = mine[:, 0:1] - near[0:1]
                d1 = mine[:, 1:2] - near[1:2]
                d2 = mine[:, 2:3] - near[2:3]
                weight = jnp.exp(-0.125 * (d0 * d0 + d1 * d1 + d2 * d2)) * listed
                if step == cells:
                    weight = jnp.where(eye, 0.0, weight)
                part = dot3(split(weight), wide[other])
                acc = part if acc is None else acc + part
            gathered.append(acc)
        total = jnp.concatenate(gathered, axis=0)
        live = masks[1]
        msg = 0.125 * dot3(split(total), split(w_msg[...]))
        out[...] = own[:slots] + jnp.where(live, msg, 0.0)
        mask[...] = jnp.broadcast_to(jnp.where(live, 1.0, 0.0), mask.shape)

    return kernel


def finish():
    def kernel(base, mask, a, b, c, w_one, w_two, out):
        spectral = a[...] + (b[...] + c[...])
        u = base[...] + spectral.T
        normed = u / jnp.sqrt(jnp.mean(u * u, axis=1, keepdims=True) + 1e-06)
        v = dot3(split(normed), split(w_one[...]))
        hidden = v / (1.0 + jnp.exp(-v))
        out[...] = (u + dot3(split(hidden), split(w_two[...]))) * mask[:, 0:1]

    return kernel


def shift(axis, by):
    size = lax.axis_size(axis)
    return [(i, (i + by) % size) for i in range(size)]


def shards(
    feats, positions, cell_counts, neighbours, nbr_count, kvec, filters, w_msg, w_val, w_one, w_two
):
    cells = cell_counts.shape[0]
    slots, width = feats.shape
    cell = slots // cells
    devices = lax.axis_size(ROWS_WAVES)
    nx = lax.axis_size(X)
    rows = lax.axis_size("rows")
    group = lax.axis_size((Z, Y))
    own_waves = kvec.shape[1] // rows
    waves = own_waves * group
    half = lax.axis_index("rows").astype(jnp.int32)
    x = lax.axis_index(X).astype(jnp.int32)
    first = lax.axis_index(ROWS_WAVES).astype(jnp.int32) * cells

    def floats(*dims):
        return jax.ShapeDtypeStruct(dims, F32)

    def halves(*dims):
        return jax.ShapeDtypeStruct(dims, BF16)

    counts = cell_counts.astype(F32)[None]
    payload = jnp.pad(feats, ((0, 8), (0, 0))) + jnp.pad(positions, ((slots, 5), (0, 0)))
    payload = payload + jnp.pad(counts, ((slots + 3, 4), (0, width - cells)))
    near2 = lax.ppermute(payload, X, shift(X, 2))
    above = lax.ppermute(payload, X, shift(X, -1))
    below = lax.ppermute(payload, X, shift(X, 1))
    other = [lax.ppermute(payload, "rows", shift("rows", 1))]

    kv = lax.dynamic_slice_in_dim(kvec * (0.5 / math.pi), half * own_waves, own_waves, 1)
    kv = jnp.pad(kv, ((0, 8 - kv.shape[0]), (0, 128 - own_waves)))
    kv = lax.all_to_all(jnp.broadcast_to(kv[None], (group, *kv.shape)), (Z, Y), 0, 0, tiled=True)
    kv, near2, above, below, again = lax.optimization_barrier((kv, near2, above, below, payload))
    ends = [(d, (d + 1) % devices) for d in range(devices) if d % nx == nx - 1]
    ends = ends + [(b, a) for a, b in ends]
    edge = lax.ppermute(again, ROWS_WAVES, ends)

    lhs = call(lattice(own_waves, group), halves(waves, 48), 1, [pltpu.VMEM((8, waves), F32)])(kv)
    line = (payload, above, below, near2)
    other += [lax.ppermute(c, "rows", shift("rows", 1)) for c in line[1:]]
    count = len(line)
    wide = halves(count, 2 * waves, slots)
    sums = floats(2 * waves, width)
    work = 12 * count * waves * slots * width
    part, *mine = call(forward(cells, cell, count, own_waves, group, True), (sums, wide, wide), 2 + count, flops=work)(
        lhs, w_val, *line
    )
    part, *theirs = call(forward(cells, cell, count, own_waves, group, False), (sums, wide, wide), 3 + count, flops=work)(
        lhs, w_val, *other, part
    )
    part, edge = lax.optimization_barrier((part, edge))
    parts = lax.all_to_all(part.reshape(group, 2 * own_waves, width), (Z, Y), 0, 0, tiled=True)
    scale = 1.0 / math.sqrt(float(slots * devices) * float(waves * rows * nx))
    spread = call(filtered(scale), floats(*parts.shape), 3, smem=(0,))(half.reshape(1), parts, filters)
    f = lax.all_to_all(spread, (Z, Y), 0, 0, tiled=True).reshape(2 * waves, width)

    ft = call(turned, (halves(width, 2 * waves),) * 2, 1)(f)
    one = floats(width, slots)
    swap = shift("rows", 1)

    def back(chunks, ft, waves_of):
        flops = len(chunks) * work // count
        return call(backward(chunks), (one,) * len(chunks), 4, flops=flops)(*ft, *waves_of)

    (far,) = back((3,), ft, theirs)
    there = lax.ppermute(far, "rows", swap)
    ft = lax.optimization_barrier((*ft, far))[:2]
    rest = [lax.ppermute(r, "rows", swap) for r in back((0, 1, 2), ft, theirs)]
    (e3,) = call(pairs, (one,), 2)(*back((3,), ft, mine), there)
    e3, *ft = lax.optimization_barrier((e3, *ft))
    e3 = lax.ppermute(e3, X, shift(X, 2))
    near = back((0, 1, 2), ft, mine)
    e0, e1, e2 = call(pairs, (one,) * 3, 6)(*near, *rest)
    e1 = lax.ppermute(e1, X, shift(X, 1))
    e2 = lax.ppermute(e2, X, shift(X, -1))

    base, mask = call(
        messages(cells, cell, cells * devices, neighbours.shape[1], nx - 1),
        (floats(slots, width), floats(slots, 128)),
        9,
        smem=(0, 1, 2, 3),
        flops=work // 4,
    )(x.reshape(1), first.reshape(1), neighbours, nbr_count, payload, below, above, edge, w_msg)
    (e0,) = call(pairs, (one,), 2)(e0, e3)
    return call(finish(), floats(slots, width), 7)(base, mask, e0, e1, e2, w_one, w_two)


def solution(mesh):
    torus = Mesh(mesh.devices.reshape(mesh.shape["rows"], 4, 4, 4), ROWS_WAVES)
    return jax.shard_map(
        shards,
        mesh=torus,
        in_specs=(
            P(ROWS_WAVES, None),
            P(None, ROWS_WAVES),
            P(ROWS_WAVES),
            P(ROWS_WAVES, None),
            P(ROWS_WAVES),
            P(None, WAVES),
            P(WAVES, None),
            P(),
            P(),
            P(),
            P(),
        ),
        out_specs=P(ROWS_WAVES, None),
        check_vma=False,
    )
```

```python
import math

import jax
import jax.numpy as jnp
from jax import lax
from jax.experimental import pallas as pl
from jax.experimental.pallas import tpu as pltpu
from jax.sharding import Mesh
from jax.sharding import PartitionSpec as P

Z, Y, X = "waves_0", "waves_1", "waves_2"
WAVES = (Z, Y, X)
ROWS_WAVES = ("rows", Z, Y, X)
F32 = jnp.float32
BF16 = jnp.bfloat16

SIN_POLY = (6.283185280154403, -10.33542015333633, 5.100154773052372, -1.1965808225334407, 0.15531182448662934)
COS_POLY = (0.9999999997791529, -4.934802136928833, 4.058709154760502, -1.335211949366169, 0.23493706849740192, -0.0243959319559508)
ROUNDER = 12582912.0


def horner(coeffs, u):
    out = coeffs[-1]
    for c in coeffs[-2::-1]:
        out = out * u + c
    return out


def split(a):
    high = a.astype(BF16)
    return high, (a - high.astype(F32)).astype(BF16)


def thirds(a):
    high = a.astype(BF16).astype(F32)
    rest = a - high
    middle = rest.astype(BF16).astype(F32)
    return high, middle, rest - middle


def dot(a, b):
    return jnp.dot(a, b, preferred_element_type=F32)


def dot3(a, b):
    return dot(a[0], b[0]) + (dot(a[1], b[0]) + dot(a[0], b[1]))


def call(kernel, outs, n_in, scratch=(), smem=(), flops=0, limit=16 << 20):
    def space(i):
        return pltpu.SMEM if i in smem else pltpu.VMEM

    return pl.pallas_call(
        kernel,
        out_shape=outs,
        in_specs=[pl.BlockSpec(memory_space=space(i)) for i in range(n_in)],
        out_specs=jax.tree.map(lambda _: pl.BlockSpec(memory_space=pltpu.VMEM), outs),
        scratch_shapes=scratch,
        cost_estimate=pl.CostEstimate(flops=flops, bytes_accessed=1 << 16, transcendentals=0),
        compiler_params=pltpu.CompilerParams(vmem_limit_bytes=limit),
    )


def live_rows(block, cells, cell):
    slots = cells * cell
    row = lax.broadcasted_iota(jnp.int32, (slots, 1), 0).astype(F32)
    limit = block[slots + 3 : slots + 4, 0:1]
    for c in range(1, cells):
        limit = jnp.where(row < c * cell, limit, c * cell + block[slots + 3 : slots + 4, c : c + 1])
    return row < limit


def lattice(own, groups):
    def kernel(kv, w_val, out, wh, wl, flat):
        wh[...], wl[...] = split(w_val[...])
        flat[...] = jnp.zeros(flat.shape, F32)
        pad = jnp.zeros((8, flat.shape[1] - 128), F32)
        for g in range(groups):
            flat[...] += pltpu.roll(jnp.concatenate([kv[g], pad], axis=1), g * own, 1)
        kh, km, kl = thirds(flat[...])
        out[...] = jnp.concatenate([kh, kh, km, kh, km, kl], axis=0).T.astype(BF16)

    return kernel


def forward(cells, cell, count, own, groups, first):
    slots = cells * cell

    def kernel(lhs, wh, wl, *refs):
        chunks, refs = refs[:count], refs[count:]
        if not first:
            before, refs = refs[0], refs[1:]
        out, mh, ml = refs
        w = wh[...], wl[...]
        for j, chunk in enumerate(chunks):
            live = live_rows(chunk, cells, cell)
            v = split(jnp.where(live, dot3(split(chunk[:slots]), w), 0.0))
            ph, pm, pl_ = thirds(chunk[slots : slots + 8])
            turns = dot(lhs[...], jnp.concatenate([ph, pm, ph, pl_, pm, ph], axis=0).astype(BF16))
            for g in range(groups):
                t = turns[g * own : (g + 1) * own]
                f = t - ((t + ROUNDER) - ROUNDER)
                u = f * f
                s = f * horner(SIN_POLY, u)
                c = horner(COS_POLY, u)
                both = jnp.concatenate([1.0 - 0.5 * (s * s), s * c], axis=0)
                rows = slice(2 * own * g, 2 * own * (g + 1))
                mh[j, rows], ml[j, rows] = split(both)
            part = dot3((mh[j], ml[j]), v)
            if j:
                out[...] += part
            elif first:
                out[...] = part
            else:
                out[...] = before[...] + part

    return kernel


def filtered(scale):
    def kernel(half, parts, filters, out):
        groups, double, _ = parts.shape
        own = double // 2
        f = filters[pl.ds(pl.multiple_of(half[0] * own, 8), own), :] * scale
        total = parts[0]
        for g in range(1, groups):
            total = total + parts[g]
        total = total * jnp.concatenate([f, f], axis=0)
        for g in range(groups):
            out[g] = total

    return kernel


def turned(f, high, low):
    high[...], low[...] = split(f[...].T)


def backward(chunks):
    def kernel(fh, fl, mh, ml, *refs):
        count = len(chunks)
        outs, added = refs[-count:], refs[:-count]
        for j, out in enumerate(outs):
            part = dot3((fh[...], fl[...]), (mh[chunks[j]], ml[chunks[j]]))
            out[...] = part + added[j][...] if added else part

    return kernel


def pairs(*refs):
    count = len(refs) // 3
    for a, b, out in zip(refs[:count], refs[count : 2 * count], refs[2 * count :]):
        out[...] = a[...] + b[...]


def messages(cells, cell, cells_all, nb, last):
    slots = cells * cell

    def kernel(at_x, at_cell, neighbours, nbr_count, own, low, high, edge, w_msg, out, mask):
        x, first = at_x[0], at_cell[0]
        lo = jnp.where(x == 0, edge[...], low[...])
        hi = jnp.where(x == last, edge[...], high[...])
        blocks = (lo, own[...], hi)
        masks = [live_rows(b, cells, cell) for b in blocks]
        parts = [split(jnp.where(m, b[:slots], 0.0)) for m, b in zip(masks, blocks)]
        wide = [tuple(p[k][c * cell : (c + 1) * cell] for k in range(2)) for p in parts for c in range(cells)]
        pos = [
            b[slots : slots + 3, c * cell : (c + 1) * cell] for b in blocks for c in range(cells)
        ]
        cols = own[slots : slots + 8].T
        eye = lax.broadcasted_iota(jnp.int32, (cell, cell), 0) == lax.broadcasted_iota(jnp.int32, (cell, cell), 1)
        gathered = []
        for c in range(cells):
            mine = cols[c * cell : (c + 1) * cell]
            acc = None
            for step in range(2 * cells + 1):
                other = c + step
                local = other - cells
                target = lax.rem(first + local + cells_all, cells_all)
                listed = jnp.float32(0.0)
                for b in range(nb):
                    hit = (neighbours[c, b] == target) & (b < nbr_count[c])
                    listed = listed + jnp.where(hit, jnp.float32(1.0), jnp.float32(0.0))
                near = pos[other]
                d0 = mine[:, 0:1] - near[0:1]
                d1 = mine[:, 1:2] - near[1:2]
                d2 = mine[:, 2:3] - near[2:3]
                weight = jnp.exp(-0.125 * (d0 * d0 + d1 * d1 + d2 * d2)) * listed
                if step == cells:
                    weight = jnp.where(eye, 0.0, weight)
                part = dot3(split(weight), wide[other])
                acc = part if acc is None else acc + part
            gathered.append(acc)
        total = jnp.concatenate(gathered, axis=0)
        live = masks[1]
        msg = 0.125 * dot3(split(total), split(w_msg[...]))
        out[...] = own[:slots] + jnp.where(live, msg, 0.0)
        mask[...] = jnp.broadcast_to(jnp.where(live, 1.0, 0.0), mask.shape)

    return kernel


def finish():
    def kernel(base, mask, a, b, c, w_one, w_two, out):
        spectral = a[...] + (b[...] + c[...])
        u = base[...] + spectral.T
        normed = u / jnp.sqrt(jnp.mean(u * u, axis=1, keepdims=True) + 1e-06)
        v = dot3(split(normed), split(w_one[...]))
        hidden = v / (1.0 + jnp.exp(-v))
        out[...] = (u + dot3(split(hidden), split(w_two[...]))) * mask[:, 0:1]

    return kernel


def shift(axis, by):
    size = lax.axis_size(axis)
    return [(i, (i + by) % size) for i in range(size)]


def shards(
    feats, positions, cell_counts, neighbours, nbr_count, kvec, filters, w_msg, w_val, w_one, w_two
):
    cells = cell_counts.shape[0]
    slots, width = feats.shape
    cell = slots // cells
    devices = lax.axis_size(ROWS_WAVES)
    nx = lax.axis_size(X)
    rows = lax.axis_size("rows")
    group = lax.axis_size((Z, Y))
    own_waves = kvec.shape[1] // rows
    waves = own_waves * group
    half = lax.axis_index("rows").astype(jnp.int32)
    x = lax.axis_index(X).astype(jnp.int32)
    first = lax.axis_index(ROWS_WAVES).astype(jnp.int32) * cells

    def floats(*dims):
        return jax.ShapeDtypeStruct(dims, F32)

    def halves(*dims):
        return jax.ShapeDtypeStruct(dims, BF16)

    counts = cell_counts.astype(F32)[None]
    payload = jnp.pad(feats, ((0, 8), (0, 0))) + jnp.pad(positions, ((slots, 5), (0, 0)))
    payload = payload + jnp.pad(counts, ((slots + 3, 4), (0, width - cells)))
    near2 = lax.ppermute(payload, X, shift(X, 2))
    above = lax.ppermute(payload, X, shift(X, -1))
    below = lax.ppermute(payload, X, shift(X, 1))
    other = [lax.ppermute(payload, "rows", shift("rows", 1))]
    kv = lax.dynamic_slice_in_dim(kvec * (0.5 / math.pi), half * own_waves, own_waves, 1)
    kv = jnp.pad(kv, ((0, 8 - kv.shape[0]), (0, 128 - own_waves)))
    kv = jnp.broadcast_to(kv[None], (group, *kv.shape))
    kv, again = lax.optimization_barrier((kv, payload))
    kv = lax.all_to_all(kv, (Z, Y), 0, 0, tiled=True)
    ends = [(d, (d + 1) % devices) for d in range(devices) if d % nx == nx - 1]
    ends = ends + [(b, a) for a, b in ends]
    edge = lax.ppermute(again, ROWS_WAVES, ends)
    lhs, *w = call(
        lattice(own_waves, group),
        (halves(waves, 48), halves(width, width), halves(width, width)),
        2,
        [pltpu.VMEM((8, waves), F32)],
    )(kv, w_val)
    lhs, near2, above, below = lax.optimization_barrier((lhs, near2, above, below))
    line = (payload, above, below, near2)
    other += [lax.ppermute(c, "rows", shift("rows", 1)) for c in line[1:]]
    lhs, edge = lax.optimization_barrier((lhs, edge))
    count = len(line)
    wide = halves(count, 2 * waves, slots)
    sums = floats(2 * waves, width)
    work = 12 * count * waves * slots * width
    part, *mine = call(forward(cells, cell, count, own_waves, group, True), (sums, wide, wide), 3 + count, flops=work)(
        lhs, *w, *line
    )
    part, *theirs = call(forward(cells, cell, count, own_waves, group, False), (sums, wide, wide), 4 + count, flops=work)(
        lhs, *w, *other, part
    )
    parts = lax.all_to_all(part.reshape(group, 2 * own_waves, width), (Z, Y), 0, 0, tiled=True)
    scale = 1.0 / math.sqrt(float(slots * devices) * float(waves * rows * nx))
    spread = call(filtered(scale), floats(*parts.shape), 3, smem=(0,))(half.reshape(1), parts, filters)
    f = lax.all_to_all(spread, (Z, Y), 0, 0, tiled=True).reshape(2 * waves, width)

    ft = call(turned, (halves(width, 2 * waves),) * 2, 1)(f)
    one = floats(width, slots)
    swap = shift("rows", 1)

    def back(chunks, ft, waves_of, *added):
        flops = len(chunks) * work // count
        outs = (one,) * len(chunks)
        return call(backward(chunks), outs, 4 + len(added), flops=flops)(*ft, *waves_of, *added)

    (far,) = back((3,), ft, theirs)
    there = lax.ppermute(far, "rows", swap)
    ft = lax.optimization_barrier((*ft, far))[:2]
    rest = [lax.ppermute(r, "rows", swap) for r in back((0, 1, 2), ft, theirs)]
    (e3,) = back((3,), ft, mine, there)
    e3, *ft = lax.optimization_barrier((e3, *ft))
    e3 = lax.ppermute(e3, X, shift(X, 2))
    e0, e1, e2 = back((0, 1, 2), ft, mine, *rest)
    e1 = lax.ppermute(e1, X, shift(X, 1))
    e2 = lax.ppermute(e2, X, shift(X, -1))

    base, mask = call(
        messages(cells, cell, cells * devices, neighbours.shape[1], nx - 1),
        (floats(slots, width), floats(slots, 128)),
        9,
        smem=(0, 1, 2, 3),
        flops=work // 4,
    )(x.reshape(1), first.reshape(1), neighbours, nbr_count, payload, below, above, edge, w_msg)
    (e0,) = call(pairs, (one,), 2)(e0, e3)
    return call(finish(), floats(slots, width), 7)(base, mask, e0, e1, e2, w_one, w_two)


def solution(mesh):
    torus = Mesh(mesh.devices.reshape(mesh.shape["rows"], 4, 4, 4), ROWS_WAVES)
    return jax.shard_map(
        shards,
        mesh=torus,
        in_specs=(
            P(ROWS_WAVES, None),
            P(None, ROWS_WAVES),
            P(ROWS_WAVES),
            P(ROWS_WAVES, None),
            P(ROWS_WAVES),
            P(None, WAVES),
            P(WAVES, None),
            P(),
            P(),
            P(),
            P(),
        ),
        out_specs=P(ROWS_WAVES, None),
        check_vma=False,
    )
```

```python
import math

import jax
import jax.numpy as jnp
from jax import lax
from jax.experimental import pallas as pl
from jax.experimental.pallas import tpu as pltpu
from jax.sharding import Mesh
from jax.sharding import PartitionSpec as P

Z, Y, X = "waves_0", "waves_1", "waves_2"
WAVES = (Z, Y, X)
ROWS_WAVES = ("rows", Z, Y, X)
F32 = jnp.float32
BF16 = jnp.bfloat16

SIN_POLY = (6.283185280154403, -10.33542015333633, 5.100154773052372, -1.1965808225334407, 0.15531182448662934)
COS_POLY = (0.999999953027512, -4.934792802489427, 4.058410790762133, -1.3318729727851486, 0.21968242357146)
ROUNDER = 12582912.0


def horner(coeffs, u):
    out = coeffs[-1]
    for c in coeffs[-2::-1]:
        out = out * u + c
    return out


def split(a):
    high = a.astype(BF16)
    return high, (a - high.astype(F32)).astype(BF16)


def thirds(a):
    high = a.astype(BF16).astype(F32)
    rest = a - high
    middle = rest.astype(BF16).astype(F32)
    return high, middle, rest - middle


def dot(a, b):
    return jnp.dot(a, b, preferred_element_type=F32)


def dot3(a, b):
    return dot(a[0], b[0]) + (dot(a[1], b[0]) + dot(a[0], b[1]))


def call(kernel, outs, n_in, scratch=(), smem=(), flops=0, limit=16 << 20):
    def space(i):
        return pltpu.SMEM if i in smem else pltpu.VMEM

    return pl.pallas_call(
        kernel,
        out_shape=outs,
        in_specs=[pl.BlockSpec(memory_space=space(i)) for i in range(n_in)],
        out_specs=jax.tree.map(lambda _: pl.BlockSpec(memory_space=pltpu.VMEM), outs),
        scratch_shapes=scratch,
        cost_estimate=pl.CostEstimate(flops=flops, bytes_accessed=1 << 16, transcendentals=0),
        compiler_params=pltpu.CompilerParams(vmem_limit_bytes=limit),
    )


def live_rows(block, cells, cell):
    slots = cells * cell
    row = lax.broadcasted_iota(jnp.int32, (slots, 1), 0).astype(F32)
    limit = block[slots + 3 : slots + 4, 0:1]
    for c in range(1, cells):
        limit = jnp.where(row < c * cell, limit, c * cell + block[slots + 3 : slots + 4, c : c + 1])
    return row < limit


def lattice(own, groups):
    def kernel(kv, w_val, out, wh, wl, flat):
        wh[...], wl[...] = split(w_val[...])
        flat[...] = jnp.zeros(flat.shape, F32)
        pad = jnp.zeros((8, flat.shape[1] - 128), F32)
        for g in range(groups):
            flat[...] += pltpu.roll(jnp.concatenate([kv[g], pad], axis=1), g * own, 1)
        kh, km, kl = thirds(flat[...])
        out[...] = jnp.concatenate([kh, kh, km, kh, km, kl], axis=0).T.astype(BF16)

    return kernel


def pack(own, groups):
    def kernel(half, kvec, out, wide):
        wide[...] = jnp.zeros(wide.shape, F32)
        wide[0:3, 0 : 2 * own] = kvec[...] * (0.5 / math.pi)
        k = jnp.where(half[0] == 0, wide[...], pltpu.roll(wide[...], 128 - own, 1))
        k = jnp.where(lax.broadcasted_iota(jnp.int32, k.shape, 1) < own, k, 0.0)
        for g in range(groups):
            out[g] = k

    return kernel


def forward(cells, cell, count, own, groups, first):
    slots = cells * cell

    def kernel(lhs, wh, wl, *refs):
        chunks, refs = refs[:count], refs[count:]
        if not first:
            before, refs = refs[0], refs[1:]
        out, mh, ml = refs
        w = wh[...], wl[...]
        turns, right = [], []
        for chunk in chunks:
            live = live_rows(chunk, cells, cell)
            vh, vl = split(jnp.where(live, dot3(split(chunk[:slots]), w), 0.0))
            right += [vh, vh, vl]
            ph, pm, pl_ = thirds(chunk[slots : slots + 8])
            turns.append(dot(lhs[...], jnp.concatenate([ph, pm, ph, pl_, pm, ph], axis=0).astype(BF16)))
        right = jnp.concatenate(right, axis=0)
        for part in range(2):
            for j in range(count):
                for g in range(part * groups // 2, (part + 1) * groups // 2):
                    t = turns[j][g * own : (g + 1) * own]
                    f = t - ((t + ROUNDER) - ROUNDER)
                    u = f * f
                    s = f * horner(SIN_POLY, u)
                    c = horner(COS_POLY, u)
                    both = jnp.concatenate([1.0 - 0.5 * (s * s), s * c], axis=0)
                    rows = slice(2 * own * g, 2 * own * (g + 1))
                    mh[j, rows], ml[j, rows] = split(both)
            rows = slice(part * own * groups, (part + 1) * own * groups)
            left = [m[j, rows] for j in range(count) for m in (mh, ml, mh)]
            total = dot(jnp.concatenate(left, axis=1), right)
            out[rows] = total if first else before[rows] + total

    return kernel


def filtered(scale):
    def kernel(half, parts, filters, out):
        groups, double, _ = parts.shape
        own = double // 2
        f = filters[pl.ds(pl.multiple_of(half[0] * own, 8), own), :] * scale
        total = parts[0]
        for g in range(1, groups):
            total = total + parts[g]
        total = total * jnp.concatenate([f, f], axis=0)
        for g in range(groups):
            out[g] = total

    return kernel


def turned(f, high, low):
    high[...], low[...] = split(f[...].T)


def backward(chunks):
    def kernel(fh, fl, mh0, ml0, mh1, ml1, *refs):
        count = len(chunks)
        outs, added = refs[-count:], refs[:-count]
        for j, (rest, at) in enumerate(chunks):
            part = dot3((fh[...], fl[...]), (mh1[at], ml1[at]) if rest else (mh0[at], ml0[at]))
            outs[j][...] = part + added[j][...] if added else part

    return kernel


def pairs(*refs):
    count = len(refs) // 3
    for a, b, out in zip(refs[:count], refs[count : 2 * count], refs[2 * count :]):
        out[...] = a[...] + b[...]


def messages(cells, cell, cells_all, nb, last):
    slots = cells * cell

    def kernel(at_x, at_cell, neighbours, nbr_count, own, low, high, edge, w_msg, out, mask):
        x, first = at_x[0], at_cell[0]
        lo = jnp.where(x == 0, edge[...], low[...])
        hi = jnp.where(x == last, edge[...], high[...])
        blocks = (lo, own[...], hi)
        masks = [live_rows(b, cells, cell) for b in blocks]
        parts = [split(jnp.where(m, b[:slots], 0.0)) for m, b in zip(masks, blocks)]
        wide = [tuple(p[k][c * cell : (c + 1) * cell] for k in range(2)) for p in parts for c in range(cells)]
        pos = [
            b[slots : slots + 3, c * cell : (c + 1) * cell] for b in blocks for c in range(cells)
        ]
        cols = own[slots : slots + 8].T
        eye = lax.broadcasted_iota(jnp.int32, (cell, cell), 0) == lax.broadcasted_iota(jnp.int32, (cell, cell), 1)
        gathered = []
        for c in range(cells):
            mine = cols[c * cell : (c + 1) * cell]
            acc = None
            for step in range(2 * cells + 1):
                other = c + step
                local = other - cells
                target = lax.rem(first + local + cells_all, cells_all)
                listed = jnp.float32(0.0)
                for b in range(nb):
                    hit = (neighbours[c, b] == target) & (b < nbr_count[c])
                    listed = listed + jnp.where(hit, jnp.float32(1.0), jnp.float32(0.0))
                near = pos[other]
                d0 = mine[:, 0:1] - near[0:1]
                d1 = mine[:, 1:2] - near[1:2]
                d2 = mine[:, 2:3] - near[2:3]
                weight = jnp.exp(-0.125 * (d0 * d0 + d1 * d1 + d2 * d2)) * listed
                if step == cells:
                    weight = jnp.where(eye, 0.0, weight)
                part = dot3(split(weight), wide[other])
                acc = part if acc is None else acc + part
            gathered.append(acc)
        total = jnp.concatenate(gathered, axis=0)
        live = masks[1]
        msg = 0.125 * dot3(split(total), split(w_msg[...]))
        out[...] = own[:slots] + jnp.where(live, msg, 0.0)
        mask[...] = jnp.broadcast_to(jnp.where(live, 1.0, 0.0), mask.shape)

    return kernel


def finish():
    def kernel(base, mask, a, b, c, w_one, w_two, out):
        spectral = a[...] + (b[...] + c[...])
        u = base[...] + spectral.T
        normed = u / jnp.sqrt(jnp.mean(u * u, axis=1, keepdims=True) + 1e-06)
        v = dot3(split(normed), split(w_one[...]))
        hidden = v / (1.0 + jnp.exp(-v))
        out[...] = (u + dot3(split(hidden), split(w_two[...]))) * mask[:, 0:1]

    return kernel


def shift(axis, by):
    size = lax.axis_size(axis)
    return [(i, (i + by) % size) for i in range(size)]


def shards(
    feats, positions, cell_counts, neighbours, nbr_count, kvec, filters, w_msg, w_val, w_one, w_two
):
    cells = cell_counts.shape[0]
    slots, width = feats.shape
    cell = slots // cells
    devices = lax.axis_size(ROWS_WAVES)
    nx = lax.axis_size(X)
    rows = lax.axis_size("rows")
    group = lax.axis_size((Z, Y))
    own_waves = kvec.shape[1] // rows
    waves = own_waves * group
    half = lax.axis_index("rows").astype(jnp.int32)
    x = lax.axis_index(X).astype(jnp.int32)
    first = lax.axis_index(ROWS_WAVES).astype(jnp.int32) * cells

    def floats(*dims):
        return jax.ShapeDtypeStruct(dims, F32)

    def halves(*dims):
        return jax.ShapeDtypeStruct(dims, BF16)

    counts = cell_counts.astype(F32)[None]
    payload = jnp.pad(feats, ((0, 8), (0, 0))) + jnp.pad(positions, ((slots, 5), (0, 0)))
    payload = payload + jnp.pad(counts, ((slots + 3, 4), (0, width - cells)))
    near2 = lax.ppermute(payload, X, shift(X, 2))
    above = lax.ppermute(payload, X, shift(X, -1))
    below = lax.ppermute(payload, X, shift(X, 1))
    kv = call(pack(own_waves, group), floats(group, 8, 128), 2, [pltpu.VMEM((8, 128), F32)], smem=(0,))(
        half.reshape(1), kvec
    )
    kv, again = lax.optimization_barrier((kv, payload))
    ends = [(d, (d + 1) % devices) for d in range(devices) if d % nx == nx - 1]
    ends = ends + [(b, a) for a, b in ends]
    edge = lax.ppermute(again, ROWS_WAVES, ends)
    kv = lax.all_to_all(kv, (Z, Y), 0, 0, tiled=True)
    lhs, *w = call(
        lattice(own_waves, group),
        (halves(waves, 48), halves(width, width), halves(width, width)),
        2,
        [pltpu.VMEM((8, waves), F32)],
    )(kv, w_val)

    unit = 12 * waves * slots * width

    def sums(chunks, *before):
        count = len(chunks)
        m = halves(count, 2 * waves, slots)
        return call(
            forward(cells, cell, count, own_waves, group, not before),
            (floats(2 * waves, width), m, m),
            3 + count + len(before),
            flops=count * unit,
        )(lhs, *w, *chunks, *before)

    part, *m_own = sums((payload,))
    part, near2, above, below = lax.optimization_barrier((part, near2, above, below))
    swap = shift("rows", 1)
    other = [lax.ppermute(c, "rows", swap) for c in (again, above, below, near2)]
    part, edge = lax.optimization_barrier((part, edge))
    part, *m_line = sums((above, below, near2), part)
    part, *m_other = sums(other, part)
    parts = lax.all_to_all(part.reshape(group, 2 * own_waves, width), (Z, Y), 0, 0, tiled=True)
    scale = 1.0 / math.sqrt(float(slots * devices) * float(waves * rows * nx))
    spread = call(filtered(scale), floats(*parts.shape), 3, smem=(0,))(half.reshape(1), parts, filters)
    f = lax.all_to_all(spread, (Z, Y), 0, 0, tiled=True).reshape(2 * waves, width)

    ft = call(turned, (halves(width, 2 * waves),) * 2, 1)(f)
    one = floats(width, slots)

    def back(chunks, ft, m, *added):
        outs = (one,) * len(chunks)
        return call(backward(chunks), outs, 6 + len(added), flops=len(chunks) * unit)(*ft, *m, *added)

    theirs = *m_other, *m_other
    mine = *m_own, *m_line
    (far,) = back(((0, 3),), ft, theirs)
    there = lax.ppermute(far, "rows", swap)
    ft = lax.optimization_barrier((*ft, far))[:2]
    rest = [lax.ppermute(r, "rows", swap) for r in back(((0, 0), (0, 1), (0, 2)), ft, theirs)]
    (e3,) = back(((1, 2),), ft, mine, there)
    e3, *ft = lax.optimization_barrier((e3, *ft))
    e3 = lax.ppermute(e3, X, shift(X, 2))
    e0, e1, e2 = back(((0, 0), (1, 0), (1, 1)), ft, mine, *rest)
    e1 = lax.ppermute(e1, X, shift(X, 1))
    e2 = lax.ppermute(e2, X, shift(X, -1))

    base, mask = call(
        messages(cells, cell, cells * devices, neighbours.shape[1], nx - 1),
        (floats(slots, width), floats(slots, 128)),
        9,
        smem=(0, 1, 2, 3),
        flops=unit,
    )(x.reshape(1), first.reshape(1), neighbours, nbr_count, payload, below, above, edge, w_msg)
    (e0,) = call(pairs, (one,), 2)(e0, e3)
    return call(finish(), floats(slots, width), 7)(base, mask, e0, e1, e2, w_one, w_two)


def solution(mesh):
    torus = Mesh(mesh.devices.reshape(mesh.shape["rows"], 4, 4, 4), ROWS_WAVES)
    return jax.shard_map(
        shards,
        mesh=torus,
        in_specs=(
            P(ROWS_WAVES, None),
            P(None, ROWS_WAVES),
            P(ROWS_WAVES),
            P(ROWS_WAVES, None),
            P(ROWS_WAVES),
            P(None, WAVES),
            P(WAVES, None),
            P(),
            P(),
            P(),
            P(),
        ),
        out_specs=P(ROWS_WAVES, None),
        check_vma=False,
    )
```

```python
import math

import jax
import jax.numpy as jnp
from jax import lax
from jax.experimental import pallas as pl
from jax.experimental.pallas import tpu as pltpu
from jax.sharding import Mesh
from jax.sharding import PartitionSpec as P

Z, Y, X = "waves_0", "waves_1", "waves_2"
WAVES = (Z, Y, X)
ROWS_WAVES = ("rows", Z, Y, X)
F32 = jnp.float32
BF16 = jnp.bfloat16

SIN_POLY = (6.283185280154403, -10.33542015333633, 5.100154773052372, -1.1965808225334407, 0.15531182448662934)
COS_POLY = (0.999999953027512, -4.934792802489427, 4.058410790762133, -1.3318729727851486, 0.21968242357146)
ROUNDER = 12582912.0


def horner(coeffs, u):
    out = coeffs[-1]
    for c in coeffs[-2::-1]:
        out = out * u + c
    return out


def split(a):
    high = a.astype(BF16)
    return high, (a - high.astype(F32)).astype(BF16)


def thirds(a):
    high = a.astype(BF16).astype(F32)
    rest = a - high
    middle = rest.astype(BF16).astype(F32)
    return high, middle, rest - middle


def dot(a, b):
    return jnp.dot(a, b, preferred_element_type=F32)


def dot3(a, b):
    return dot(a[0], b[0]) + (dot(a[1], b[0]) + dot(a[0], b[1]))


def call(kernel, outs, n_in, scratch=(), smem=(), flops=0, limit=8 << 20):
    def space(i):
        return pltpu.SMEM if i in smem else pltpu.VMEM

    return pl.pallas_call(
        kernel,
        out_shape=outs,
        in_specs=[pl.BlockSpec(memory_space=space(i)) for i in range(n_in)],
        out_specs=jax.tree.map(lambda _: pl.BlockSpec(memory_space=pltpu.VMEM), outs),
        scratch_shapes=scratch,
        cost_estimate=pl.CostEstimate(flops=flops, bytes_accessed=1 << 16, transcendentals=0),
        compiler_params=pltpu.CompilerParams(vmem_limit_bytes=limit),
    )


def live_rows(block, cells, cell):
    slots = cells * cell
    row = lax.broadcasted_iota(jnp.int32, (slots, 1), 0).astype(F32)
    limit = block[slots + 3 : slots + 4, 0:1]
    for c in range(1, cells):
        limit = jnp.where(row < c * cell, limit, c * cell + block[slots + 3 : slots + 4, c : c + 1])
    return row < limit


def lattice(own, groups):
    def kernel(kv, out, flat):
        flat[...] = jnp.zeros(flat.shape, F32)
        pad = jnp.zeros((8, flat.shape[1] - 128), F32)
        for g in range(groups):
            flat[...] += pltpu.roll(jnp.concatenate([kv[g], pad], axis=1), g * own, 1)
        kh, km, kl = thirds(flat[...])
        out[...] = jnp.concatenate([kh, kh, km, kh, km, kl], axis=0).T.astype(BF16)

    return kernel


def pack(slots, own, groups):
    def kernel(own_block, out):
        rows = own_block[slots : slots + 8, :128] * (0.5 / math.pi)
        rows = pltpu.roll(rows, 4, 0)
        k = jnp.where(lax.axis_index("rows") == 0, rows, pltpu.roll(rows, 128 - own, 1))
        lane = lax.broadcasted_iota(jnp.int32, k.shape, 1)
        line = lax.broadcasted_iota(jnp.int32, k.shape, 0)
        k = jnp.where((lane < own) & (line < 3), k, 0.0)
        for g in range(groups):
            out[g] = k

    return kernel


def own_trig(slots, own, groups):
    def kernel(lhs, chunk, mh, ml):
        turns = dot(lhs[...], spots(chunk, slots))
        for g in range(groups):
            rows = slice(2 * own * g, 2 * own * (g + 1))
            mh[0, rows], ml[0, rows] = split(cos_and_sin(turns[g * own : (g + 1) * own]))

    return kernel


def spots(chunk, slots):
    x, y, z = thirds(jnp.where(lax.broadcasted_iota(jnp.int32, (8, slots), 0) < 3, chunk[slots : slots + 8], 0.0))
    return jnp.concatenate([x, y, x, z, y, x], axis=0).astype(BF16)


def cos_and_sin(t):
    f = t - ((t + ROUNDER) - ROUNDER)
    u = f * f
    s = f * horner(SIN_POLY, u)
    c = horner(COS_POLY, u)
    return jnp.concatenate([1.0 - 0.5 * (s * s), s * c], axis=0)


def forward(cells, cell, count, own, groups, first):
    slots = cells * cell

    def kernel(lhs, w_val, *refs):
        chunks, refs = refs[:count], refs[count:]
        if first:
            ready, refs = refs[:2], refs[2:]
        else:
            before, refs = refs[0], refs[1:]
        out, mh, ml = refs
        skip = 1 if first else 0
        w = split(w_val[...])
        turns, right = [], []
        for j, chunk in enumerate(chunks):
            live = live_rows(chunk, cells, cell)
            vh, vl = split(jnp.where(live, dot3(split(chunk[:slots]), w), 0.0))
            right += [vh, vh, vl]
            turns.append(dot(lhs[...], spots(chunk, slots)) if j >= skip else None)
        right = jnp.concatenate(right, axis=0)
        for part in range(2):
            for j in range(skip, count):
                for g in range(part * groups // 2, (part + 1) * groups // 2):
                    rows = slice(2 * own * g, 2 * own * (g + 1))
                    pieces = split(cos_and_sin(turns[j][g * own : (g + 1) * own]))
                    mh[j - skip, rows], ml[j - skip, rows] = pieces
            rows = slice(part * own * groups, (part + 1) * own * groups)
            pairs_of = [(ready[0][0, rows], ready[1][0, rows])] if first else []
            pairs_of += [(mh[j, rows], ml[j, rows]) for j in range(count - skip)]
            left = [m for high, low in pairs_of for m in (high, low, high)]
            total = dot(jnp.concatenate(left, axis=1), right)
            out[rows] = total if first else before[rows] + total

    return kernel


def filtered(scale):
    def kernel(parts, filters, out):
        groups, double, _ = parts.shape
        own = double // 2
        f = jnp.where(lax.axis_index("rows") == 0, filters[:own], filters[own:]) * scale
        total = parts[0]
        for g in range(1, groups):
            total = total + parts[g]
        total = total * jnp.concatenate([f, f], axis=0)
        for g in range(groups):
            out[g] = total

    return kernel


def line_end(below, above, out):
    out[...] = jnp.where(lax.axis_index(X) == 0, below[...], above[...])


def turned(f, high, low):
    high[...], low[...] = split(f[...].T)


def backward(chunks):
    def kernel(fh, fl, mh0, ml0, mh1, ml1, *refs):
        count = len(chunks)
        outs, added = refs[-count:], refs[:-count]
        for j, (rest, at) in enumerate(chunks):
            part = dot3((fh[...], fl[...]), (mh1[at], ml1[at]) if rest else (mh0[at], ml0[at]))
            outs[j][...] = part + added[j][...] if added else part

    return kernel


def pairs(*refs):
    count = len(refs) // 3
    for a, b, out in zip(refs[:count], refs[count : 2 * count], refs[2 * count :]):
        out[...] = a[...] + b[...]


def messages(cells, cell, cells_all, nb, last):
    slots = cells * cell

    def kernel(neighbours, nbr_count, own, low, high, edge, w_msg, out, mask):
        x, first = lax.axis_index(X), lax.axis_index(ROWS_WAVES) * cells
        lo = jnp.where(x == 0, edge[...], low[...])
        hi = jnp.where(x == last, edge[...], high[...])
        blocks = (lo, own[...], hi)
        masks = [live_rows(b, cells, cell) for b in blocks]
        parts = [split(jnp.where(m, b[:slots], 0.0)) for m, b in zip(masks, blocks)]
        wide = [tuple(p[k][c * cell : (c + 1) * cell] for k in range(2)) for p in parts for c in range(cells)]
        pos = [
            b[slots : slots + 3, c * cell : (c + 1) * cell] for b in blocks for c in range(cells)
        ]
        cols = own[slots : slots + 8].T
        eye = lax.broadcasted_iota(jnp.int32, (cell, cell), 0) == lax.broadcasted_iota(jnp.int32, (cell, cell), 1)
        gathered = []
        for c in range(cells):
            mine = cols[c * cell : (c + 1) * cell]
            acc = None
            for step in range(2 * cells + 1):
                other = c + step
                local = other - cells
                target = lax.rem(first + local + cells_all, cells_all)
                listed = jnp.float32(0.0)
                for b in range(nb):
                    hit = (neighbours[c, b] == target) & (b < nbr_count[c])
                    listed = listed + jnp.where(hit, jnp.float32(1.0), jnp.float32(0.0))
                near = pos[other]
                d0 = mine[:, 0:1] - near[0:1]
                d1 = mine[:, 1:2] - near[1:2]
                d2 = mine[:, 2:3] - near[2:3]
                weight = jnp.exp(-0.125 * (d0 * d0 + d1 * d1 + d2 * d2)) * listed
                if step == cells:
                    weight = jnp.where(eye, 0.0, weight)
                part = dot3(split(weight), wide[other])
                acc = part if acc is None else acc + part
            gathered.append(acc)
        total = jnp.concatenate(gathered, axis=0)
        live = masks[1]
        msg = 0.125 * dot3(split(total), split(w_msg[...]))
        out[...] = own[:slots] + jnp.where(live, msg, 0.0)
        mask[...] = jnp.broadcast_to(jnp.where(live, 1.0, 0.0), mask.shape)

    return kernel


def finish():
    def kernel(base, mask, a, b, c, w_one, w_two, out):
        spectral = a[...] + (b[...] + c[...])
        u = base[...] + spectral.T
        normed = u / jnp.sqrt(jnp.mean(u * u, axis=1, keepdims=True) + 1e-06)
        v = dot3(split(normed), split(w_one[...]))
        hidden = v / (1.0 + jnp.exp(-v))
        out[...] = (u + dot3(split(hidden), split(w_two[...]))) * mask[:, 0:1]

    return kernel


def shift(axis, by):
    size = lax.axis_size(axis)
    return [(i, (i + by) % size) for i in range(size)]


def shards(
    feats, positions, cell_counts, neighbours, nbr_count, kvec, filters, w_msg, w_val, w_one, w_two
):
    cells = cell_counts.shape[0]
    slots, width = feats.shape
    cell = slots // cells
    devices = lax.axis_size(ROWS_WAVES)
    nx = lax.axis_size(X)
    rows = lax.axis_size("rows")
    group = lax.axis_size((Z, Y))
    own_waves = kvec.shape[1] // rows
    waves = own_waves * group

    def floats(*dims):
        return jax.ShapeDtypeStruct(dims, F32)

    def halves(*dims):
        return jax.ShapeDtypeStruct(dims, BF16)

    counts = cell_counts.astype(F32)[None]
    payload = jnp.pad(feats, ((0, 8), (0, 0))) + jnp.pad(positions, ((slots, 5), (0, 0)))
    payload = payload + jnp.pad(counts, ((slots + 3, 4), (0, width - cells)))
    payload = payload + jnp.pad(kvec, ((slots + 4, 1), (0, width - kvec.shape[1])))
    near2 = lax.ppermute(payload, X, shift(X, 2))
    above = lax.ppermute(payload, X, shift(X, -1))
    below = lax.ppermute(payload, X, shift(X, 1))
    kv = call(pack(slots, own_waves, group), floats(group, 8, 128), 1)(payload)
    kv = lax.all_to_all(kv, (Z, Y), 0, 0, tiled=True)
    lhs = call(lattice(own_waves, group), halves(waves, 48), 1, [pltpu.VMEM((8, waves), F32)])(kv)

    unit = 12 * waves * slots * width

    def sums(chunks, first, *more):
        count = len(chunks)
        m = halves(count - 1 if first else count, 2 * waves, slots)
        return call(
            forward(cells, cell, count, own_waves, group, first),
            (floats(2 * waves, width), m, m),
            2 + count + len(more),
            flops=count * unit,
        )(lhs, w_val, *chunks, *more)

    m_own = call(own_trig(slots, own_waves, group), (halves(1, 2 * waves, slots),) * 2, 2, flops=unit)(lhs, payload)
    *m_own, near2, above, below = lax.optimization_barrier((*m_own, near2, above, below))
    swap = shift("rows", 1)
    other = [lax.ppermute(c, "rows", swap) for c in (payload, above, below, near2)]
    part, *m_line = sums((payload, above, below, near2), True, *m_own)
    part, *m_other = sums(other, False, part)
    passed = call(line_end, floats(*payload.shape), 2)(below, above)
    part, passed = lax.optimization_barrier((part, passed))
    parts = lax.all_to_all(part.reshape(group, 2 * own_waves, width), (Z, Y), 0, 0, tiled=True)
    scale = 1.0 / math.sqrt(float(slots * devices) * float(waves * rows * nx))
    spread = call(filtered(scale), floats(*parts.shape), 2)(parts, filters)
    f = lax.all_to_all(spread, (Z, Y), 0, 0, tiled=True).reshape(2 * waves, width)

    ends = [(d, (d + nx) % devices) for d in range(devices) if d % nx == 0]
    ends += [(d, (d - nx) % devices) for d in range(devices) if d % nx == nx - 1]
    f, passed = lax.optimization_barrier((f, passed))
    edge = lax.ppermute(passed, ROWS_WAVES, ends)
    ft = call(turned, (halves(width, 2 * waves),) * 2, 1)(f)
    one = floats(width, slots)

    def back(chunks, ft, m, *added):
        outs = (one,) * len(chunks)
        return call(backward(chunks), outs, 6 + len(added), flops=len(chunks) * unit)(*ft, *m, *added)

    theirs = *m_other, *m_other
    mine = *m_own, *m_line
    (far,) = back(((0, 3),), ft, theirs)
    there = lax.ppermute(far, "rows", swap)
    ft = lax.optimization_barrier((*ft, far))[:2]
    rest = [lax.ppermute(r, "rows", swap) for r in back(((0, 0), (0, 1), (0, 2)), ft, theirs)]
    (e3,) = back(((1, 2),), ft, mine, there)
    e3, *ft = lax.optimization_barrier((e3, *ft))
    e3 = lax.ppermute(e3, X, shift(X, 2))
    e0, e1, e2 = back(((0, 0), (1, 0), (1, 1)), ft, mine, *rest)
    e1 = lax.ppermute(e1, X, shift(X, 1))
    e2 = lax.ppermute(e2, X, shift(X, -1))

    base, mask = call(
        messages(cells, cell, cells * devices, neighbours.shape[1], nx - 1),
        (floats(slots, width), floats(slots, 128)),
        7,
        smem=(0, 1),
        flops=unit,
    )(neighbours, nbr_count, payload, below, above, edge, w_msg)
    (e0,) = call(pairs, (one,), 2)(e0, e3)
    return call(finish(), floats(slots, width), 7)(base, mask, e0, e1, e2, w_one, w_two)


def solution(mesh):
    torus = Mesh(mesh.devices.reshape(mesh.shape["rows"], 4, 4, 4), ROWS_WAVES)
    return jax.shard_map(
        shards,
        mesh=torus,
        in_specs=(
            P(ROWS_WAVES, None),
            P(None, ROWS_WAVES),
            P(ROWS_WAVES),
            P(ROWS_WAVES, None),
            P(ROWS_WAVES),
            P(None, WAVES),
            P(WAVES, None),
            P(),
            P(),
            P(),
            P(),
        ),
        out_specs=P(ROWS_WAVES, None),
        check_vma=False,
    )
```

```python
import math

import jax
import jax.numpy as jnp
from jax import lax
from jax.experimental import pallas as pl
from jax.experimental.pallas import tpu as pltpu
from jax.sharding import Mesh
from jax.sharding import PartitionSpec as P

Z, Y, X = "waves_0", "waves_1", "waves_2"
WAVES = (Z, Y, X)
ROWS_WAVES = ("rows", Z, Y, X)
F32 = jnp.float32
BF16 = jnp.bfloat16

SIN_POLY = (6.283185280154403, -10.33542015333633, 5.100154773052372, -1.1965808225334407, 0.15531182448662934)
COS_POLY = (0.999999953027512, -4.934792802489427, 4.058410790762133, -1.3318729727851486, 0.21968242357146)
ROUNDER = 12582912.0


def horner(coeffs, u):
    out = coeffs[-1]
    for c in coeffs[-2::-1]:
        out = out * u + c
    return out


def split(a):
    high = a.astype(BF16)
    return high, (a - high.astype(F32)).astype(BF16)


def thirds(a):
    high = a.astype(BF16).astype(F32)
    rest = a - high
    middle = rest.astype(BF16).astype(F32)
    return high, middle, rest - middle


def dot(a, b):
    return jnp.dot(a, b, preferred_element_type=F32)


def dot3(a, b):
    return dot(a[0], b[0]) + (dot(a[1], b[0]) + dot(a[0], b[1]))


def call(kernel, outs, n_in, scratch=(), smem=(), flops=0, alias={}, limit=8 << 20):
    def space(i):
        return pltpu.SMEM if i in smem else pltpu.VMEM

    return pl.pallas_call(
        kernel,
        out_shape=outs,
        in_specs=[pl.BlockSpec(memory_space=space(i)) for i in range(n_in)],
        out_specs=jax.tree.map(lambda _: pl.BlockSpec(memory_space=pltpu.VMEM), outs),
        scratch_shapes=scratch,
        input_output_aliases=alias,
        cost_estimate=pl.CostEstimate(flops=flops, bytes_accessed=1 << 16, transcendentals=0),
        compiler_params=pltpu.CompilerParams(vmem_limit_bytes=limit),
    )


def live_rows(block, cells, cell):
    slots = cells * cell
    row = lax.broadcasted_iota(jnp.int32, (slots, 1), 0).astype(F32)
    limit = block[slots + 3 : slots + 4, 0:1]
    for c in range(1, cells):
        limit = jnp.where(row < c * cell, limit, c * cell + block[slots + 3 : slots + 4, c : c + 1])
    return row < limit


def stamp(slots, cells):
    def kernel(counts, _, out):
        out[slots + 3 : slots + 4, 0:cells] = counts[...].astype(F32).reshape(1, cells)

    return kernel


def lattice(own, groups):
    def kernel(kv, out, flat):
        flat[...] = jnp.zeros(flat.shape, F32)
        pad = jnp.zeros((8, flat.shape[1] - 128), F32)
        for g in range(groups):
            flat[...] += pltpu.roll(jnp.concatenate([kv[g], pad], axis=1), g * own, 1)
        kh, km, kl = thirds(flat[...])
        out[...] = jnp.concatenate([kh, kh, km, kh, km, kl], axis=0).T.astype(BF16)

    return kernel


def pack(slots, own, groups):
    def kernel(own_block, out):
        rows = own_block[slots : slots + 8, :128] * (0.5 / math.pi)
        rows = pltpu.roll(rows, 4, 0)
        k = jnp.where(lax.axis_index("rows") == 0, rows, pltpu.roll(rows, 128 - own, 1))
        lane = lax.broadcasted_iota(jnp.int32, k.shape, 1)
        line = lax.broadcasted_iota(jnp.int32, k.shape, 0)
        k = jnp.where((lane < own) & (line < 3), k, 0.0)
        for g in range(groups):
            out[g] = k

    return kernel


def own_trig(slots, own, groups):
    def kernel(lhs, chunk, mh, ml):
        turns = dot(lhs[...], spots(chunk, slots))
        for g in range(groups):
            rows = slice(2 * own * g, 2 * own * (g + 1))
            mh[0, rows], ml[0, rows] = split(cos_and_sin(turns[g * own : (g + 1) * own]))

    return kernel


def spots(chunk, slots):
    x, y, z = thirds(jnp.where(lax.broadcasted_iota(jnp.int32, (8, slots), 0) < 3, chunk[slots : slots + 8], 0.0))
    return jnp.concatenate([x, y, x, z, y, x], axis=0).astype(BF16)


def cos_and_sin(t):
    f = t - ((t + ROUNDER) - ROUNDER)
    u = f * f
    s = f * horner(SIN_POLY, u)
    c = horner(COS_POLY, u)
    return jnp.concatenate([1.0 - 0.5 * (s * s), s * c], axis=0)


def forward(cells, cell, count, own, groups, first):
    slots = cells * cell

    def kernel(lhs, w_val, *refs):
        chunks, refs = refs[:count], refs[count:]
        if first:
            ready, refs = refs[:2], refs[2:]
        else:
            before, refs = refs[0], refs[1:]
        out, mh, ml = refs
        skip = 1 if first else 0
        w = split(w_val[...])
        turns, right = [], []
        for j, chunk in enumerate(chunks):
            live = live_rows(chunk, cells, cell)
            vh, vl = split(jnp.where(live, dot3(split(chunk[:slots]), w), 0.0))
            right += [vh, vh, vl]
            turns.append(dot(lhs[...], spots(chunk, slots)) if j >= skip else None)
        right = jnp.concatenate(right, axis=0)
        for part in range(2):
            for j in range(skip, count):
                for g in range(part * groups // 2, (part + 1) * groups // 2):
                    rows = slice(2 * own * g, 2 * own * (g + 1))
                    pieces = split(cos_and_sin(turns[j][g * own : (g + 1) * own]))
                    mh[j - skip, rows], ml[j - skip, rows] = pieces
            rows = slice(part * own * groups, (part + 1) * own * groups)
            pairs_of = [(ready[0][0, rows], ready[1][0, rows])] if first else []
            pairs_of += [(mh[j, rows], ml[j, rows]) for j in range(count - skip)]
            left = [m for high, low in pairs_of for m in (high, low, high)]
            total = dot(jnp.concatenate(left, axis=1), right)
            out[rows] = total if first else before[rows] + total

    return kernel


def filtered(scale):
    def kernel(parts, filters, out):
        groups, double, _ = parts.shape
        own = double // 2
        f = jnp.where(lax.axis_index("rows") == 0, filters[:own], filters[own:]) * scale
        total = parts[0]
        for g in range(1, groups):
            total = total + parts[g]
        total = total * jnp.concatenate([f, f], axis=0)
        for g in range(groups):
            out[g] = total

    return kernel


def line_end(below, above, out):
    out[...] = jnp.where(lax.axis_index(X) == 0, below[...], above[...])


def backward_first(at):
    def kernel(f, mh, ml, out, high, low):
        ft = split(f[...].T)
        high[...], low[...] = ft
        out[...] = dot3(ft, (mh[at], ml[at]))

    return kernel


def backward(chunks):
    def kernel(fh, fl, mh0, ml0, mh1, ml1, *refs):
        count = len(chunks)
        outs, added = refs[-count:], refs[:-count]
        for j, (rest, at) in enumerate(chunks):
            part = dot3((fh[...], fl[...]), (mh1[at], ml1[at]) if rest else (mh0[at], ml0[at]))
            outs[j][...] = part + added[j][...] if added else part

    return kernel


def pairs(*refs):
    count = len(refs) // 3
    for a, b, out in zip(refs[:count], refs[count : 2 * count], refs[2 * count :]):
        out[...] = a[...] + b[...]


def messages(cells, cell, cells_all, nb, last):
    slots = cells * cell

    def kernel(neighbours, nbr_count, own, low, high, edge, w_msg, out, mask):
        x, first = lax.axis_index(X), lax.axis_index(ROWS_WAVES) * cells
        lo = jnp.where(x == 0, edge[...], low[...])
        hi = jnp.where(x == last, edge[...], high[...])
        blocks = (lo, own[...], hi)
        masks = [live_rows(b, cells, cell) for b in blocks]
        parts = [split(jnp.where(m, b[:slots], 0.0)) for m, b in zip(masks, blocks)]
        wide = [tuple(p[k][c * cell : (c + 1) * cell] for k in range(2)) for p in parts for c in range(cells)]
        pos = [
            b[slots : slots + 3, c * cell : (c + 1) * cell] for b in blocks for c in range(cells)
        ]
        cols = own[slots : slots + 8].T
        eye = lax.broadcasted_iota(jnp.int32, (cell, cell), 0) == lax.broadcasted_iota(jnp.int32, (cell, cell), 1)
        gathered = []
        for c in range(cells):
            mine = cols[c * cell : (c + 1) * cell]
            acc = None
            for step in range(2 * cells + 1):
                other = c + step
                local = other - cells
                target = lax.rem(first + local + cells_all, cells_all)
                listed = jnp.float32(0.0)
                for b in range(nb):
                    hit = (neighbours[c, b] == target) & (b < nbr_count[c])
                    listed = listed + jnp.where(hit, jnp.float32(1.0), jnp.float32(0.0))
                near = pos[other]
                d0 = mine[:, 0:1] - near[0:1]
                d1 = mine[:, 1:2] - near[1:2]
                d2 = mine[:, 2:3] - near[2:3]
                weight = jnp.exp(-0.125 * (d0 * d0 + d1 * d1 + d2 * d2)) * listed
                if step == cells:
                    weight = jnp.where(eye, 0.0, weight)
                part = dot3(split(weight), wide[other])
                acc = part if acc is None else acc + part
            gathered.append(acc)
        total = jnp.concatenate(gathered, axis=0)
        live = masks[1]
        msg = 0.125 * dot3(split(total), split(w_msg[...]))
        out[...] = own[:slots] + jnp.where(live, msg, 0.0)
        mask[...] = jnp.broadcast_to(jnp.where(live, 1.0, 0.0), mask.shape)

    return kernel


def finish():
    def kernel(base, mask, a, b, c, w_one, w_two, out):
        spectral = a[...] + (b[...] + c[...])
        u = base[...] + spectral.T
        normed = u / jnp.sqrt(jnp.mean(u * u, axis=1, keepdims=True) + 1e-06)
        v = dot3(split(normed), split(w_one[...]))
        hidden = v / (1.0 + jnp.exp(-v))
        out[...] = (u + dot3(split(hidden), split(w_two[...]))) * mask[:, 0:1]

    return kernel


def shift(axis, by):
    size = lax.axis_size(axis)
    return [(i, (i + by) % size) for i in range(size)]


def shards(
    feats, positions, cell_counts, neighbours, nbr_count, kvec, filters, w_msg, w_val, w_one, w_two
):
    cells = cell_counts.shape[0]
    slots, width = feats.shape
    cell = slots // cells
    devices = lax.axis_size(ROWS_WAVES)
    nx = lax.axis_size(X)
    rows = lax.axis_size("rows")
    group = lax.axis_size((Z, Y))
    own_waves = kvec.shape[1] // rows
    waves = own_waves * group

    def floats(*dims):
        return jax.ShapeDtypeStruct(dims, F32)

    def halves(*dims):
        return jax.ShapeDtypeStruct(dims, BF16)

    payload = jnp.pad(feats, ((0, 8), (0, 0))) + jnp.pad(positions, ((slots, 5), (0, 0)))
    payload = payload + jnp.pad(kvec, ((slots + 4, 1), (0, width - kvec.shape[1])))
    payload = call(stamp(slots, cells), floats(*payload.shape), 2, alias={1: 0})(cell_counts, payload)
    near2 = lax.ppermute(payload, X, shift(X, 2))
    above = lax.ppermute(payload, X, shift(X, -1))
    below = lax.ppermute(payload, X, shift(X, 1))
    kv = call(pack(slots, own_waves, group), floats(group, 8, 128), 1)(payload)
    kv, again = lax.optimization_barrier((kv, payload))
    swap = shift("rows", 1)
    beside = lax.ppermute(again, "rows", swap)
    kv = lax.all_to_all(kv, (Z, Y), 0, 0, tiled=True)
    lhs = call(lattice(own_waves, group), halves(waves, 48), 1, [pltpu.VMEM((8, waves), F32)])(kv)

    unit = 12 * waves * slots * width

    def sums(chunks, first, *more):
        count = len(chunks)
        m = halves(count - 1 if first else count, 2 * waves, slots)
        return call(
            forward(cells, cell, count, own_waves, group, first),
            (floats(2 * waves, width), m, m),
            2 + count + len(more),
            flops=count * unit,
        )(lhs, w_val, *chunks, *more)

    m_own = call(own_trig(slots, own_waves, group), (halves(1, 2 * waves, slots),) * 2, 2, flops=unit)(lhs, payload)
    part, *m_beside = sums((payload, beside), True, *m_own)
    part, near2, above, below = lax.optimization_barrier((part, near2, above, below))
    line = (above, below, near2)
    other = [lax.ppermute(c, "rows", swap) for c in line]
    part, *m_line = sums(line, False, part)
    part, *m_other = sums(other, False, part)
    passed = call(line_end, floats(*payload.shape), 2)(below, above)
    part, passed = lax.optimization_barrier((part, passed))
    parts = lax.all_to_all(part.reshape(group, 2 * own_waves, width), (Z, Y), 0, 0, tiled=True)
    scale = 1.0 / math.sqrt(float(slots * devices) * float(waves * rows * nx))
    spread = call(filtered(scale), floats(*parts.shape), 2)(parts, filters)
    f = lax.all_to_all(spread, (Z, Y), 0, 0, tiled=True).reshape(2 * waves, width)

    one = floats(width, slots)

    def back(chunks, ft, m, *added):
        outs = (one,) * len(chunks)
        return call(backward(chunks), outs, 6 + len(added), flops=len(chunks) * unit)(*ft, *m, *added)

    theirs = *m_beside, *m_other
    mine = *m_own, *m_line
    far, *ft = call(backward_first(2), (one, *(halves(width, 2 * waves),) * 2), 3, flops=unit)(f, *m_other)
    there = lax.ppermute(far, "rows", swap)
    ft = lax.optimization_barrier((*ft, far))[:2]
    rest = [lax.ppermute(r, "rows", swap) for r in back(((0, 0), (1, 0), (1, 1)), ft, theirs)]
    (e3,) = back(((1, 2),), ft, mine, there)
    e3, passed, *ft = lax.optimization_barrier((e3, passed, *ft))
    e3 = lax.ppermute(e3, X, shift(X, 2))
    ends = [(d, (d + nx) % devices) for d in range(devices) if d % nx == 0]
    ends += [(d, (d - nx) % devices) for d in range(devices) if d % nx == nx - 1]
    edge = lax.ppermute(passed, ROWS_WAVES, ends)
    e0, e1, e2 = back(((0, 0), (1, 0), (1, 1)), ft, mine, *rest)
    e1 = lax.ppermute(e1, X, shift(X, 1))
    e2 = lax.ppermute(e2, X, shift(X, -1))

    base, mask = call(
        messages(cells, cell, cells * devices, neighbours.shape[1], nx - 1),
        (floats(slots, width), floats(slots, 128)),
        7,
        smem=(0, 1),
        flops=unit,
    )(neighbours, nbr_count, payload, below, above, edge, w_msg)
    (e0,) = call(pairs, (one,), 2)(e0, e3)
    return call(finish(), floats(slots, width), 7)(base, mask, e0, e1, e2, w_one, w_two)


def solution(mesh):
    torus = Mesh(mesh.devices.reshape(mesh.shape["rows"], 4, 4, 4), ROWS_WAVES)
    return jax.shard_map(
        shards,
        mesh=torus,
        in_specs=(
            P(ROWS_WAVES, None),
            P(None, ROWS_WAVES),
            P(ROWS_WAVES),
            P(ROWS_WAVES, None),
            P(ROWS_WAVES),
            P(None, WAVES),
            P(WAVES, None),
            P(),
            P(),
            P(),
            P(),
        ),
        out_specs=P(ROWS_WAVES, None),
        check_vma=False,
    )
```

```python
import math

import jax
import jax.numpy as jnp
from jax import lax
from jax.experimental import pallas as pl
from jax.experimental.pallas import tpu as pltpu
from jax.sharding import Mesh
from jax.sharding import PartitionSpec as P

Z, Y, X = "waves_0", "waves_1", "waves_2"
WAVES = (Z, Y, X)
ROWS_WAVES = ("rows", Z, Y, X)
F32 = jnp.float32
BF16 = jnp.bfloat16

SIN_POLY = (6.283185280154403, -10.33542015333633, 5.100154773052372, -1.1965808225334407, 0.15531182448662934)
COS_POLY = (0.999999953027512, -4.934792802489427, 4.058410790762133, -1.3318729727851486, 0.21968242357146)
ROUNDER = 12582912.0


def horner(coeffs, u):
    out = coeffs[-1]
    for c in coeffs[-2::-1]:
        out = out * u + c
    return out


def split(a):
    high = a.astype(BF16)
    return high, (a - high.astype(F32)).astype(BF16)


def thirds(a):
    high = a.astype(BF16).astype(F32)
    rest = a - high
    middle = rest.astype(BF16).astype(F32)
    return high, middle, rest - middle


def dot(a, b):
    return jnp.dot(a, b, preferred_element_type=F32)


def dot3(a, b):
    return dot(a[0], b[0]) + (dot(a[1], b[0]) + dot(a[0], b[1]))


def call(kernel, outs, n_in, scratch=(), smem=(), flops=0, alias={}, limit=8 << 20):
    def space(i):
        return pltpu.SMEM if i in smem else pltpu.VMEM

    return pl.pallas_call(
        kernel,
        out_shape=outs,
        in_specs=[pl.BlockSpec(memory_space=space(i)) for i in range(n_in)],
        out_specs=jax.tree.map(lambda _: pl.BlockSpec(memory_space=pltpu.VMEM), outs),
        scratch_shapes=scratch,
        input_output_aliases=alias,
        cost_estimate=pl.CostEstimate(flops=flops, bytes_accessed=1 << 16, transcendentals=0),
        compiler_params=pltpu.CompilerParams(vmem_limit_bytes=limit),
    )


def live_rows(block, cells, cell):
    slots = cells * cell
    row = lax.broadcasted_iota(jnp.int32, (slots, 1), 0).astype(F32)
    limit = block[slots + 3 : slots + 4, 0:1]
    for c in range(1, cells):
        limit = jnp.where(row < c * cell, limit, c * cell + block[slots + 3 : slots + 4, c : c + 1])
    return row < limit


def stamp(slots, cells):
    def kernel(counts, _, out):
        out[slots + 3 : slots + 4, 0:cells] = counts[...].astype(F32).reshape(1, cells)

    return kernel


def lattice(own, groups):
    def kernel(kv, out, flat):
        flat[...] = jnp.zeros(flat.shape, F32)
        pad = jnp.zeros((8, flat.shape[1] - 128), F32)
        for g in range(groups):
            flat[...] += pltpu.roll(jnp.concatenate([kv[g], pad], axis=1), g * own, 1)
        kh, km, kl = thirds(flat[...])
        out[...] = jnp.concatenate([kh, kh, km, kh, km, kl], axis=0).T.astype(BF16)

    return kernel


def pack(slots, own, groups):
    def kernel(own_block, out):
        rows = own_block[slots : slots + 8, :128] * (0.5 / math.pi)
        rows = pltpu.roll(rows, 4, 0)
        k = jnp.where(lax.axis_index("rows") == 0, rows, pltpu.roll(rows, 128 - own, 1))
        lane = lax.broadcasted_iota(jnp.int32, k.shape, 1)
        line = lax.broadcasted_iota(jnp.int32, k.shape, 0)
        k = jnp.where((lane < own) & (line < 3), k, 0.0)
        for g in range(groups):
            out[g] = k

    return kernel


def own_trig(slots, own, groups):
    def kernel(lhs, chunk, mh, ml):
        turns = dot(lhs[...], spots(chunk, slots))
        for g in range(groups):
            rows = slice(2 * own * g, 2 * own * (g + 1))
            mh[0, rows], ml[0, rows] = split(cos_and_sin(turns[g * own : (g + 1) * own]))

    return kernel


def spots(chunk, slots):
    x, y, z = thirds(jnp.where(lax.broadcasted_iota(jnp.int32, (8, slots), 0) < 3, chunk[slots : slots + 8], 0.0))
    return jnp.concatenate([x, y, x, z, y, x], axis=0).astype(BF16)


def cos_and_sin(t):
    f = t - ((t + ROUNDER) - ROUNDER)
    u = f * f
    s = f * horner(SIN_POLY, u)
    c = horner(COS_POLY, u)
    return jnp.concatenate([1.0 - 0.5 * (s * s), s * c], axis=0)


def forward(cells, cell, count, own, groups, first):
    slots = cells * cell

    def kernel(lhs, w_val, *refs):
        chunks, refs = refs[:count], refs[count:]
        if first:
            ready, refs = refs[:2], refs[2:]
        else:
            before, refs = refs[0], refs[1:]
        out, mh, ml = refs
        skip = 1 if first else 0
        w = split(w_val[...])
        turns, right = [], []
        for j, chunk in enumerate(chunks):
            live = live_rows(chunk, cells, cell)
            vh, vl = split(jnp.where(live, dot3(split(chunk[:slots]), w), 0.0))
            right += [vh, vh, vl]
            turns.append(dot(lhs[...], spots(chunk, slots)) if j >= skip else None)
        right = jnp.concatenate(right, axis=0)
        for part in range(2):
            for j in range(skip, count):
                for g in range(part * groups // 2, (part + 1) * groups // 2):
                    rows = slice(2 * own * g, 2 * own * (g + 1))
                    pieces = split(cos_and_sin(turns[j][g * own : (g + 1) * own]))
                    mh[j - skip, rows], ml[j - skip, rows] = pieces
            rows = slice(part * own * groups, (part + 1) * own * groups)
            pairs_of = [(ready[0][0, rows], ready[1][0, rows])] if first else []
            pairs_of += [(mh[j, rows], ml[j, rows]) for j in range(count - skip)]
            left = [m for high, low in pairs_of for m in (high, low, high)]
            total = dot(jnp.concatenate(left, axis=1), right)
            out[rows] = total if first else before[rows] + total

    return kernel


def filtered(scale):
    def kernel(parts, filters, out):
        groups, double, _ = parts.shape
        own = double // 2
        f = jnp.where(lax.axis_index("rows") == 0, filters[:own], filters[own:]) * scale
        total = parts[0]
        for g in range(1, groups):
            total = total + parts[g]
        total = total * jnp.concatenate([f, f], axis=0)
        for g in range(groups):
            out[g] = total

    return kernel


def line_end(below, above, out):
    out[...] = jnp.where(lax.axis_index(X) == 0, below[...], above[...])


def backward_first(at):
    def kernel(f, mh, ml, out, high, low):
        ft = split(f[...].T)
        high[...], low[...] = ft
        out[0] = dot3(ft, (mh[at], ml[at]))

    return kernel


def backward(chunks, stacked, adds):
    def kernel(fh, fl, mh0, ml0, mh1, ml1, *refs):
        added, outs = refs[0] if adds else None, refs[1:] if adds else refs
        for j, (rest, at) in enumerate(chunks):
            part = dot3((fh[...], fl[...]), (mh1[at], ml1[at]) if rest else (mh0[at], ml0[at]))
            part = part + added[j] if adds else part
            if stacked:
                outs[0][j] = part
            else:
                outs[j][...] = part

    return kernel


def pairs(*refs):
    count = len(refs) // 3
    for a, b, out in zip(refs[:count], refs[count : 2 * count], refs[2 * count :]):
        out[...] = a[...] + b[...]


def messages(cells, cell, cells_all, nb, last):
    slots = cells * cell

    def kernel(neighbours, nbr_count, own, low, high, edge, w_msg, out, mask):
        x, first = lax.axis_index(X), lax.axis_index(ROWS_WAVES) * cells
        lo = jnp.where(x == 0, edge[...], low[...])
        hi = jnp.where(x == last, edge[...], high[...])
        blocks = (lo, own[...], hi)
        masks = [live_rows(b, cells, cell) for b in blocks]
        parts = [split(jnp.where(m, b[:slots], 0.0)) for m, b in zip(masks, blocks)]
        wide = [tuple(p[k][c * cell : (c + 1) * cell] for k in range(2)) for p in parts for c in range(cells)]
        pos = [
            b[slots : slots + 3, c * cell : (c + 1) * cell] for b in blocks for c in range(cells)
        ]
        cols = own[slots : slots + 8].T
        eye = lax.broadcasted_iota(jnp.int32, (cell, cell), 0) == lax.broadcasted_iota(jnp.int32, (cell, cell), 1)
        gathered = []
        for c in range(cells):
            mine = cols[c * cell : (c + 1) * cell]
            acc = None
            for step in range(2 * cells + 1):
                other = c + step
                local = other - cells
                target = lax.rem(first + local + cells_all, cells_all)
                listed = jnp.float32(0.0)
                for b in range(nb):
                    hit = (neighbours[c, b] == target) & (b < nbr_count[c])
                    listed = listed + jnp.where(hit, jnp.float32(1.0), jnp.float32(0.0))
                near = pos[other]
                d0 = mine[:, 0:1] - near[0:1]
                d1 = mine[:, 1:2] - near[1:2]
                d2 = mine[:, 2:3] - near[2:3]
                weight = jnp.exp(-0.125 * (d0 * d0 + d1 * d1 + d2 * d2)) * listed
                if step == cells:
                    weight = jnp.where(eye, 0.0, weight)
                part = dot3(split(weight), wide[other])
                acc = part if acc is None else acc + part
            gathered.append(acc)
        total = jnp.concatenate(gathered, axis=0)
        live = masks[1]
        msg = 0.125 * dot3(split(total), split(w_msg[...]))
        out[...] = own[:slots] + jnp.where(live, msg, 0.0)
        mask[...] = jnp.broadcast_to(jnp.where(live, 1.0, 0.0), mask.shape)

    return kernel


def finish():
    def kernel(base, mask, a, b, c, w_one, w_two, out):
        spectral = a[...] + (b[...] + c[...])
        u = base[...] + spectral.T
        normed = u / jnp.sqrt(jnp.mean(u * u, axis=1, keepdims=True) + 1e-06)
        v = dot3(split(normed), split(w_one[...]))
        hidden = v / (1.0 + jnp.exp(-v))
        out[...] = (u + dot3(split(hidden), split(w_two[...]))) * mask[:, 0:1]

    return kernel


def shift(axis, by):
    size = lax.axis_size(axis)
    return [(i, (i + by) % size) for i in range(size)]


def shards(
    feats, positions, cell_counts, neighbours, nbr_count, kvec, filters, w_msg, w_val, w_one, w_two
):
    cells = cell_counts.shape[0]
    slots, width = feats.shape
    cell = slots // cells
    devices = lax.axis_size(ROWS_WAVES)
    nx = lax.axis_size(X)
    rows = lax.axis_size("rows")
    group = lax.axis_size((Z, Y))
    own_waves = kvec.shape[1] // rows
    waves = own_waves * group

    def floats(*dims):
        return jax.ShapeDtypeStruct(dims, F32)

    def halves(*dims):
        return jax.ShapeDtypeStruct(dims, BF16)

    payload = jnp.pad(feats, ((0, 8), (0, 0))) + jnp.pad(positions, ((slots, 5), (0, 0)))
    payload = payload + jnp.pad(kvec, ((slots + 4, 1), (0, width - kvec.shape[1])))
    payload = call(stamp(slots, cells), floats(*payload.shape), 2, alias={1: 0})(cell_counts, payload)
    near2 = lax.ppermute(payload, X, shift(X, 2))
    above = lax.ppermute(payload, X, shift(X, -1))
    below = lax.ppermute(payload, X, shift(X, 1))
    kv = call(pack(slots, own_waves, group), floats(group, 8, 128), 1)(payload)
    kv, again = lax.optimization_barrier((kv, payload))
    swap = shift("rows", 1)
    beside = lax.ppermute(again, "rows", swap)
    kv = lax.all_to_all(kv, (Z, Y), 0, 0, tiled=True)
    lhs = call(lattice(own_waves, group), halves(waves, 48), 1, [pltpu.VMEM((8, waves), F32)])(kv)

    unit = 12 * waves * slots * width

    def sums(chunks, first, *more):
        count = len(chunks)
        m = halves(count - 1 if first else count, 2 * waves, slots)
        return call(
            forward(cells, cell, count, own_waves, group, first),
            (floats(2 * waves, width), m, m),
            2 + count + len(more),
            flops=count * unit,
        )(lhs, w_val, *chunks, *more)

    m_own = call(own_trig(slots, own_waves, group), (halves(1, 2 * waves, slots),) * 2, 2, flops=unit)(lhs, payload)
    part, *m_beside = sums((payload, beside), True, *m_own)
    part, near2, above, below = lax.optimization_barrier((part, near2, above, below))
    line = (above, below, near2)
    other = [lax.ppermute(c, "rows", swap) for c in line]
    part, *m_line = sums(line, False, part)
    part, *m_other = sums(other, False, part)
    passed = call(line_end, floats(*payload.shape), 2)(below, above)
    part, passed = lax.optimization_barrier((part, passed))
    parts = lax.all_to_all(part.reshape(group, 2 * own_waves, width), (Z, Y), 0, 0, tiled=True)
    scale = 1.0 / math.sqrt(float(slots * devices) * float(waves * rows * nx))
    spread = call(filtered(scale), floats(*parts.shape), 2)(parts, filters)
    f = lax.all_to_all(spread, (Z, Y), 0, 0, tiled=True).reshape(2 * waves, width)

    one = floats(width, slots)

    def back(chunks, ft, m, *added, stacked=False):
        count = len(chunks)
        outs = floats(count, width, slots) if stacked else (one,) * count
        kernel = backward(chunks, stacked, bool(added))
        return call(kernel, outs, 6 + len(added), flops=count * unit)(*ft, *m, *added)

    theirs = *m_beside, *m_other
    mine = *m_own, *m_line
    outs = floats(1, width, slots), *(halves(width, 2 * waves),) * 2
    far, *ft = call(backward_first(2), outs, 3, flops=unit)(f, *m_other)
    there = lax.ppermute(far, "rows", swap)
    ft = lax.optimization_barrier((*ft, far))[:2]
    rest = back(((0, 0), (1, 0), (1, 1)), ft, theirs, stacked=True)
    (e3,) = back(((1, 2),), ft, mine, there)
    e3, passed, rest, *ft = lax.optimization_barrier((e3, passed, rest, *ft))
    rest = lax.ppermute(rest, "rows", swap)
    e3 = lax.ppermute(e3, X, shift(X, 2))
    ends = [(d, (d + nx) % devices) for d in range(devices) if d % nx == 0]
    ends += [(d, (d - nx) % devices) for d in range(devices) if d % nx == nx - 1]
    edge = lax.ppermute(passed, ROWS_WAVES, ends)
    e0, e1, e2 = back(((0, 0), (1, 0), (1, 1)), ft, mine, rest)
    e1 = lax.ppermute(e1, X, shift(X, 1))
    e2 = lax.ppermute(e2, X, shift(X, -1))

    base, mask = call(
        messages(cells, cell, cells * devices, neighbours.shape[1], nx - 1),
        (floats(slots, width), floats(slots, 128)),
        7,
        smem=(0, 1),
        flops=unit,
    )(neighbours, nbr_count, payload, below, above, edge, w_msg)
    (e0,) = call(pairs, (one,), 2)(e0, e3)
    return call(finish(), floats(slots, width), 7)(base, mask, e0, e1, e2, w_one, w_two)


def solution(mesh):
    torus = Mesh(mesh.devices.reshape(mesh.shape["rows"], 4, 4, 4), ROWS_WAVES)
    return jax.shard_map(
        shards,
        mesh=torus,
        in_specs=(
            P(ROWS_WAVES, None),
            P(None, ROWS_WAVES),
            P(ROWS_WAVES),
            P(ROWS_WAVES, None),
            P(ROWS_WAVES),
            P(None, WAVES),
            P(WAVES, None),
            P(),
            P(),
            P(),
            P(),
        ),
        out_specs=P(ROWS_WAVES, None),
        check_vma=False,
    )
```

```python
import math

import jax
import jax.numpy as jnp
from jax import lax
from jax.experimental import pallas as pl
from jax.experimental.pallas import tpu as pltpu
from jax.sharding import Mesh
from jax.sharding import PartitionSpec as P

Z, Y, X = "waves_0", "waves_1", "waves_2"
WAVES = (Z, Y, X)
ROWS_WAVES = ("rows", Z, Y, X)
F32 = jnp.float32
BF16 = jnp.bfloat16

SIN_POLY = (6.283185280154403, -10.33542015333633, 5.100154773052372, -1.1965808225334407, 0.15531182448662934)
COS_POLY = (0.999999953027512, -4.934792802489427, 4.058410790762133, -1.3318729727851486, 0.21968242357146)
ROUNDER = 12582912.0


def horner(coeffs, u):
    out = coeffs[-1]
    for c in coeffs[-2::-1]:
        out = out * u + c
    return out


def split(a):
    high = a.astype(BF16)
    return high, (a - high.astype(F32)).astype(BF16)


def thirds(a):
    high = a.astype(BF16).astype(F32)
    rest = a - high
    middle = rest.astype(BF16).astype(F32)
    return high, middle, rest - middle


def dot(a, b):
    return jnp.dot(a, b, preferred_element_type=F32)


def dot3(a, b):
    return dot(a[0], b[0]) + (dot(a[1], b[0]) + dot(a[0], b[1]))


def call(kernel, outs, n_in, scratch=(), smem=(), flops=0, alias={}, limit=8 << 20):
    def space(i):
        return pltpu.SMEM if i in smem else pltpu.VMEM

    return pl.pallas_call(
        kernel,
        out_shape=outs,
        in_specs=[pl.BlockSpec(memory_space=space(i)) for i in range(n_in)],
        out_specs=jax.tree.map(lambda _: pl.BlockSpec(memory_space=pltpu.VMEM), outs),
        scratch_shapes=scratch,
        input_output_aliases=alias,
        cost_estimate=pl.CostEstimate(flops=flops, bytes_accessed=1 << 16, transcendentals=0),
        compiler_params=pltpu.CompilerParams(vmem_limit_bytes=limit),
    )


def live_rows(block, cells, cell):
    slots = cells * cell
    row = lax.broadcasted_iota(jnp.int32, (slots, 1), 0).astype(F32)
    limit = block[slots + 3 : slots + 4, 0:1]
    for c in range(1, cells):
        limit = jnp.where(row < c * cell, limit, c * cell + block[slots + 3 : slots + 4, c : c + 1])
    return row < limit


def stamp(slots, cells):
    def kernel(counts, _, out):
        out[slots + 3 : slots + 4, 0:cells] = counts[...].astype(F32).reshape(1, cells)

    return kernel


def lattice(own, groups):
    def kernel(kv, out, flat):
        flat[...] = jnp.zeros(flat.shape, F32)
        pad = jnp.zeros((8, flat.shape[1] - 128), F32)
        for g in range(groups):
            flat[...] += pltpu.roll(jnp.concatenate([kv[g], pad], axis=1), g * own, 1)
        kh, km, kl = thirds(flat[...])
        out[...] = jnp.concatenate([kh, kh, km, kh, km, kl], axis=0).T.astype(BF16)

    return kernel


def pack(slots, own, groups):
    def kernel(own_block, out):
        rows = own_block[slots : slots + 8, :128] * (0.5 / math.pi)
        rows = pltpu.roll(rows, 4, 0)
        k = jnp.where(lax.axis_index("rows") == 0, rows, pltpu.roll(rows, 128 - own, 1))
        lane = lax.broadcasted_iota(jnp.int32, k.shape, 1)
        line = lax.broadcasted_iota(jnp.int32, k.shape, 0)
        k = jnp.where((lane < own) & (line < 3), k, 0.0)
        for g in range(groups):
            out[g] = k

    return kernel


def own_trig(slots, own, groups):
    def kernel(lhs, chunk, mh, ml):
        turns = dot(lhs[...], spots(chunk, slots))
        for g in range(groups):
            rows = slice(2 * own * g, 2 * own * (g + 1))
            mh[0, rows], ml[0, rows] = split(cos_and_sin(turns[g * own : (g + 1) * own]))

    return kernel


def spots(chunk, slots):
    x, y, z = thirds(jnp.where(lax.broadcasted_iota(jnp.int32, (8, slots), 0) < 3, chunk[slots : slots + 8], 0.0))
    return jnp.concatenate([x, y, x, z, y, x], axis=0).astype(BF16)


def cos_and_sin(t):
    f = t - ((t + ROUNDER) - ROUNDER)
    u = f * f
    s = f * horner(SIN_POLY, u)
    c = horner(COS_POLY, u)
    return jnp.concatenate([1.0 - 0.5 * (s * s), s * c], axis=0)


def forward(cells, cell, count, own, groups, first):
    slots = cells * cell

    def kernel(lhs, w_val, *refs):
        chunks, refs = refs[:count], refs[count:]
        if first:
            ready, refs = refs[:2], refs[2:]
        else:
            before, refs = refs[0], refs[1:]
        out, mh, ml = refs
        skip = 1 if first else 0
        w = split(w_val[...])
        turns, right = [], []
        for j, chunk in enumerate(chunks):
            live = live_rows(chunk, cells, cell)
            vh, vl = split(jnp.where(live, dot3(split(chunk[:slots]), w), 0.0))
            right += [vh, vh, vl]
            turns.append(dot(lhs[...], spots(chunk, slots)) if j >= skip else None)
        right = jnp.concatenate(right, axis=0)
        for part in range(2):
            for j in range(skip, count):
                for g in range(part * groups // 2, (part + 1) * groups // 2):
                    rows = slice(2 * own * g, 2 * own * (g + 1))
                    pieces = split(cos_and_sin(turns[j][g * own : (g + 1) * own]))
                    mh[j - skip, rows], ml[j - skip, rows] = pieces
            rows = slice(part * own * groups, (part + 1) * own * groups)
            pairs_of = [(ready[0][0, rows], ready[1][0, rows])] if first else []
            pairs_of += [(mh[j, rows], ml[j, rows]) for j in range(count - skip)]
            left = [m for high, low in pairs_of for m in (high, low, high)]
            total = dot(jnp.concatenate(left, axis=1), right)
            out[rows] = total if first else before[rows] + total

    return kernel


def filtered(scale):
    def kernel(parts, filters, out):
        groups, double, _ = parts.shape
        own = double // 2
        f = jnp.where(lax.axis_index("rows") == 0, filters[:own], filters[own:]) * scale
        total = parts[0]
        for g in range(1, groups):
            total = total + parts[g]
        total = total * jnp.concatenate([f, f], axis=0)
        for g in range(groups):
            out[g] = total

    return kernel


def line_end(below, above, out):
    out[...] = jnp.where(lax.axis_index(X) == 0, below[...], above[...])


def backward_first(at):
    def kernel(f, mh, ml, out, high, low):
        ft = split(f[...].T)
        high[...], low[...] = ft
        out[0] = dot3(ft, (mh[at], ml[at]))

    return kernel


def backward(chunks, stacked, adds):
    def kernel(fh, fl, mh0, ml0, mh1, ml1, *refs):
        added, outs = refs[0] if adds else None, refs[1:] if adds else refs
        for j, (rest, at) in enumerate(chunks):
            part = dot3((fh[...], fl[...]), (mh1[at], ml1[at]) if rest else (mh0[at], ml0[at]))
            part = part + added[j] if adds else part
            if stacked:
                outs[0][j] = part
            else:
                outs[j][...] = part

    return kernel


def pairs(*refs):
    count = len(refs) // 3
    for a, b, out in zip(refs[:count], refs[count : 2 * count], refs[2 * count :]):
        out[...] = a[...] + b[...]


def messages(cells, cell, cells_all, nb, last):
    slots = cells * cell

    def kernel(neighbours, nbr_count, own, low, high, edge, w_msg, out, mask):
        x, first = lax.axis_index(X), lax.axis_index(ROWS_WAVES) * cells
        lo = jnp.where(x == 0, edge[...], low[...])
        hi = jnp.where(x == last, edge[...], high[...])
        blocks = (lo, own[...], hi)
        masks = [live_rows(b, cells, cell) for b in blocks]
        parts = [split(jnp.where(m, b[:slots], 0.0)) for m, b in zip(masks, blocks)]
        wide = [tuple(p[k][c * cell : (c + 1) * cell] for k in range(2)) for p in parts for c in range(cells)]
        pos = [
            b[slots : slots + 3, c * cell : (c + 1) * cell] for b in blocks for c in range(cells)
        ]
        cols = own[slots : slots + 8].T
        eye = lax.broadcasted_iota(jnp.int32, (cell, cell), 0) == lax.broadcasted_iota(jnp.int32, (cell, cell), 1)
        gathered = []
        for c in range(cells):
            mine = cols[c * cell : (c + 1) * cell]
            acc = None
            for step in range(2 * cells + 1):
                other = c + step
                local = other - cells
                target = lax.rem(first + local + cells_all, cells_all)
                listed = jnp.float32(0.0)
                for b in range(nb):
                    hit = (neighbours[c, b] == target) & (b < nbr_count[c])
                    listed = listed + jnp.where(hit, jnp.float32(1.0), jnp.float32(0.0))
                near = pos[other]
                d0 = mine[:, 0:1] - near[0:1]
                d1 = mine[:, 1:2] - near[1:2]
                d2 = mine[:, 2:3] - near[2:3]
                weight = jnp.exp(-0.125 * (d0 * d0 + d1 * d1 + d2 * d2)) * listed
                if step == cells:
                    weight = jnp.where(eye, 0.0, weight)
                part = dot3(split(weight), wide[other])
                acc = part if acc is None else acc + part
            gathered.append(acc)
        total = jnp.concatenate(gathered, axis=0)
        live = masks[1]
        msg = 0.125 * dot3(split(total), split(w_msg[...]))
        out[...] = own[:slots] + jnp.where(live, msg, 0.0)
        mask[...] = jnp.broadcast_to(jnp.where(live, 1.0, 0.0), mask.shape)

    return kernel


def finish():
    def kernel(base, mask, a, b, c, w_one, w_two, out):
        spectral = a[...] + (b[...] + c[...])
        u = base[...] + spectral.T
        normed = u / jnp.sqrt(jnp.mean(u * u, axis=1, keepdims=True) + 1e-06)
        v = dot3(split(normed), split(w_one[...]))
        hidden = v / (1.0 + jnp.exp(-v))
        out[...] = (u + dot3(split(hidden), split(w_two[...]))) * mask[:, 0:1]

    return kernel


def shift(axis, by):
    size = lax.axis_size(axis)
    return [(i, (i + by) % size) for i in range(size)]


def shards(
    feats, positions, cell_counts, neighbours, nbr_count, kvec, filters, w_msg, w_val, w_one, w_two
):
    cells = cell_counts.shape[0]
    slots, width = feats.shape
    cell = slots // cells
    devices = lax.axis_size(ROWS_WAVES)
    nx = lax.axis_size(X)
    rows = lax.axis_size("rows")
    group = lax.axis_size((Z, Y))
    own_waves = kvec.shape[1] // rows
    waves = own_waves * group

    def floats(*dims):
        return jax.ShapeDtypeStruct(dims, F32)

    def halves(*dims):
        return jax.ShapeDtypeStruct(dims, BF16)

    payload = jnp.pad(feats, ((0, 8), (0, 0))) + jnp.pad(positions, ((slots, 5), (0, 0)))
    payload = payload + jnp.pad(kvec, ((slots + 4, 1), (0, width - kvec.shape[1])))
    payload = call(stamp(slots, cells), floats(*payload.shape), 2, alias={1: 0})(cell_counts, payload)
    near2 = lax.ppermute(payload, X, shift(X, 2))
    above = lax.ppermute(payload, X, shift(X, -1))
    below = lax.ppermute(payload, X, shift(X, 1))
    kv = call(pack(slots, own_waves, group), floats(group, 8, 128), 1)(payload)
    kv, again = lax.optimization_barrier((kv, payload))
    swap = shift("rows", 1)
    beside = lax.ppermute(again, "rows", swap)
    kv = lax.all_to_all(kv, (Z, Y), 0, 0, tiled=True)
    lhs = call(lattice(own_waves, group), halves(waves, 48), 1, [pltpu.VMEM((8, waves), F32)])(kv)

    unit = 12 * waves * slots * width

    def sums(chunks, first, *more):
        count = len(chunks)
        m = halves(count - 1 if first else count, 2 * waves, slots)
        return call(
            forward(cells, cell, count, own_waves, group, first),
            (floats(2 * waves, width), m, m),
            2 + count + len(more),
            flops=count * unit,
        )(lhs, w_val, *chunks, *more)

    m_own = call(own_trig(slots, own_waves, group), (halves(1, 2 * waves, slots),) * 2, 2, flops=unit)(lhs, payload)
    part, *m_beside = sums((payload, beside), True, *m_own)
    part, near2, above, below = lax.optimization_barrier((part, near2, above, below))
    line = (above, below, near2)
    other = [lax.ppermute(c, "rows", swap) for c in line]
    part, *m_line = sums(line, False, part)
    part, *m_other = sums(other, False, part)
    passed = call(line_end, floats(*payload.shape), 2)(below, above)
    part, passed = lax.optimization_barrier((part, passed))
    parts = lax.all_to_all(part.reshape(group, 2 * own_waves, width), (Z, Y), 0, 0, tiled=True)
    scale = 1.0 / math.sqrt(float(slots * devices) * float(waves * rows * nx))
    spread = call(filtered(scale), floats(*parts.shape), 2)(parts, filters)
    f = lax.all_to_all(spread, (Z, Y), 0, 0, tiled=True).reshape(2 * waves, width)

    f, passed = lax.optimization_barrier((f, passed))
    ends = [(d, (d + nx) % devices) for d in range(devices) if d % nx == 0]
    ends += [(d, (d - nx) % devices) for d in range(devices) if d % nx == nx - 1]
    edge = lax.ppermute(passed, ROWS_WAVES, ends)
    one = floats(width, slots)

    def back(chunks, ft, m, *added, stacked=False):
        count = len(chunks)
        outs = floats(count, width, slots) if stacked else (one,) * count
        kernel = backward(chunks, stacked, bool(added))
        return call(kernel, outs, 6 + len(added), flops=count * unit)(*ft, *m, *added)

    theirs = *m_beside, *m_other
    mine = *m_own, *m_line
    outs = floats(1, width, slots), *(halves(width, 2 * waves),) * 2
    far, *ft = call(backward_first(2), outs, 3, flops=unit)(f, *m_other)
    there = lax.ppermute(far, "rows", swap)
    ft = lax.optimization_barrier((*ft, far))[:2]
    rest = back(((0, 0), (1, 0), (1, 1)), ft, theirs, stacked=True)
    (e3,) = back(((1, 2),), ft, mine, there)
    e3, rest, *ft = lax.optimization_barrier((e3, rest, *ft))
    rest = lax.ppermute(rest, "rows", swap)
    e3 = lax.ppermute(e3, X, shift(X, 2))
    e0, e1, e2 = back(((0, 0), (1, 0), (1, 1)), ft, mine, rest)
    e1 = lax.ppermute(e1, X, shift(X, 1))
    e2 = lax.ppermute(e2, X, shift(X, -1))

    base, mask = call(
        messages(cells, cell, cells * devices, neighbours.shape[1], nx - 1),
        (floats(slots, width), floats(slots, 128)),
        7,
        smem=(0, 1),
        flops=unit,
    )(neighbours, nbr_count, payload, below, above, edge, w_msg)
    (e0,) = call(pairs, (one,), 2)(e0, e3)
    return call(finish(), floats(slots, width), 7)(base, mask, e0, e1, e2, w_one, w_two)


def solution(mesh):
    torus = Mesh(mesh.devices.reshape(mesh.shape["rows"], 4, 4, 4), ROWS_WAVES)
    return jax.shard_map(
        shards,
        mesh=torus,
        in_specs=(
            P(ROWS_WAVES, None),
            P(None, ROWS_WAVES),
            P(ROWS_WAVES),
            P(ROWS_WAVES, None),
            P(ROWS_WAVES),
            P(None, WAVES),
            P(WAVES, None),
            P(),
            P(),
            P(),
            P(),
        ),
        out_specs=P(ROWS_WAVES, None),
        check_vma=False,
    )
```

```python
import math

import jax
import jax.numpy as jnp
from jax import lax
from jax.experimental import pallas as pl
from jax.experimental.pallas import tpu as pltpu
from jax.sharding import Mesh
from jax.sharding import PartitionSpec as P

Z, Y, X = "waves_0", "waves_1", "waves_2"
WAVES = (Z, Y, X)
ROWS_WAVES = ("rows", Z, Y, X)
F32 = jnp.float32
BF16 = jnp.bfloat16

SIN_POLY = (6.283185280154403, -10.33542015333633, 5.100154773052372, -1.1965808225334407, 0.15531182448662934)
COS_POLY = (0.999999953027512, -4.934792802489427, 4.058410790762133, -1.3318729727851486, 0.21968242357146)
ROUNDER = 12582912.0


def horner(coeffs, u):
    out = coeffs[-1]
    for c in coeffs[-2::-1]:
        out = out * u + c
    return out


def split(a):
    high = a.astype(BF16)
    return high, (a - high.astype(F32)).astype(BF16)


def thirds(a):
    high = a.astype(BF16).astype(F32)
    rest = a - high
    middle = rest.astype(BF16).astype(F32)
    return high, middle, rest - middle


def dot(a, b):
    return jnp.dot(a, b, preferred_element_type=F32)


def dot3(a, b):
    return dot(a[0], b[0]) + (dot(a[1], b[0]) + dot(a[0], b[1]))


def call(kernel, outs, n_in, scratch=(), smem=(), flops=0, alias={}, limit=8 << 20):
    def space(i):
        return pltpu.SMEM if i in smem else pltpu.VMEM

    return pl.pallas_call(
        kernel,
        out_shape=outs,
        in_specs=[pl.BlockSpec(memory_space=space(i)) for i in range(n_in)],
        out_specs=jax.tree.map(lambda _: pl.BlockSpec(memory_space=pltpu.VMEM), outs),
        scratch_shapes=scratch,
        input_output_aliases=alias,
        cost_estimate=pl.CostEstimate(flops=flops, bytes_accessed=1 << 16, transcendentals=0),
        compiler_params=pltpu.CompilerParams(vmem_limit_bytes=limit),
    )


def live_rows(block, cells, cell):
    slots = cells * cell
    row = lax.broadcasted_iota(jnp.int32, (slots, 1), 0).astype(F32)
    limit = block[slots + 3 : slots + 4, 0:1]
    for c in range(1, cells):
        limit = jnp.where(row < c * cell, limit, c * cell + block[slots + 3 : slots + 4, c : c + 1])
    return row < limit


def stamp(slots, cells):
    def kernel(counts, _, out):
        out[slots + 3 : slots + 4, 0:cells] = counts[...].astype(F32).reshape(1, cells)

    return kernel


def lattice(own, groups):
    def kernel(kv, out, flat):
        flat[...] = jnp.zeros(flat.shape, F32)
        pad = jnp.zeros((8, flat.shape[1] - 128), F32)
        for g in range(groups):
            flat[...] += pltpu.roll(jnp.concatenate([kv[g], pad], axis=1), g * own, 1)
        kh, km, kl = thirds(flat[...])
        out[...] = jnp.concatenate([kh, kh, km, kh, km, kl], axis=0).T.astype(BF16)

    return kernel


def pack(slots, own, groups):
    def kernel(own_block, out):
        rows = own_block[slots : slots + 8, :128] * (0.5 / math.pi)
        rows = pltpu.roll(rows, 4, 0)
        k = jnp.where(lax.axis_index("rows") == 0, rows, pltpu.roll(rows, 128 - own, 1))
        lane = lax.broadcasted_iota(jnp.int32, k.shape, 1)
        line = lax.broadcasted_iota(jnp.int32, k.shape, 0)
        k = jnp.where((lane < own) & (line < 3), k, 0.0)
        for g in range(groups):
            out[g] = k

    return kernel


def own_trig(slots, own, groups):
    def kernel(lhs, chunk, mh, ml):
        turns = dot(lhs[...], spots(chunk, slots))
        for g in range(groups):
            rows = slice(2 * own * g, 2 * own * (g + 1))
            mh[0, rows], ml[0, rows] = split(cos_and_sin(turns[g * own : (g + 1) * own]))

    return kernel


def spots(chunk, slots):
    x, y, z = thirds(jnp.where(lax.broadcasted_iota(jnp.int32, (8, slots), 0) < 3, chunk[slots : slots + 8], 0.0))
    return jnp.concatenate([x, y, x, z, y, x], axis=0).astype(BF16)


def cos_and_sin(t):
    f = t - ((t + ROUNDER) - ROUNDER)
    u = f * f
    s = f * horner(SIN_POLY, u)
    c = horner(COS_POLY, u)
    return jnp.concatenate([1.0 - 0.5 * (s * s), s * c], axis=0)


def forward(cells, cell, count, own, groups, first):
    slots = cells * cell

    def kernel(lhs, w_val, *refs):
        chunks, refs = refs[:count], refs[count:]
        if first:
            ready, refs = refs[:2], refs[2:]
        else:
            before, refs = refs[0], refs[1:]
        out, mh, ml = refs
        skip = 1 if first else 0
        w = split(w_val[...])
        turns, right = [], []
        for j, chunk in enumerate(chunks):
            live = live_rows(chunk, cells, cell)
            vh, vl = split(jnp.where(live, dot3(split(chunk[:slots]), w), 0.0))
            right += [vh, vh, vl]
            turns.append(dot(lhs[...], spots(chunk, slots)) if j >= skip else None)
        right = jnp.concatenate(right, axis=0)
        for part in range(2):
            for j in range(skip, count):
                for g in range(part * groups // 2, (part + 1) * groups // 2):
                    rows = slice(2 * own * g, 2 * own * (g + 1))
                    pieces = split(cos_and_sin(turns[j][g * own : (g + 1) * own]))
                    mh[j - skip, rows], ml[j - skip, rows] = pieces
            rows = slice(part * own * groups, (part + 1) * own * groups)
            pairs_of = [(ready[0][0, rows], ready[1][0, rows])] if first else []
            pairs_of += [(mh[j, rows], ml[j, rows]) for j in range(count - skip)]
            left = [m for high, low in pairs_of for m in (high, low, high)]
            total = dot(jnp.concatenate(left, axis=1), right)
            out[rows] = total if first else before[rows] + total

    return kernel


def filtered(scale):
    def kernel(parts, filters, out):
        groups, double, _ = parts.shape
        own = double // 2
        f = jnp.where(lax.axis_index("rows") == 0, filters[:own], filters[own:]) * scale
        total = parts[0]
        for g in range(1, groups):
            total = total + parts[g]
        total = total * jnp.concatenate([f, f], axis=0)
        for g in range(groups):
            out[g] = total

    return kernel


def line_end(below, above, out):
    out[...] = jnp.where(lax.axis_index(X) == 0, below[...], above[...])


def backward_first(at):
    def kernel(f, mh, ml, out, high, low):
        ft = split(f[...].T)
        high[...], low[...] = ft
        out[0] = dot3(ft, (mh[at], ml[at]))

    return kernel


def backward(chunks, stacked, adds):
    def kernel(fh, fl, mh0, ml0, mh1, ml1, *refs):
        added, outs = refs[0] if adds else None, refs[1:] if adds else refs
        for j, (rest, at) in enumerate(chunks):
            part = dot3((fh[...], fl[...]), (mh1[at], ml1[at]) if rest else (mh0[at], ml0[at]))
            part = part + added[j] if adds else part
            if stacked:
                outs[0][j] = part
            else:
                outs[j][...] = part

    return kernel


def pairs(*refs):
    count = len(refs) // 3
    for a, b, out in zip(refs[:count], refs[count : 2 * count], refs[2 * count :]):
        out[...] = a[...] + b[...]


def listed_factor(neighbours, nbr_count, c, target, nb):
    listed = jnp.float32(0.0)
    for b in range(nb):
        hit = (neighbours[c, b] == target) & (b < nbr_count[c])
        listed = listed + jnp.where(hit, jnp.float32(1.0), jnp.float32(0.0))
    return listed


def gather(neighbours, nbr_count, mine, blocks, use, cells, cell, cells_all, nb):
    slots = cells * cell
    first = lax.axis_index(ROWS_WAVES) * cells
    wide, pos = {}, {}
    for k in use:
        live = live_rows(blocks[k], cells, cell)
        halves = split(jnp.where(live, blocks[k][:slots], 0.0))
        for c in range(cells):
            wide[k * cells + c] = tuple(p[c * cell : (c + 1) * cell] for p in halves)
            pos[k * cells + c] = blocks[k][slots : slots + 3, c * cell : (c + 1) * cell]
    eye = lax.broadcasted_iota(jnp.int32, (cell, cell), 0) == lax.broadcasted_iota(jnp.int32, (cell, cell), 1)
    gathered = []
    for c in range(cells):
        here = mine[c * cell : (c + 1) * cell]
        acc = jnp.zeros((cell, blocks[use[0]].shape[1]), F32)
        for step in range(2 * cells + 1):
            other = c + step
            if other not in wide:
                continue
            target = lax.rem(first + other - cells + cells_all, cells_all)
            near = pos[other]
            d0 = here[:, 0:1] - near[0:1]
            d1 = here[:, 1:2] - near[1:2]
            d2 = here[:, 2:3] - near[2:3]
            weight = jnp.exp(-0.125 * (d0 * d0 + d1 * d1 + d2 * d2))
            weight = weight * listed_factor(neighbours, nbr_count, c, target, nb)
            if step == cells:
                weight = jnp.where(eye, 0.0, weight)
            acc = acc + dot3(split(weight), wide[other])
        gathered.append(acc)
    return jnp.concatenate(gathered, axis=0)


def messages(cells, cell, cells_all, nb, last):
    slots = cells * cell

    def kernel(neighbours, nbr_count, own, low, high, w_msg, out, mask):
        x = lax.axis_index(X)
        lo = jnp.where(x == 0, 0.0, low[...])
        hi = jnp.where(x == last, 0.0, high[...])
        blocks = lo, own[...], hi
        mine = own[slots : slots + 8].T
        total = gather(neighbours, nbr_count, mine, blocks, (0, 1, 2), cells, cell, cells_all, nb)
        live = live_rows(own, cells, cell)
        msg = 0.125 * dot3(split(total), split(w_msg[...]))
        out[...] = own[:slots] + jnp.where(live, msg, 0.0)
        mask[...] = jnp.broadcast_to(jnp.where(live, 1.0, 0.0), mask.shape)

    return kernel


def end_messages(cells, cell, cells_all, nb, last):
    slots = cells * cell

    def kernel(neighbours, nbr_count, base, own, edge, w_msg, out):
        x = lax.axis_index(X)
        out[...] = base[...]
        for at, side in ((0, 0), (last, 2)):

            @pl.when(x == at)
            def _(side=side):
                mine = own[slots : slots + 8].T
                blocks = {side: edge[...]}
                total = gather(neighbours, nbr_count, mine, blocks, (side,), cells, cell, cells_all, nb)
                msg = 0.125 * dot3(split(total), split(w_msg[...]))
                out[...] = base[...] + jnp.where(live_rows(own, cells, cell), msg, 0.0)

    return kernel


def finish():
    def kernel(base, mask, a, b, c, w_one, w_two, out):
        spectral = a[...] + (b[...] + c[...])
        u = base[...] + spectral.T
        normed = u / jnp.sqrt(jnp.mean(u * u, axis=1, keepdims=True) + 1e-06)
        v = dot3(split(normed), split(w_one[...]))
        hidden = v / (1.0 + jnp.exp(-v))
        out[...] = (u + dot3(split(hidden), split(w_two[...]))) * mask[:, 0:1]

    return kernel


def shift(axis, by):
    size = lax.axis_size(axis)
    return [(i, (i + by) % size) for i in range(size)]


def shards(
    feats, positions, cell_counts, neighbours, nbr_count, kvec, filters, w_msg, w_val, w_one, w_two
):
    cells = cell_counts.shape[0]
    slots, width = feats.shape
    cell = slots // cells
    devices = lax.axis_size(ROWS_WAVES)
    nx = lax.axis_size(X)
    rows = lax.axis_size("rows")
    group = lax.axis_size((Z, Y))
    own_waves = kvec.shape[1] // rows
    waves = own_waves * group

    def floats(*dims):
        return jax.ShapeDtypeStruct(dims, F32)

    def halves(*dims):
        return jax.ShapeDtypeStruct(dims, BF16)

    payload = jnp.pad(feats, ((0, 8), (0, 0))) + jnp.pad(positions, ((slots, 5), (0, 0)))
    payload = payload + jnp.pad(kvec, ((slots + 4, 1), (0, width - kvec.shape[1])))
    payload = call(stamp(slots, cells), floats(*payload.shape), 2, alias={1: 0})(cell_counts, payload)
    near2 = lax.ppermute(payload, X, shift(X, 2))
    above = lax.ppermute(payload, X, shift(X, -1))
    below = lax.ppermute(payload, X, shift(X, 1))
    kv = call(pack(slots, own_waves, group), floats(group, 8, 128), 1)(payload)
    kv, again = lax.optimization_barrier((kv, payload))
    swap = shift("rows", 1)
    beside = lax.ppermute(again, "rows", swap)
    kv = lax.all_to_all(kv, (Z, Y), 0, 0, tiled=True)
    lhs = call(lattice(own_waves, group), halves(waves, 48), 1, [pltpu.VMEM((8, waves), F32)])(kv)

    unit = 12 * waves * slots * width

    def sums(chunks, first, *more):
        count = len(chunks)
        m = halves(count - 1 if first else count, 2 * waves, slots)
        return call(
            forward(cells, cell, count, own_waves, group, first),
            (floats(2 * waves, width), m, m),
            2 + count + len(more),
            flops=count * unit,
        )(lhs, w_val, *chunks, *more)

    m_own = call(own_trig(slots, own_waves, group), (halves(1, 2 * waves, slots),) * 2, 2, flops=unit)(lhs, payload)
    part, *m_beside = sums((payload, beside), True, *m_own)
    part, near2, above, below = lax.optimization_barrier((part, near2, above, below))
    line = (above, below, near2)
    other = [lax.ppermute(c, "rows", swap) for c in line]
    part, *m_line = sums(line, False, part)
    part, *m_other = sums(other, False, part)
    passed = call(line_end, floats(*payload.shape), 2)(below, above)
    part, passed = lax.optimization_barrier((part, passed))
    parts = lax.all_to_all(part.reshape(group, 2 * own_waves, width), (Z, Y), 0, 0, tiled=True)
    scale = 1.0 / math.sqrt(float(slots * devices) * float(waves * rows * nx))
    spread = call(filtered(scale), floats(*parts.shape), 2)(parts, filters)
    f = lax.all_to_all(spread, (Z, Y), 0, 0, tiled=True).reshape(2 * waves, width)

    one = floats(width, slots)

    def back(chunks, ft, m, *added, stacked=False):
        count = len(chunks)
        outs = floats(count, width, slots) if stacked else (one,) * count
        kernel = backward(chunks, stacked, bool(added))
        return call(kernel, outs, 6 + len(added), flops=count * unit)(*ft, *m, *added)

    theirs = *m_beside, *m_other
    mine = *m_own, *m_line
    outs = floats(1, width, slots), *(halves(width, 2 * waves),) * 2
    far, *ft = call(backward_first(2), outs, 3, flops=unit)(f, *m_other)
    there = lax.ppermute(far, "rows", swap)
    ft = lax.optimization_barrier((*ft, far))[:2]
    rest = back(((0, 0), (1, 0), (1, 1)), ft, theirs, stacked=True)
    (e3,) = back(((1, 2),), ft, mine, there)
    e3, passed, rest, *ft = lax.optimization_barrier((e3, passed, rest, *ft))
    rest = lax.ppermute(rest, "rows", swap)
    e3 = lax.ppermute(e3, X, shift(X, 2))
    ends = [(d, (d + nx) % devices) for d in range(devices) if d % nx == 0]
    ends += [(d, (d - nx) % devices) for d in range(devices) if d % nx == nx - 1]
    edge = lax.ppermute(passed, ROWS_WAVES, ends)
    e0, e1, e2 = back(((0, 0), (1, 0), (1, 1)), ft, mine, rest)
    e1 = lax.ppermute(e1, X, shift(X, 1))
    e2 = lax.ppermute(e2, X, shift(X, -1))

    sizes = cells, cell, cells * devices, neighbours.shape[1], nx - 1
    base, mask = call(messages(*sizes), (floats(slots, width), floats(slots, 128)), 6, smem=(0, 1))(
        neighbours, nbr_count, payload, below, above, w_msg
    )
    base = call(end_messages(*sizes), floats(slots, width), 6, smem=(0, 1))(
        neighbours, nbr_count, base, payload, edge, w_msg
    )
    (e0,) = call(pairs, (one,), 2)(e0, e3)
    return call(finish(), floats(slots, width), 7)(base, mask, e0, e1, e2, w_one, w_two)


def solution(mesh):
    torus = Mesh(mesh.devices.reshape(mesh.shape["rows"], 4, 4, 4), ROWS_WAVES)
    return jax.shard_map(
        shards,
        mesh=torus,
        in_specs=(
            P(ROWS_WAVES, None),
            P(None, ROWS_WAVES),
            P(ROWS_WAVES),
            P(ROWS_WAVES, None),
            P(ROWS_WAVES),
            P(None, WAVES),
            P(WAVES, None),
            P(),
            P(),
            P(),
            P(),
        ),
        out_specs=P(ROWS_WAVES, None),
        check_vma=False,
    )
```

```python
import math

import jax
import jax.numpy as jnp
from jax import lax
from jax.experimental import pallas as pl
from jax.experimental.pallas import tpu as pltpu
from jax.sharding import Mesh
from jax.sharding import PartitionSpec as P

Z, Y, X = "waves_0", "waves_1", "waves_2"
WAVES = (Z, Y, X)
ROWS_WAVES = ("rows", Z, Y, X)
F32 = jnp.float32
BF16 = jnp.bfloat16

SIN_POLY = (6.283185280154403, -10.33542015333633, 5.100154773052372, -1.1965808225334407, 0.15531182448662934)
COS_POLY = (0.999999953027512, -4.934792802489427, 4.058410790762133, -1.3318729727851486, 0.21968242357146)
ROUNDER = 12582912.0


def horner(coeffs, u):
    out = coeffs[-1]
    for c in coeffs[-2::-1]:
        out = out * u + c
    return out


def split(a):
    high = a.astype(BF16)
    return high, (a - high.astype(F32)).astype(BF16)


def thirds(a):
    high = a.astype(BF16).astype(F32)
    rest = a - high
    middle = rest.astype(BF16).astype(F32)
    return high, middle, rest - middle


def dot(a, b):
    return jnp.dot(a, b, preferred_element_type=F32)


def dot3(a, b):
    return dot(a[0], b[0]) + (dot(a[1], b[0]) + dot(a[0], b[1]))


def call(kernel, outs, n_in, scratch=(), smem=(), flops=0, alias={}, limit=8 << 20):
    def space(i):
        return pltpu.SMEM if i in smem else pltpu.VMEM

    return pl.pallas_call(
        kernel,
        out_shape=outs,
        in_specs=[pl.BlockSpec(memory_space=space(i)) for i in range(n_in)],
        out_specs=jax.tree.map(lambda _: pl.BlockSpec(memory_space=pltpu.VMEM), outs),
        scratch_shapes=scratch,
        input_output_aliases=alias,
        cost_estimate=pl.CostEstimate(flops=flops, bytes_accessed=1 << 16, transcendentals=0),
        compiler_params=pltpu.CompilerParams(vmem_limit_bytes=limit),
    )


def live_rows(block, cells, cell):
    slots = cells * cell
    row = lax.broadcasted_iota(jnp.int32, (slots, 1), 0).astype(F32)
    limit = block[slots + 3 : slots + 4, 0:1]
    for c in range(1, cells):
        limit = jnp.where(row < c * cell, limit, c * cell + block[slots + 3 : slots + 4, c : c + 1])
    return row < limit


def stamp(slots, cells):
    def kernel(counts, _, out):
        out[slots + 3 : slots + 4, 0:cells] = counts[...].astype(F32).reshape(1, cells)

    return kernel


def lattice(own, groups):
    def kernel(kv, out, flat):
        flat[...] = jnp.zeros(flat.shape, F32)
        pad = jnp.zeros((8, flat.shape[1] - 128), F32)
        for g in range(groups):
            flat[...] += pltpu.roll(jnp.concatenate([kv[g], pad], axis=1), g * own, 1)
        kh, km, kl = thirds(flat[...])
        out[...] = jnp.concatenate([kh, kh, km, kh, km, kl], axis=0).T.astype(BF16)

    return kernel


def pack(slots, own, groups):
    def kernel(own_block, out):
        rows = own_block[slots : slots + 8, :128] * (0.5 / math.pi)
        rows = pltpu.roll(rows, 4, 0)
        k = jnp.where(lax.axis_index("rows") == 0, rows, pltpu.roll(rows, 128 - own, 1))
        lane = lax.broadcasted_iota(jnp.int32, k.shape, 1)
        line = lax.broadcasted_iota(jnp.int32, k.shape, 0)
        k = jnp.where((lane < own) & (line < 3), k, 0.0)
        for g in range(groups):
            out[g] = k

    return kernel


def own_trig(slots, own, groups):
    def kernel(lhs, chunk, mh, ml):
        turns = dot(lhs[...], spots(chunk, slots))
        for g in range(groups):
            rows = slice(2 * own * g, 2 * own * (g + 1))
            mh[0, rows], ml[0, rows] = split(cos_and_sin(turns[g * own : (g + 1) * own]))

    return kernel


def spots(chunk, slots):
    x, y, z = thirds(jnp.where(lax.broadcasted_iota(jnp.int32, (8, slots), 0) < 3, chunk[slots : slots + 8], 0.0))
    return jnp.concatenate([x, y, x, z, y, x], axis=0).astype(BF16)


def cos_and_sin(t):
    f = t - ((t + ROUNDER) - ROUNDER)
    u = f * f
    s = f * horner(SIN_POLY, u)
    c = horner(COS_POLY, u)
    return jnp.concatenate([1.0 - 0.5 * (s * s), s * c], axis=0)


def forward(cells, cell, count, own, groups, first):
    slots = cells * cell

    def kernel(lhs, w_val, *refs):
        chunks, refs = refs[:count], refs[count:]
        if first:
            ready, refs = refs[:2], refs[2:]
        else:
            before, refs = refs[0], refs[1:]
        out, mh, ml = refs
        skip = 1 if first else 0
        w = split(w_val[...])
        turns, right = [], []
        for j, chunk in enumerate(chunks):
            live = live_rows(chunk, cells, cell)
            vh, vl = split(jnp.where(live, dot3(split(chunk[:slots]), w), 0.0))
            right += [vh, vh, vl]
            turns.append(dot(lhs[...], spots(chunk, slots)) if j >= skip else None)
        right = jnp.concatenate(right, axis=0)
        for part in range(2):
            for j in range(skip, count):
                for g in range(part * groups // 2, (part + 1) * groups // 2):
                    rows = slice(2 * own * g, 2 * own * (g + 1))
                    pieces = split(cos_and_sin(turns[j][g * own : (g + 1) * own]))
                    mh[j - skip, rows], ml[j - skip, rows] = pieces
            rows = slice(part * own * groups, (part + 1) * own * groups)
            pairs_of = [(ready[0][0, rows], ready[1][0, rows])] if first else []
            pairs_of += [(mh[j, rows], ml[j, rows]) for j in range(count - skip)]
            left = [m for high, low in pairs_of for m in (high, low, high)]
            total = dot(jnp.concatenate(left, axis=1), right)
            out[rows] = total if first else before[rows] + total

    return kernel


def filtered(scale):
    def kernel(parts, filters, out):
        groups, double, _ = parts.shape
        own = double // 2
        f = jnp.where(lax.axis_index("rows") == 0, filters[:own], filters[own:]) * scale
        total = parts[0]
        for g in range(1, groups):
            total = total + parts[g]
        total = total * jnp.concatenate([f, f], axis=0)
        for g in range(groups):
            out[g] = total

    return kernel


def line_end(below, above, out):
    out[...] = jnp.where(lax.axis_index(X) == 0, below[...], above[...])


def backward_first(at):
    def kernel(f, mh, ml, out, high, low):
        ft = split(f[...].T)
        high[...], low[...] = ft
        out[0] = dot3(ft, (mh[at], ml[at]))

    return kernel


def backward(chunks, stacked, adds):
    def kernel(fh, fl, mh0, ml0, mh1, ml1, *refs):
        added, outs = refs[0] if adds else None, refs[1:] if adds else refs
        for j, (rest, at) in enumerate(chunks):
            part = dot3((fh[...], fl[...]), (mh1[at], ml1[at]) if rest else (mh0[at], ml0[at]))
            part = part + added[j] if adds else part
            if stacked:
                outs[0][j] = part
            else:
                outs[j][...] = part

    return kernel


def pairs(*refs):
    count = len(refs) // 3
    for a, b, out in zip(refs[:count], refs[count : 2 * count], refs[2 * count :]):
        out[...] = a[...] + b[...]


def listed_factor(neighbours, nbr_count, c, target, nb):
    listed = jnp.float32(0.0)
    for b in range(nb):
        hit = (neighbours[c, b] == target) & (b < nbr_count[c])
        listed = listed + jnp.where(hit, jnp.float32(1.0), jnp.float32(0.0))
    return listed


def gather(neighbours, nbr_count, mine, blocks, use, cells, cell, cells_all, nb):
    slots = cells * cell
    first = lax.axis_index(ROWS_WAVES) * cells
    wide, pos = {}, {}
    for k in use:
        live = live_rows(blocks[k], cells, cell)
        halves = split(jnp.where(live, blocks[k][:slots], 0.0))
        for c in range(cells):
            wide[k * cells + c] = tuple(p[c * cell : (c + 1) * cell] for p in halves)
            pos[k * cells + c] = blocks[k][slots : slots + 3, c * cell : (c + 1) * cell]
    eye = lax.broadcasted_iota(jnp.int32, (cell, cell), 0) == lax.broadcasted_iota(jnp.int32, (cell, cell), 1)
    gathered = []
    for c in range(cells):
        here = mine[c * cell : (c + 1) * cell]
        acc = jnp.zeros((cell, blocks[use[0]].shape[1]), F32)
        for step in range(2 * cells + 1):
            other = c + step
            if other not in wide:
                continue
            target = lax.rem(first + other - cells + cells_all, cells_all)
            near = pos[other]
            d0 = here[:, 0:1] - near[0:1]
            d1 = here[:, 1:2] - near[1:2]
            d2 = here[:, 2:3] - near[2:3]
            weight = jnp.exp(-0.125 * (d0 * d0 + d1 * d1 + d2 * d2))
            weight = weight * listed_factor(neighbours, nbr_count, c, target, nb)
            if step == cells:
                weight = jnp.where(eye, 0.0, weight)
            acc = acc + dot3(split(weight), wide[other])
        gathered.append(acc)
    return jnp.concatenate(gathered, axis=0)


def messages(cells, cell, cells_all, nb, last):
    slots = cells * cell

    def kernel(neighbours, nbr_count, own, low, high, w_msg, w_one, w_two, out, mask, cols, *parts):
        x = lax.axis_index(X)
        lo = jnp.where(x == 0, 0.0, low[...])
        hi = jnp.where(x == last, 0.0, high[...])
        blocks = lo, own[...], hi
        mine = own[slots : slots + 8].T
        cols[...] = mine
        for k, w in enumerate((w_msg, w_one, w_two)):
            parts[2 * k][...], parts[2 * k + 1][...] = split(w[...])
        total = gather(neighbours, nbr_count, mine, blocks, (0, 1, 2), cells, cell, cells_all, nb)
        live = live_rows(own, cells, cell)
        msg = 0.125 * dot3(split(total), (parts[0][...], parts[1][...]))
        out[...] = own[:slots] + jnp.where(live, msg, 0.0)
        mask[...] = jnp.broadcast_to(jnp.where(live, 1.0, 0.0), mask.shape)

    return kernel


def end_messages(cells, cell, cells_all, nb, last):
    def kernel(neighbours, nbr_count, _, mask, cols, edge, wh, wl, out):
        x = lax.axis_index(X)
        for at, side in ((0, 0), (last, 2)):

            @pl.when(x == at)
            def _(side=side):
                blocks = {side: edge[...]}
                total = gather(neighbours, nbr_count, cols[...], blocks, (side,), cells, cell, cells_all, nb)
                msg = 0.125 * dot3(split(total), (wh[...], wl[...]))
                out[...] = out[...] + msg * mask[:, 0:1]

    return kernel


def finish():
    def kernel(base, mask, a, b, c, oh, ol, th, tl, out):
        spectral = a[...] + (b[...] + c[...])
        u = base[...] + spectral.T
        normed = u / jnp.sqrt(jnp.mean(u * u, axis=1, keepdims=True) + 1e-06)
        v = dot3(split(normed), (oh[...], ol[...]))
        hidden = v / (1.0 + jnp.exp(-v))
        out[...] = (u + dot3(split(hidden), (th[...], tl[...]))) * mask[:, 0:1]

    return kernel


def shift(axis, by):
    size = lax.axis_size(axis)
    return [(i, (i + by) % size) for i in range(size)]


def shards(
    feats, positions, cell_counts, neighbours, nbr_count, kvec, filters, w_msg, w_val, w_one, w_two
):
    cells = cell_counts.shape[0]
    slots, width = feats.shape
    cell = slots // cells
    devices = lax.axis_size(ROWS_WAVES)
    nx = lax.axis_size(X)
    rows = lax.axis_size("rows")
    group = lax.axis_size((Z, Y))
    own_waves = kvec.shape[1] // rows
    waves = own_waves * group

    def floats(*dims):
        return jax.ShapeDtypeStruct(dims, F32)

    def halves(*dims):
        return jax.ShapeDtypeStruct(dims, BF16)

    payload = jnp.pad(feats, ((0, 8), (0, 0))) + jnp.pad(positions, ((slots, 5), (0, 0)))
    payload = payload + jnp.pad(kvec, ((slots + 4, 1), (0, width - kvec.shape[1])))
    payload = call(stamp(slots, cells), floats(*payload.shape), 2, alias={1: 0})(cell_counts, payload)
    near2 = lax.ppermute(payload, X, shift(X, 2))
    above = lax.ppermute(payload, X, shift(X, -1))
    below = lax.ppermute(payload, X, shift(X, 1))
    kv = call(pack(slots, own_waves, group), floats(group, 8, 128), 1)(payload)
    kv, again = lax.optimization_barrier((kv, payload))
    swap = shift("rows", 1)
    beside = lax.ppermute(again, "rows", swap)
    kv = lax.all_to_all(kv, (Z, Y), 0, 0, tiled=True)
    lhs = call(lattice(own_waves, group), halves(waves, 48), 1, [pltpu.VMEM((8, waves), F32)])(kv)

    unit = 12 * waves * slots * width

    def sums(chunks, first, *more):
        count = len(chunks)
        m = halves(count - 1 if first else count, 2 * waves, slots)
        return call(
            forward(cells, cell, count, own_waves, group, first),
            (floats(2 * waves, width), m, m),
            2 + count + len(more),
            flops=count * unit,
        )(lhs, w_val, *chunks, *more)

    m_own = call(own_trig(slots, own_waves, group), (halves(1, 2 * waves, slots),) * 2, 2, flops=unit)(lhs, payload)
    part, *m_beside = sums((payload, beside), True, *m_own)
    part, near2, above, below = lax.optimization_barrier((part, near2, above, below))
    line = (above, below, near2)
    other = [lax.ppermute(c, "rows", swap) for c in line]
    part, *m_line = sums(line, False, part)
    part, *m_other = sums(other, False, part)
    passed = call(line_end, floats(*payload.shape), 2)(below, above)
    part, passed = lax.optimization_barrier((part, passed))
    parts = lax.all_to_all(part.reshape(group, 2 * own_waves, width), (Z, Y), 0, 0, tiled=True)
    scale = 1.0 / math.sqrt(float(slots * devices) * float(waves * rows * nx))
    spread = call(filtered(scale), floats(*parts.shape), 2)(parts, filters)
    f = lax.all_to_all(spread, (Z, Y), 0, 0, tiled=True).reshape(2 * waves, width)

    one = floats(width, slots)

    def back(chunks, ft, m, *added, stacked=False):
        count = len(chunks)
        outs = floats(count, width, slots) if stacked else (one,) * count
        kernel = backward(chunks, stacked, bool(added))
        return call(kernel, outs, 6 + len(added), flops=count * unit)(*ft, *m, *added)

    theirs = *m_beside, *m_other
    mine = *m_own, *m_line
    outs = floats(1, width, slots), *(halves(width, 2 * waves),) * 2
    far, *ft = call(backward_first(2), outs, 3, flops=unit)(f, *m_other)
    there = lax.ppermute(far, "rows", swap)
    ft = lax.optimization_barrier((*ft, far))[:2]
    rest = back(((0, 0), (1, 0), (1, 1)), ft, theirs, stacked=True)
    (e3,) = back(((1, 2),), ft, mine, there)
    e3, passed, rest, *ft = lax.optimization_barrier((e3, passed, rest, *ft))
    rest = lax.ppermute(rest, "rows", swap)
    e3 = lax.ppermute(e3, X, shift(X, 2))
    ends = [(d, (d + nx) % devices) for d in range(devices) if d % nx == 0]
    ends += [(d, (d - nx) % devices) for d in range(devices) if d % nx == nx - 1]
    edge = lax.ppermute(passed, ROWS_WAVES, ends)
    e0, e1, e2 = back(((0, 0), (1, 0), (1, 1)), ft, mine, rest)
    e1 = lax.ppermute(e1, X, shift(X, 1))
    e2 = lax.ppermute(e2, X, shift(X, -1))

    sizes = cells, cell, cells * devices, neighbours.shape[1], nx - 1
    sizes = cells, cell, cells * devices, neighbours.shape[1], nx - 1
    outs = floats(slots, width), floats(slots, 128), floats(slots, 8), *(halves(width, width),) * 6
    base, mask, cols, *w = call(messages(*sizes), outs, 8, smem=(0, 1))(
        neighbours, nbr_count, payload, below, above, w_msg, w_one, w_two
    )
    base = call(end_messages(*sizes), floats(slots, width), 8, smem=(0, 1), alias={2: 0})(
        neighbours, nbr_count, base, mask, cols, edge, *w[:2]
    )
    (e0,) = call(pairs, (one,), 2)(e0, e3)
    return call(finish(), floats(slots, width), 9)(base, mask, e0, e1, e2, *w[2:])


def solution(mesh):
    torus = Mesh(mesh.devices.reshape(mesh.shape["rows"], 4, 4, 4), ROWS_WAVES)
    return jax.shard_map(
        shards,
        mesh=torus,
        in_specs=(
            P(ROWS_WAVES, None),
            P(None, ROWS_WAVES),
            P(ROWS_WAVES),
            P(ROWS_WAVES, None),
            P(ROWS_WAVES),
            P(None, WAVES),
            P(WAVES, None),
            P(),
            P(),
            P(),
            P(),
        ),
        out_specs=P(ROWS_WAVES, None),
        check_vma=False,
    )
```

```python
import math

import jax
import jax.numpy as jnp
from jax import lax
from jax.experimental import pallas as pl
from jax.experimental.pallas import tpu as pltpu
from jax.sharding import Mesh
from jax.sharding import PartitionSpec as P

Z, Y, X = "waves_0", "waves_1", "waves_2"
WAVES = (Z, Y, X)
ROWS_WAVES = ("rows", Z, Y, X)
F32 = jnp.float32
BF16 = jnp.bfloat16

SIN_POLY = (6.283185280154403, -10.33542015333633, 5.100154773052372, -1.1965808225334407, 0.15531182448662934)
COS_POLY = (0.999999953027512, -4.934792802489427, 4.058410790762133, -1.3318729727851486, 0.21968242357146)
ROUNDER = 12582912.0


def horner(coeffs, u):
    out = coeffs[-1]
    for c in coeffs[-2::-1]:
        out = out * u + c
    return out


def split(a):
    high = a.astype(BF16)
    return high, (a - high.astype(F32)).astype(BF16)


def thirds(a):
    high = a.astype(BF16).astype(F32)
    rest = a - high
    middle = rest.astype(BF16).astype(F32)
    return high, middle, rest - middle


def dot(a, b):
    return jnp.dot(a, b, preferred_element_type=F32)


def dot3(a, b):
    return dot(a[0], b[0]) + (dot(a[1], b[0]) + dot(a[0], b[1]))


def call(kernel, outs, n_in, scratch=(), smem=(), flops=0, alias={}, limit=8 << 20):
    def space(i):
        return pltpu.SMEM if i in smem else pltpu.VMEM

    return pl.pallas_call(
        kernel,
        out_shape=outs,
        in_specs=[pl.BlockSpec(memory_space=space(i)) for i in range(n_in)],
        out_specs=jax.tree.map(lambda _: pl.BlockSpec(memory_space=pltpu.VMEM), outs),
        scratch_shapes=scratch,
        input_output_aliases=alias,
        cost_estimate=pl.CostEstimate(flops=flops, bytes_accessed=1 << 16, transcendentals=0),
        compiler_params=pltpu.CompilerParams(vmem_limit_bytes=limit),
    )


def live_rows(block, cells, cell):
    slots = cells * cell
    row = lax.broadcasted_iota(jnp.int32, (slots, 1), 0).astype(F32)
    limit = block[slots + 3 : slots + 4, 0:1]
    for c in range(1, cells):
        limit = jnp.where(row < c * cell, limit, c * cell + block[slots + 3 : slots + 4, c : c + 1])
    return row < limit


def stamp(slots, cells):
    def kernel(counts, _, out):
        out[slots + 3 : slots + 4, 0:cells] = counts[...].astype(F32).reshape(1, cells)

    return kernel


def lattice(own, groups):
    def kernel(kv, out, flat):
        flat[...] = jnp.zeros(flat.shape, F32)
        pad = jnp.zeros((8, flat.shape[1] - 128), F32)
        for g in range(groups):
            flat[...] += pltpu.roll(jnp.concatenate([kv[g], pad], axis=1), g * own, 1)
        kh, km, kl = thirds(flat[...])
        out[...] = jnp.concatenate([kh, kh, km, kh, km, kl], axis=0).T.astype(BF16)

    return kernel


def pack(slots, own, groups):
    def kernel(own_block, out):
        rows = own_block[slots : slots + 8, :128] * (0.5 / math.pi)
        rows = pltpu.roll(rows, 4, 0)
        k = jnp.where(lax.axis_index("rows") == 0, rows, pltpu.roll(rows, 128 - own, 1))
        lane = lax.broadcasted_iota(jnp.int32, k.shape, 1)
        line = lax.broadcasted_iota(jnp.int32, k.shape, 0)
        k = jnp.where((lane < own) & (line < 3), k, 0.0)
        for g in range(groups):
            out[g] = k

    return kernel


def own_trig(slots, own, groups):
    def kernel(lhs, chunk, mh, ml):
        turns = dot(lhs[...], spots(chunk, slots))
        for g in range(groups):
            rows = slice(2 * own * g, 2 * own * (g + 1))
            mh[0, rows], ml[0, rows] = split(cos_and_sin(turns[g * own : (g + 1) * own]))

    return kernel


def spots(chunk, slots):
    x, y, z = thirds(jnp.where(lax.broadcasted_iota(jnp.int32, (8, slots), 0) < 3, chunk[slots : slots + 8], 0.0))
    return jnp.concatenate([x, y, x, z, y, x], axis=0).astype(BF16)


def cos_and_sin(t):
    f = t - ((t + ROUNDER) - ROUNDER)
    u = f * f
    s = f * horner(SIN_POLY, u)
    c = horner(COS_POLY, u)
    return jnp.concatenate([1.0 - 0.5 * (s * s), s * c], axis=0)


def forward(cells, cell, count, own, groups, first):
    slots = cells * cell

    def kernel(lhs, w_val, *refs):
        chunks, refs = refs[:count], refs[count:]
        if first:
            ready, refs = refs[:2], refs[2:]
        else:
            before, refs = refs[0], refs[1:]
        out, mh, ml = refs
        skip = 1 if first else 0
        w = split(w_val[...])
        turns, right = [], []
        for j, chunk in enumerate(chunks):
            live = live_rows(chunk, cells, cell)
            vh, vl = split(jnp.where(live, dot3(split(chunk[:slots]), w), 0.0))
            right += [vh, vh, vl]
            turns.append(dot(lhs[...], spots(chunk, slots)) if j >= skip else None)
        right = jnp.concatenate(right, axis=0)
        for part in range(2):
            for j in range(skip, count):
                for g in range(part * groups // 2, (part + 1) * groups // 2):
                    rows = slice(2 * own * g, 2 * own * (g + 1))
                    pieces = split(cos_and_sin(turns[j][g * own : (g + 1) * own]))
                    mh[j - skip, rows], ml[j - skip, rows] = pieces
            rows = slice(part * own * groups, (part + 1) * own * groups)
            pairs_of = [(ready[0][0, rows], ready[1][0, rows])] if first else []
            pairs_of += [(mh[j, rows], ml[j, rows]) for j in range(count - skip)]
            left = [m for high, low in pairs_of for m in (high, low, high)]
            total = dot(jnp.concatenate(left, axis=1), right)
            out[rows] = total if first else before[rows] + total

    return kernel


def filtered(scale):
    def kernel(parts, filters, out):
        groups, double, _ = parts.shape
        own = double // 2
        f = jnp.where(lax.axis_index("rows") == 0, filters[:own], filters[own:]) * scale
        total = parts[0]
        for g in range(1, groups):
            total = total + parts[g]
        total = total * jnp.concatenate([f, f], axis=0)
        for g in range(groups):
            out[g] = total

    return kernel


def line_end(below, above, out):
    out[...] = jnp.where(lax.axis_index(X) == 0, below[...], above[...])


def backward_first(at):
    def kernel(f, mh, ml, out, high, low):
        ft = split(f[...].T)
        high[...], low[...] = ft
        out[0] = dot3(ft, (mh[at], ml[at]))

    return kernel


def backward(chunks, stacked, adds):
    def kernel(fh, fl, mh0, ml0, mh1, ml1, *refs):
        added, outs = refs[0] if adds else None, refs[1:] if adds else refs
        for j, (rest, at) in enumerate(chunks):
            part = dot3((fh[...], fl[...]), (mh1[at], ml1[at]) if rest else (mh0[at], ml0[at]))
            part = part + added[j] if adds else part
            if stacked:
                outs[0][j] = part
            else:
                outs[j][...] = part

    return kernel


def pairs(*refs):
    count = len(refs) // 3
    for a, b, out in zip(refs[:count], refs[count : 2 * count], refs[2 * count :]):
        out[...] = a[...] + b[...]


def listed_factor(neighbours, nbr_count, c, target, nb):
    listed = jnp.float32(0.0)
    for b in range(nb):
        hit = (neighbours[c, b] == target) & (b < nbr_count[c])
        listed = listed + jnp.where(hit, jnp.float32(1.0), jnp.float32(0.0))
    return listed


def gather(factor, mine, blocks, use, cells, cell):
    slots = cells * cell
    wide, pos = {}, {}
    for k in use:
        live = live_rows(blocks[k], cells, cell)
        halves = split(jnp.where(live, blocks[k][:slots], 0.0))
        for c in range(cells):
            wide[k * cells + c] = tuple(p[c * cell : (c + 1) * cell] for p in halves)
            pos[k * cells + c] = blocks[k][slots : slots + 3, c * cell : (c + 1) * cell]
    eye = lax.broadcasted_iota(jnp.int32, (cell, cell), 0) == lax.broadcasted_iota(jnp.int32, (cell, cell), 1)
    gathered = []
    for c in range(cells):
        here = mine[c * cell : (c + 1) * cell]
        acc = jnp.zeros((cell, blocks[use[0]].shape[1]), F32)
        for step in range(2 * cells + 1):
            other = c + step
            if other not in wide:
                continue
            near = pos[other]
            d0 = here[:, 0:1] - near[0:1]
            d1 = here[:, 1:2] - near[1:2]
            d2 = here[:, 2:3] - near[2:3]
            weight = jnp.exp(-0.125 * (d0 * d0 + d1 * d1 + d2 * d2))
            weight = weight * factor(c, other)
            if step == cells:
                weight = jnp.where(eye, 0.0, weight)
            acc = acc + dot3(split(weight), wide[other])
        gathered.append(acc)
    return jnp.concatenate(gathered, axis=0)


def messages(cells, cell, cells_all, nb, last):
    slots = cells * cell

    def kernel(neighbours, nbr_count, own, low, high, w_msg, w_one, w_two, out, mask, cols, factors, *parts):
        x = lax.axis_index(X)
        lo = jnp.where(x == 0, 0.0, low[...])
        hi = jnp.where(x == last, 0.0, high[...])
        blocks = lo, own[...], hi
        mine = own[slots : slots + 8].T
        cols[...] = mine
        for k, w in enumerate((w_msg, w_one, w_two)):
            parts[2 * k][...], parts[2 * k + 1][...] = split(w[...])
        first = lax.axis_index(ROWS_WAVES) * cells

        def factor(c, other):
            target = lax.rem(first + other - cells + cells_all, cells_all)
            listed = listed_factor(neighbours, nbr_count, c, target, nb)
            row = 3 * cells * c + other
            factors[row : row + 1] = jnp.full((1, 128), listed)
            return listed

        total = gather(factor, mine, blocks, (0, 1, 2), cells, cell)
        live = live_rows(own, cells, cell)
        msg = 0.125 * dot3(split(total), (parts[0][...], parts[1][...]))
        out[...] = own[:slots] + jnp.where(live, msg, 0.0)
        mask[...] = jnp.broadcast_to(jnp.where(live, 1.0, 0.0), mask.shape)

    return kernel


def end_messages(cells, cell, last):
    def kernel(_, mask, cols, factors, edge, wh, wl, out):
        x = lax.axis_index(X)
        for at, side in ((0, 0), (last, 2)):

            @pl.when(x == at)
            def _(side=side):
                blocks = {side: edge[...]}

                def factor(c, other):
                    row = 3 * cells * c + other
                    return factors[row : row + 1, 0:1]

                total = gather(factor, cols[...], blocks, (side,), cells, cell)
                msg = 0.125 * dot3(split(total), (wh[...], wl[...]))
                out[...] = out[...] + msg * mask[:, 0:1]

    return kernel


def finish():
    def kernel(base, mask, a, b, c, oh, ol, th, tl, out):
        spectral = a[...] + (b[...] + c[...])
        u = base[...] + spectral.T
        normed = u / jnp.sqrt(jnp.mean(u * u, axis=1, keepdims=True) + 1e-06)
        v = dot3(split(normed), (oh[...], ol[...]))
        hidden = v / (1.0 + jnp.exp(-v))
        out[...] = (u + dot3(split(hidden), (th[...], tl[...]))) * mask[:, 0:1]

    return kernel


def shift(axis, by):
    size = lax.axis_size(axis)
    return [(i, (i + by) % size) for i in range(size)]


def shards(
    feats, positions, cell_counts, neighbours, nbr_count, kvec, filters, w_msg, w_val, w_one, w_two
):
    cells = cell_counts.shape[0]
    slots, width = feats.shape
    cell = slots // cells
    devices = lax.axis_size(ROWS_WAVES)
    nx = lax.axis_size(X)
    rows = lax.axis_size("rows")
    group = lax.axis_size((Z, Y))
    own_waves = kvec.shape[1] // rows
    waves = own_waves * group

    def floats(*dims):
        return jax.ShapeDtypeStruct(dims, F32)

    def halves(*dims):
        return jax.ShapeDtypeStruct(dims, BF16)

    payload = jnp.pad(feats, ((0, 8), (0, 0))) + jnp.pad(positions, ((slots, 5), (0, 0)))
    payload = payload + jnp.pad(kvec, ((slots + 4, 1), (0, width - kvec.shape[1])))
    payload = call(stamp(slots, cells), floats(*payload.shape), 2, alias={1: 0})(cell_counts, payload)
    near2 = lax.ppermute(payload, X, shift(X, 2))
    above = lax.ppermute(payload, X, shift(X, -1))
    below = lax.ppermute(payload, X, shift(X, 1))
    kv = call(pack(slots, own_waves, group), floats(group, 8, 128), 1)(payload)
    kv, again = lax.optimization_barrier((kv, payload))
    swap = shift("rows", 1)
    beside = lax.ppermute(again, "rows", swap)
    kv = lax.all_to_all(kv, (Z, Y), 0, 0, tiled=True)
    lhs = call(lattice(own_waves, group), halves(waves, 48), 1, [pltpu.VMEM((8, waves), F32)])(kv)

    unit = 12 * waves * slots * width

    def sums(chunks, first, *more):
        count = len(chunks)
        m = halves(count - 1 if first else count, 2 * waves, slots)
        return call(
            forward(cells, cell, count, own_waves, group, first),
            (floats(2 * waves, width), m, m),
            2 + count + len(more),
            flops=count * unit,
        )(lhs, w_val, *chunks, *more)

    m_own = call(own_trig(slots, own_waves, group), (halves(1, 2 * waves, slots),) * 2, 2, flops=unit)(lhs, payload)
    part, *m_beside = sums((payload, beside), True, *m_own)
    part, near2, above, below = lax.optimization_barrier((part, near2, above, below))
    line = (above, below, near2)
    other = [lax.ppermute(c, "rows", swap) for c in line]
    part, *m_line = sums(line, False, part)
    part, *m_other = sums(other, False, part)
    passed = call(line_end, floats(*payload.shape), 2)(below, above)
    part, passed = lax.optimization_barrier((part, passed))
    parts = lax.all_to_all(part.reshape(group, 2 * own_waves, width), (Z, Y), 0, 0, tiled=True)
    scale = 1.0 / math.sqrt(float(slots * devices) * float(waves * rows * nx))
    spread = call(filtered(scale), floats(*parts.shape), 2)(parts, filters)
    f = lax.all_to_all(spread, (Z, Y), 0, 0, tiled=True).reshape(2 * waves, width)

    one = floats(width, slots)

    def back(chunks, ft, m, *added, stacked=False):
        count = len(chunks)
        outs = floats(count, width, slots) if stacked else (one,) * count
        kernel = backward(chunks, stacked, bool(added))
        return call(kernel, outs, 6 + len(added), flops=count * unit)(*ft, *m, *added)

    theirs = *m_beside, *m_other
    mine = *m_own, *m_line
    outs = floats(1, width, slots), *(halves(width, 2 * waves),) * 2
    far, *ft = call(backward_first(2), outs, 3, flops=unit)(f, *m_other)
    there = lax.ppermute(far, "rows", swap)
    ft = lax.optimization_barrier((*ft, far))[:2]
    rest = back(((0, 0), (1, 0), (1, 1)), ft, theirs, stacked=True)
    (e3,) = back(((1, 2),), ft, mine, there)
    e3, passed, rest, *ft = lax.optimization_barrier((e3, passed, rest, *ft))
    rest = lax.ppermute(rest, "rows", swap)
    e3 = lax.ppermute(e3, X, shift(X, 2))
    ends = [(d, (d + nx) % devices) for d in range(devices) if d % nx == 0]
    ends += [(d, (d - nx) % devices) for d in range(devices) if d % nx == nx - 1]
    edge = lax.ppermute(passed, ROWS_WAVES, ends)
    e0, e1, e2 = back(((0, 0), (1, 0), (1, 1)), ft, mine, rest)
    e1 = lax.ppermute(e1, X, shift(X, 1))
    e2 = lax.ppermute(e2, X, shift(X, -1))

    sizes = cells, cell, cells * devices, neighbours.shape[1], nx - 1
    sizes = cells, cell, cells * devices, neighbours.shape[1], nx - 1
    small = floats(slots, 128), floats(slots, 8), floats(16, 128)
    outs = floats(slots, width), *small, *(halves(width, width),) * 6
    base, mask, cols, factors, w0, w1, *w = call(messages(*sizes), outs, 8, smem=(0, 1))(
        neighbours, nbr_count, payload, below, above, w_msg, w_one, w_two
    )
    base = call(end_messages(cells, cell, nx - 1), floats(slots, width), 7, alias={0: 0})(
        base, mask, cols, factors, edge, w0, w1
    )
    (e0,) = call(pairs, (one,), 2)(e0, e3)
    return call(finish(), floats(slots, width), 9)(base, mask, e0, e1, e2, *w)


def solution(mesh):
    torus = Mesh(mesh.devices.reshape(mesh.shape["rows"], 4, 4, 4), ROWS_WAVES)
    return jax.shard_map(
        shards,
        mesh=torus,
        in_specs=(
            P(ROWS_WAVES, None),
            P(None, ROWS_WAVES),
            P(ROWS_WAVES),
            P(ROWS_WAVES, None),
            P(ROWS_WAVES),
            P(None, WAVES),
            P(WAVES, None),
            P(),
            P(),
            P(),
            P(),
        ),
        out_specs=P(ROWS_WAVES, None),
        check_vma=False,
    )
```

```python
import math

import jax
import jax.numpy as jnp
from jax import lax
from jax.experimental import pallas as pl
from jax.experimental.pallas import tpu as pltpu
from jax.sharding import Mesh
from jax.sharding import PartitionSpec as P

Z, Y, X = "waves_0", "waves_1", "waves_2"
WAVES = (Z, Y, X)
ROWS_WAVES = ("rows", Z, Y, X)
F32 = jnp.float32
BF16 = jnp.bfloat16

SIN_POLY = (6.283185280154403, -10.33542015333633, 5.100154773052372, -1.1965808225334407, 0.15531182448662934)
COS_POLY = (0.999999953027512, -4.934792802489427, 4.058410790762133, -1.3318729727851486, 0.21968242357146)
ROUNDER = 12582912.0


def horner(coeffs, u):
    out = coeffs[-1]
    for c in coeffs[-2::-1]:
        out = out * u + c
    return out


def split(a):
    high = a.astype(BF16)
    return high, (a - high.astype(F32)).astype(BF16)


def thirds(a):
    high = a.astype(BF16).astype(F32)
    rest = a - high
    middle = rest.astype(BF16).astype(F32)
    return high, middle, rest - middle


def dot(a, b):
    return jnp.dot(a, b, preferred_element_type=F32)


def dot3(a, b):
    return dot(a[0], b[0]) + (dot(a[1], b[0]) + dot(a[0], b[1]))


def call(kernel, outs, n_in, scratch=(), smem=(), flops=0, alias={}, limit=8 << 20):
    def space(i):
        return pltpu.SMEM if i in smem else pltpu.VMEM

    return pl.pallas_call(
        kernel,
        out_shape=outs,
        in_specs=[pl.BlockSpec(memory_space=space(i)) for i in range(n_in)],
        out_specs=jax.tree.map(lambda _: pl.BlockSpec(memory_space=pltpu.VMEM), outs),
        scratch_shapes=scratch,
        input_output_aliases=alias,
        cost_estimate=pl.CostEstimate(flops=flops, bytes_accessed=1 << 16, transcendentals=0),
        compiler_params=pltpu.CompilerParams(vmem_limit_bytes=limit),
    )


def live_rows(block, cells, cell):
    slots = cells * cell
    row = lax.broadcasted_iota(jnp.int32, (slots, 1), 0).astype(F32)
    limit = block[slots + 3 : slots + 4, 0:1]
    for c in range(1, cells):
        limit = jnp.where(row < c * cell, limit, c * cell + block[slots + 3 : slots + 4, c : c + 1])
    return row < limit


def stamp(slots, cells):
    def kernel(counts, _, out):
        out[slots + 3 : slots + 4, 0:cells] = counts[...].astype(F32).reshape(1, cells)

    return kernel


def lattice(own, groups):
    def kernel(kv, out, flat):
        flat[...] = jnp.zeros(flat.shape, F32)
        pad = jnp.zeros((8, flat.shape[1] - 128), F32)
        for g in range(groups):
            flat[...] += pltpu.roll(jnp.concatenate([kv[g], pad], axis=1), g * own, 1)
        kh, km, kl = thirds(flat[...])
        out[...] = jnp.concatenate([kh, kh, km, kh, km, kl], axis=0).T.astype(BF16)

    return kernel


def pack(slots, own, groups):
    def kernel(own_block, out):
        rows = own_block[slots : slots + 8, :128] * (0.5 / math.pi)
        rows = pltpu.roll(rows, 4, 0)
        k = jnp.where(lax.axis_index("rows") == 0, rows, pltpu.roll(rows, 128 - own, 1))
        lane = lax.broadcasted_iota(jnp.int32, k.shape, 1)
        line = lax.broadcasted_iota(jnp.int32, k.shape, 0)
        k = jnp.where((lane < own) & (line < 3), k, 0.0)
        for g in range(groups):
            out[g] = k

    return kernel


def own_trig(slots, own, groups):
    def kernel(lhs, chunk, mh, ml):
        turns = dot(lhs[...], spots(chunk, slots))
        for g in range(groups):
            rows = slice(2 * own * g, 2 * own * (g + 1))
            mh[0, rows], ml[0, rows] = split(cos_and_sin(turns[g * own : (g + 1) * own]))

    return kernel


def spots(chunk, slots):
    x, y, z = thirds(jnp.where(lax.broadcasted_iota(jnp.int32, (8, slots), 0) < 3, chunk[slots : slots + 8], 0.0))
    return jnp.concatenate([x, y, x, z, y, x], axis=0).astype(BF16)


def cos_and_sin(t):
    f = t - ((t + ROUNDER) - ROUNDER)
    u = f * f
    s = f * horner(SIN_POLY, u)
    c = horner(COS_POLY, u)
    return jnp.concatenate([1.0 - 0.5 * (s * s), s * c], axis=0)


def forward(cells, cell, count, own, groups, first):
    slots = cells * cell

    def kernel(lhs, w_val, *refs):
        chunks, refs = refs[:count], refs[count:]
        if first:
            ready, refs = refs[:2], refs[2:]
        else:
            before, refs = refs[0], refs[1:]
        out, mh, ml = refs
        skip = 1 if first else 0
        w = split(w_val[...])
        turns, right = [], []
        for j, chunk in enumerate(chunks):
            live = live_rows(chunk, cells, cell)
            vh, vl = split(jnp.where(live, dot3(split(chunk[:slots]), w), 0.0))
            right += [vh, vh, vl]
            turns.append(dot(lhs[...], spots(chunk, slots)) if j >= skip else None)
        right = jnp.concatenate(right, axis=0)
        for begin, stop in ((0, 10), (10, groups)):
            for j in range(skip, count):
                for g in range(begin, stop):
                    rows = slice(2 * own * g, 2 * own * (g + 1))
                    pieces = split(cos_and_sin(turns[j][g * own : (g + 1) * own]))
                    mh[j - skip, rows], ml[j - skip, rows] = pieces
            rows = slice(2 * own * begin, 2 * own * stop)
            pairs_of = [(ready[0][0, rows], ready[1][0, rows])] if first else []
            pairs_of += [(mh[j, rows], ml[j, rows]) for j in range(count - skip)]
            left = [m for high, low in pairs_of for m in (high, low, high)]
            total = dot(jnp.concatenate(left, axis=1), right)
            out[rows] = total if first else before[rows] + total

    return kernel


def filtered(scale):
    def kernel(parts, filters, out):
        groups, double, _ = parts.shape
        own = double // 2
        f = jnp.where(lax.axis_index("rows") == 0, filters[:own], filters[own:]) * scale
        total = parts[0]
        for g in range(1, groups):
            total = total + parts[g]
        total = total * jnp.concatenate([f, f], axis=0)
        for g in range(groups):
            out[g] = total

    return kernel


def line_end(below, above, out):
    out[...] = jnp.where(lax.axis_index(X) == 0, below[...], above[...])


def backward_first(at):
    def kernel(f, mh, ml, out, high, low):
        ft = split(f[...].T)
        high[...], low[...] = ft
        out[0] = dot3(ft, (mh[at], ml[at]))

    return kernel


def backward(chunks, stacked, adds):
    def kernel(fh, fl, mh0, ml0, mh1, ml1, *refs):
        added, outs = refs[0] if adds else None, refs[1:] if adds else refs
        for j, (rest, at) in enumerate(chunks):
            part = dot3((fh[...], fl[...]), (mh1[at], ml1[at]) if rest else (mh0[at], ml0[at]))
            part = part + added[j] if adds else part
            if stacked:
                outs[0][j] = part
            else:
                outs[j][...] = part

    return kernel


def pairs(*refs):
    count = len(refs) // 3
    for a, b, out in zip(refs[:count], refs[count : 2 * count], refs[2 * count :]):
        out[...] = a[...] + b[...]


def listed_factor(neighbours, nbr_count, c, target, nb):
    listed = jnp.float32(0.0)
    for b in range(nb):
        hit = (neighbours[c, b] == target) & (b < nbr_count[c])
        listed = listed + jnp.where(hit, jnp.float32(1.0), jnp.float32(0.0))
    return listed


def gather(factor, mine, blocks, use, cells, cell):
    slots = cells * cell
    wide, pos = {}, {}
    for k in use:
        live = live_rows(blocks[k], cells, cell)
        halves = split(jnp.where(live, blocks[k][:slots], 0.0))
        for c in range(cells):
            wide[k * cells + c] = tuple(p[c * cell : (c + 1) * cell] for p in halves)
            pos[k * cells + c] = blocks[k][slots : slots + 3, c * cell : (c + 1) * cell]
    eye = lax.broadcasted_iota(jnp.int32, (cell, cell), 0) == lax.broadcasted_iota(jnp.int32, (cell, cell), 1)
    gathered = []
    for c in range(cells):
        here = mine[c * cell : (c + 1) * cell]
        acc = jnp.zeros((cell, blocks[use[0]].shape[1]), F32)
        for step in range(2 * cells + 1):
            other = c + step
            if other not in wide:
                continue
            near = pos[other]
            d0 = here[:, 0:1] - near[0:1]
            d1 = here[:, 1:2] - near[1:2]
            d2 = here[:, 2:3] - near[2:3]
            weight = jnp.exp(-0.125 * (d0 * d0 + d1 * d1 + d2 * d2))
            weight = weight * factor(c, other)
            if step == cells:
                weight = jnp.where(eye, 0.0, weight)
            acc = acc + dot3(split(weight), wide[other])
        gathered.append(acc)
    return jnp.concatenate(gathered, axis=0)


def messages(cells, cell, cells_all, nb, last):
    slots = cells * cell

    def kernel(neighbours, nbr_count, own, low, high, w_msg, w_one, w_two, out, mask, cols, factors, *parts):
        x = lax.axis_index(X)
        lo = jnp.where(x == 0, 0.0, low[...])
        hi = jnp.where(x == last, 0.0, high[...])
        blocks = lo, own[...], hi
        mine = own[slots : slots + 8].T
        cols[...] = mine
        for k, w in enumerate((w_msg, w_one, w_two)):
            parts[2 * k][...], parts[2 * k + 1][...] = split(w[...])
        first = lax.axis_index(ROWS_WAVES) * cells

        def factor(c, other):
            target = lax.rem(first + other - cells + cells_all, cells_all)
            listed = listed_factor(neighbours, nbr_count, c, target, nb)
            row = 3 * cells * c + other
            factors[row : row + 1] = jnp.full((1, 128), listed)
            return listed

        total = gather(factor, mine, blocks, (0, 1, 2), cells, cell)
        live = live_rows(own, cells, cell)
        msg = 0.125 * dot3(split(total), (parts[0][...], parts[1][...]))
        out[...] = own[:slots] + jnp.where(live, msg, 0.0)
        mask[...] = jnp.broadcast_to(jnp.where(live, 1.0, 0.0), mask.shape)

    return kernel


def end_messages(cells, cell, last):
    def kernel(_, mask, cols, factors, edge, wh, wl, out):
        x = lax.axis_index(X)
        for at, side in ((0, 0), (last, 2)):

            @pl.when(x == at)
            def _(side=side):
                blocks = {side: edge[...]}

                def factor(c, other):
                    row = 3 * cells * c + other
                    return factors[row : row + 1, 0:1]

                total = gather(factor, cols[...], blocks, (side,), cells, cell)
                msg = 0.125 * dot3(split(total), (wh[...], wl[...]))
                out[...] = out[...] + msg * mask[:, 0:1]

    return kernel


def finish():
    def kernel(base, mask, a, b, c, oh, ol, th, tl, out):
        spectral = a[...] + (b[...] + c[...])
        u = base[...] + spectral.T
        normed = u / jnp.sqrt(jnp.mean(u * u, axis=1, keepdims=True) + 1e-06)
        v = dot3(split(normed), (oh[...], ol[...]))
        hidden = v / (1.0 + jnp.exp(-v))
        out[...] = (u + dot3(split(hidden), (th[...], tl[...]))) * mask[:, 0:1]

    return kernel


def shift(axis, by):
    size = lax.axis_size(axis)
    return [(i, (i + by) % size) for i in range(size)]


def shards(
    feats, positions, cell_counts, neighbours, nbr_count, kvec, filters, w_msg, w_val, w_one, w_two
):
    cells = cell_counts.shape[0]
    slots, width = feats.shape
    cell = slots // cells
    devices = lax.axis_size(ROWS_WAVES)
    nx = lax.axis_size(X)
    rows = lax.axis_size("rows")
    group = lax.axis_size((Z, Y))
    own_waves = kvec.shape[1] // rows
    waves = own_waves * group

    def floats(*dims):
        return jax.ShapeDtypeStruct(dims, F32)

    def halves(*dims):
        return jax.ShapeDtypeStruct(dims, BF16)

    payload = jnp.pad(feats, ((0, 8), (0, 0))) + jnp.pad(positions, ((slots, 5), (0, 0)))
    payload = payload + jnp.pad(kvec, ((slots + 4, 1), (0, width - kvec.shape[1])))
    kv = call(pack(slots, own_waves, group), floats(group, 8, 128), 1)(payload)
    kv, payload = lax.optimization_barrier((kv, payload))
    payload = call(stamp(slots, cells), floats(*payload.shape), 2, alias={1: 0})(cell_counts, payload)
    near2 = lax.ppermute(payload, X, shift(X, 2))
    above = lax.ppermute(payload, X, shift(X, -1))
    below = lax.ppermute(payload, X, shift(X, 1))
    kv, again = lax.optimization_barrier((kv, payload))
    swap = shift("rows", 1)
    beside = lax.ppermute(again, "rows", swap)
    kv = lax.all_to_all(kv, (Z, Y), 0, 0, tiled=True)
    lhs = call(lattice(own_waves, group), halves(waves, 48), 1, [pltpu.VMEM((8, waves), F32)])(kv)

    unit = 12 * waves * slots * width

    def sums(chunks, first, *more):
        count = len(chunks)
        m = halves(count - 1 if first else count, 2 * waves, slots)
        return call(
            forward(cells, cell, count, own_waves, group, first),
            (floats(2 * waves, width), m, m),
            2 + count + len(more),
            flops=count * unit,
        )(lhs, w_val, *chunks, *more)

    m_own = call(own_trig(slots, own_waves, group), (halves(1, 2 * waves, slots),) * 2, 2, flops=unit)(lhs, payload)
    part, *m_beside = sums((payload, beside), True, *m_own)
    part, near2, above, below = lax.optimization_barrier((part, near2, above, below))
    line = (above, below, near2)
    other = [lax.ppermute(c, "rows", swap) for c in line]
    part, *m_line = sums(line, False, part)
    part, *m_other = sums(other, False, part)
    passed = call(line_end, floats(*payload.shape), 2)(below, above)
    part, passed = lax.optimization_barrier((part, passed))
    parts = lax.all_to_all(part.reshape(group, 2 * own_waves, width), (Z, Y), 0, 0, tiled=True)
    scale = 1.0 / math.sqrt(float(slots * devices) * float(waves * rows * nx))
    spread = call(filtered(scale), floats(*parts.shape), 2)(parts, filters)
    f = lax.all_to_all(spread, (Z, Y), 0, 0, tiled=True).reshape(2 * waves, width)

    one = floats(width, slots)

    def back(chunks, ft, m, *added, stacked=False):
        count = len(chunks)
        outs = floats(count, width, slots) if stacked else (one,) * count
        kernel = backward(chunks, stacked, bool(added))
        return call(kernel, outs, 6 + len(added), flops=count * unit)(*ft, *m, *added)

    theirs = *m_beside, *m_other
    mine = *m_own, *m_line
    outs = floats(1, width, slots), *(halves(width, 2 * waves),) * 2
    far, *ft = call(backward_first(2), outs, 3, flops=unit)(f, *m_other)
    there = lax.ppermute(far, "rows", swap)
    ft = lax.optimization_barrier((*ft, far))[:2]
    rest = back(((0, 0), (1, 0), (1, 1)), ft, theirs, stacked=True)
    (e3,) = back(((1, 2),), ft, mine, there)
    e3, passed, rest, *ft = lax.optimization_barrier((e3, passed, rest, *ft))
    rest = lax.ppermute(rest, "rows", swap)
    e3 = lax.ppermute(e3, X, shift(X, 2))
    ends = [(d, (d + nx) % devices) for d in range(devices) if d % nx == 0]
    ends += [(d, (d - nx) % devices) for d in range(devices) if d % nx == nx - 1]
    edge = lax.ppermute(passed, ROWS_WAVES, ends)
    e0, e1, e2 = back(((0, 0), (1, 0), (1, 1)), ft, mine, rest)
    e1 = lax.ppermute(e1, X, shift(X, 1))
    e2 = lax.ppermute(e2, X, shift(X, -1))

    sizes = cells, cell, cells * devices, neighbours.shape[1], nx - 1
    sizes = cells, cell, cells * devices, neighbours.shape[1], nx - 1
    small = floats(slots, 128), floats(slots, 8), floats(16, 128)
    outs = floats(slots, width), *small, *(halves(width, width),) * 6
    base, mask, cols, factors, w0, w1, *w = call(messages(*sizes), outs, 8, smem=(0, 1))(
        neighbours, nbr_count, payload, below, above, w_msg, w_one, w_two
    )
    base = call(end_messages(cells, cell, nx - 1), floats(slots, width), 7, alias={0: 0})(
        base, mask, cols, factors, edge, w0, w1
    )
    (e0,) = call(pairs, (one,), 2)(e0, e3)
    return call(finish(), floats(slots, width), 9)(base, mask, e0, e1, e2, *w)


def solution(mesh):
    torus = Mesh(mesh.devices.reshape(mesh.shape["rows"], 4, 4, 4), ROWS_WAVES)
    return jax.shard_map(
        shards,
        mesh=torus,
        in_specs=(
            P(ROWS_WAVES, None),
            P(None, ROWS_WAVES),
            P(ROWS_WAVES),
            P(ROWS_WAVES, None),
            P(ROWS_WAVES),
            P(None, WAVES),
            P(WAVES, None),
            P(),
            P(),
            P(),
            P(),
        ),
        out_specs=P(ROWS_WAVES, None),
        check_vma=False,
    )
```

```python
import math

import jax
import jax.numpy as jnp
from jax import lax
from jax.experimental import pallas as pl
from jax.experimental.pallas import tpu as pltpu
from jax.sharding import Mesh
from jax.sharding import PartitionSpec as P

Z, Y, X = "waves_0", "waves_1", "waves_2"
WAVES = (Z, Y, X)
ROWS_WAVES = ("rows", Z, Y, X)
F32 = jnp.float32
BF16 = jnp.bfloat16

SIN_POLY = (6.283185280154403, -10.33542015333633, 5.100154773052372, -1.1965808225334407, 0.15531182448662934)
COS_POLY = (0.999999953027512, -4.934792802489427, 4.058410790762133, -1.3318729727851486, 0.21968242357146)
ROUNDER = 12582912.0


def horner(coeffs, u):
    out = coeffs[-1]
    for c in coeffs[-2::-1]:
        out = out * u + c
    return out


def split(a):
    high = a.astype(BF16)
    return high, (a - high.astype(F32)).astype(BF16)


def thirds(a):
    high = a.astype(BF16).astype(F32)
    rest = a - high
    middle = rest.astype(BF16).astype(F32)
    return high, middle, rest - middle


def dot(a, b):
    return jnp.dot(a, b, preferred_element_type=F32)


def dot3(a, b):
    return dot(a[0], b[0]) + (dot(a[1], b[0]) + dot(a[0], b[1]))


def call(kernel, outs, n_in, scratch=(), smem=(), flops=0, alias={}, limit=8 << 20):
    def space(i):
        return pltpu.SMEM if i in smem else pltpu.VMEM

    return pl.pallas_call(
        kernel,
        out_shape=outs,
        in_specs=[pl.BlockSpec(memory_space=space(i)) for i in range(n_in)],
        out_specs=jax.tree.map(lambda _: pl.BlockSpec(memory_space=pltpu.VMEM), outs),
        scratch_shapes=scratch,
        input_output_aliases=alias,
        cost_estimate=pl.CostEstimate(flops=flops, bytes_accessed=1 << 16, transcendentals=0),
        compiler_params=pltpu.CompilerParams(vmem_limit_bytes=limit),
    )


def live_rows(block, cells, cell):
    slots = cells * cell
    row = lax.broadcasted_iota(jnp.int32, (slots, 1), 0).astype(F32)
    limit = block[slots + 3 : slots + 4, 0:1]
    for c in range(1, cells):
        limit = jnp.where(row < c * cell, limit, c * cell + block[slots + 3 : slots + 4, c : c + 1])
    return row < limit


def stamp(slots, cells):
    def kernel(counts, _, out):
        out[slots + 3 : slots + 4, 0:cells] = counts[...].astype(F32).reshape(1, cells)

    return kernel


def lattice(own, groups):
    def kernel(kv, out, flat):
        flat[...] = jnp.zeros(flat.shape, F32)
        pad = jnp.zeros((8, flat.shape[1] - 128), F32)
        for g in range(groups):
            flat[...] += pltpu.roll(jnp.concatenate([kv[g], pad], axis=1), g * own, 1)
        kh, km, kl = thirds(flat[...])
        out[...] = jnp.concatenate([kh, kh, km, kh, km, kl], axis=0).T.astype(BF16)

    return kernel


def pack(slots, own, groups):
    def kernel(own_block, out):
        rows = own_block[slots : slots + 8, :128] * (0.5 / math.pi)
        rows = pltpu.roll(rows, 4, 0)
        k = jnp.where(lax.axis_index("rows") == 0, rows, pltpu.roll(rows, 128 - own, 1))
        lane = lax.broadcasted_iota(jnp.int32, k.shape, 1)
        line = lax.broadcasted_iota(jnp.int32, k.shape, 0)
        k = jnp.where((lane < own) & (line < 3), k, 0.0)
        for g in range(groups):
            out[g] = k

    return kernel


def own_trig(slots, own, groups):
    def kernel(lhs, chunk, mh, ml):
        turns = dot(lhs[...], spots(chunk, slots))
        for g in range(groups):
            rows = slice(2 * own * g, 2 * own * (g + 1))
            mh[0, rows], ml[0, rows] = split(cos_and_sin(turns[g * own : (g + 1) * own]))

    return kernel


def spots(chunk, slots):
    x, y, z = thirds(jnp.where(lax.broadcasted_iota(jnp.int32, (8, slots), 0) < 3, chunk[slots : slots + 8], 0.0))
    return jnp.concatenate([x, y, x, z, y, x], axis=0).astype(BF16)


def cos_and_sin(t):
    f = t - ((t + ROUNDER) - ROUNDER)
    u = f * f
    s = f * horner(SIN_POLY, u)
    c = horner(COS_POLY, u)
    return jnp.concatenate([1.0 - 0.5 * (s * s), s * c], axis=0)


def forward(cells, cell, count, own, groups, first):
    slots = cells * cell

    def kernel(lhs, w_val, *refs):
        chunks, refs = refs[:count], refs[count:]
        if first:
            ready, refs = refs[:2], refs[2:]
        else:
            before, refs = refs[0], refs[1:]
        out, mh, ml = refs
        skip = 1 if first else 0
        w = split(w_val[...])
        turns, right = [], []
        for j, chunk in enumerate(chunks):
            live = live_rows(chunk, cells, cell)
            vh, vl = split(jnp.where(live, dot3(split(chunk[:slots]), w), 0.0))
            right += [vh, vh, vl]
            turns.append(dot(lhs[...], spots(chunk, slots)) if j >= skip else None)
        right = jnp.concatenate(right, axis=0)
        for begin, stop in ((0, groups // 2), (groups // 2, groups)):
            for j in range(skip, count):
                for g in range(begin, stop):
                    rows = slice(2 * own * g, 2 * own * (g + 1))
                    pieces = split(cos_and_sin(turns[j][g * own : (g + 1) * own]))
                    mh[j - skip, rows], ml[j - skip, rows] = pieces
            rows = slice(2 * own * begin, 2 * own * stop)
            pairs_of = [(ready[0][0, rows], ready[1][0, rows])] if first else []
            pairs_of += [(mh[j, rows], ml[j, rows]) for j in range(count - skip)]
            left = [m for high, low in pairs_of for m in (high, low, high)]
            total = dot(jnp.concatenate(left, axis=1), right)
            out[rows] = total if first else before[rows] + total

    return kernel


def filtered(scale):
    def kernel(parts, filters, out):
        groups, double, _ = parts.shape
        own = double // 2
        f = jnp.where(lax.axis_index("rows") == 0, filters[:own], filters[own:]) * scale
        total = parts[0]
        for g in range(1, groups):
            total = total + parts[g]
        total = total * jnp.concatenate([f, f], axis=0)
        for g in range(groups):
            out[g] = total

    return kernel


def line_end(below, above, out):
    out[...] = jnp.where(lax.axis_index(X) == 0, below[...], above[...])


def backward_first(at):
    def kernel(f, mh, ml, out, high, low):
        ft = split(f[...].T)
        high[...], low[...] = ft
        out[0] = dot3(ft, (mh[at], ml[at]))

    return kernel


def backward(chunks, stacked, adds):
    def kernel(fh, fl, mh0, ml0, mh1, ml1, *refs):
        added, outs = refs[0] if adds else None, refs[1:] if adds else refs
        for j, (rest, at) in enumerate(chunks):
            part = dot3((fh[...], fl[...]), (mh1[at], ml1[at]) if rest else (mh0[at], ml0[at]))
            part = part + added[j] if adds else part
            if stacked:
                outs[0][j] = part
            else:
                outs[j][...] = part

    return kernel


def pairs(*refs):
    count = len(refs) // 3
    for a, b, out in zip(refs[:count], refs[count : 2 * count], refs[2 * count :]):
        out[...] = a[...] + b[...]


def listed_factor(neighbours, nbr_count, c, target, nb):
    listed = jnp.float32(0.0)
    for b in range(nb):
        hit = (neighbours[c, b] == target) & (b < nbr_count[c])
        listed = listed + jnp.where(hit, jnp.float32(1.0), jnp.float32(0.0))
    return listed


def gather(factor, mine, blocks, use, cells, cell):
    slots = cells * cell
    wide, pos = {}, {}
    for k in use:
        live = live_rows(blocks[k], cells, cell)
        halves = split(jnp.where(live, blocks[k][:slots], 0.0))
        for c in range(cells):
            wide[k * cells + c] = tuple(p[c * cell : (c + 1) * cell] for p in halves)
            pos[k * cells + c] = blocks[k][slots : slots + 3, c * cell : (c + 1) * cell]
    eye = lax.broadcasted_iota(jnp.int32, (cell, cell), 0) == lax.broadcasted_iota(jnp.int32, (cell, cell), 1)
    gathered = []
    for c in range(cells):
        here = mine[c * cell : (c + 1) * cell]
        acc = jnp.zeros((cell, blocks[use[0]].shape[1]), F32)
        for step in range(2 * cells + 1):
            other = c + step
            if other not in wide:
                continue
            near = pos[other]
            d0 = here[:, 0:1] - near[0:1]
            d1 = here[:, 1:2] - near[1:2]
            d2 = here[:, 2:3] - near[2:3]
            weight = jnp.exp(-0.125 * (d0 * d0 + d1 * d1 + d2 * d2))
            weight = weight * factor(c, other)
            if step == cells:
                weight = jnp.where(eye, 0.0, weight)
            acc = acc + dot3(split(weight), wide[other])
        gathered.append(acc)
    return jnp.concatenate(gathered, axis=0)


def messages(cells, cell, cells_all, nb, last):
    slots = cells * cell

    def kernel(neighbours, nbr_count, own, low, high, w_msg, w_one, w_two, out, mask, cols, factors, *parts):
        x = lax.axis_index(X)
        lo = jnp.where(x == 0, 0.0, low[...])
        hi = jnp.where(x == last, 0.0, high[...])
        blocks = lo, own[...], hi
        mine = own[slots : slots + 8].T
        cols[...] = mine
        for k, w in enumerate((w_msg, w_one, w_two)):
            parts[2 * k][...], parts[2 * k + 1][...] = split(w[...])
        first = lax.axis_index(ROWS_WAVES) * cells

        def factor(c, other):
            target = lax.rem(first + other - cells + cells_all, cells_all)
            listed = listed_factor(neighbours, nbr_count, c, target, nb)
            row = 3 * cells * c + other
            factors[row : row + 1] = jnp.full((1, 128), listed)
            return listed

        total = gather(factor, mine, blocks, (0, 1, 2), cells, cell)
        live = live_rows(own, cells, cell)
        msg = 0.125 * dot3(split(total), (parts[0][...], parts[1][...]))
        out[...] = own[:slots] + jnp.where(live, msg, 0.0)
        mask[...] = jnp.broadcast_to(jnp.where(live, 1.0, 0.0), mask.shape)

    return kernel


def end_messages(cells, cell, last):
    def kernel(_, mask, cols, factors, edge, wh, wl, out):
        x = lax.axis_index(X)
        for at, side in ((0, 0), (last, 2)):

            @pl.when(x == at)
            def _(side=side):
                blocks = {side: edge[...]}

                def factor(c, other):
                    row = 3 * cells * c + other
                    return factors[row : row + 1, 0:1]

                total = gather(factor, cols[...], blocks, (side,), cells, cell)
                msg = 0.125 * dot3(split(total), (wh[...], wl[...]))
                out[...] = out[...] + msg * mask[:, 0:1]

    return kernel


def finish():
    def kernel(base, mask, a, b, c, oh, ol, th, tl, out):
        spectral = a[...] + (b[...] + c[...])
        u = base[...] + spectral.T
        normed = u / jnp.sqrt(jnp.mean(u * u, axis=1, keepdims=True) + 1e-06)
        v = dot3(split(normed), (oh[...], ol[...]))
        hidden = v / (1.0 + jnp.exp(-v))
        out[...] = (u + dot3(split(hidden), (th[...], tl[...]))) * mask[:, 0:1]

    return kernel


def shift(axis, by):
    size = lax.axis_size(axis)
    return [(i, (i + by) % size) for i in range(size)]


def shards(
    feats, positions, cell_counts, neighbours, nbr_count, kvec, filters, w_msg, w_val, w_one, w_two
):
    cells = cell_counts.shape[0]
    slots, width = feats.shape
    cell = slots // cells
    devices = lax.axis_size(ROWS_WAVES)
    nx = lax.axis_size(X)
    rows = lax.axis_size("rows")
    group = lax.axis_size((Z, Y))
    own_waves = kvec.shape[1] // rows
    waves = own_waves * group

    def floats(*dims):
        return jax.ShapeDtypeStruct(dims, F32)

    def halves(*dims):
        return jax.ShapeDtypeStruct(dims, BF16)

    payload = jnp.pad(feats, ((0, 8), (0, 0))) + jnp.pad(positions, ((slots, 5), (0, 0)))
    payload = payload + jnp.pad(kvec, ((slots + 4, 1), (0, width - kvec.shape[1])))
    kv = call(pack(slots, own_waves, group), floats(group, 8, 128), 1)(payload)
    kv, payload = lax.optimization_barrier((kv, payload))
    payload = call(stamp(slots, cells), floats(*payload.shape), 2, alias={1: 0})(cell_counts, payload)
    near2 = lax.ppermute(payload, X, shift(X, 2))
    above = lax.ppermute(payload, X, shift(X, -1))
    below = lax.ppermute(payload, X, shift(X, 1))
    kv, again = lax.optimization_barrier((kv, payload))
    swap = shift("rows", 1)
    beside = lax.ppermute(again, "rows", swap)
    kv = lax.all_to_all(kv, (Z, Y), 0, 0, tiled=True)
    lhs = call(lattice(own_waves, group), halves(waves, 48), 1, [pltpu.VMEM((8, waves), F32)])(kv)

    unit = 12 * waves * slots * width

    def sums(chunks, first, *more):
        count = len(chunks)
        m = halves(count - 1 if first else count, 2 * waves, slots)
        return call(
            forward(cells, cell, count, own_waves, group, first),
            (floats(2 * waves, width), m, m),
            2 + count + len(more),
            flops=count * unit,
        )(lhs, w_val, *chunks, *more)

    m_own = call(own_trig(slots, own_waves, group), (halves(1, 2 * waves, slots),) * 2, 2, flops=unit)(lhs, payload)
    part, *m_beside = sums((payload, beside), True, *m_own)
    part, near2, above, below = lax.optimization_barrier((part, near2, above, below))
    line = (above, below, near2)
    other = [lax.ppermute(c, "rows", swap) for c in line]
    part, *m_line = sums(line, False, part)
    part, *m_other = sums(other, False, part)
    passed = call(line_end, floats(*payload.shape), 2)(below, above)
    part, passed = lax.optimization_barrier((part, passed))
    parts = lax.all_to_all(part.reshape(group, 2 * own_waves, width), (Z, Y), 0, 0, tiled=True)
    scale = 1.0 / math.sqrt(float(slots * devices) * float(waves * rows * nx))
    spread = call(filtered(scale), floats(*parts.shape), 2)(parts, filters)
    f = lax.all_to_all(spread, (Z, Y), 0, 0, tiled=True).reshape(2 * waves, width)

    one = floats(width, slots)

    def back(chunks, ft, m, *added, stacked=False):
        count = len(chunks)
        outs = floats(count, width, slots) if stacked else (one,) * count
        kernel = backward(chunks, stacked, bool(added))
        return call(kernel, outs, 6 + len(added), flops=count * unit)(*ft, *m, *added)

    theirs = *m_beside, *m_other
    mine = *m_own, *m_line
    outs = floats(1, width, slots), *(halves(width, 2 * waves),) * 2
    far, *ft = call(backward_first(2), outs, 3, flops=unit)(f, *m_other)
    there = lax.ppermute(far, "rows", swap)
    ft = lax.optimization_barrier((*ft, far))[:2]
    rest = back(((0, 0), (1, 0), (1, 1)), ft, theirs, stacked=True)
    (e3,) = back(((1, 2),), ft, mine, there)
    e3, passed, rest, *ft = lax.optimization_barrier((e3, passed, rest, *ft))
    rest = lax.ppermute(rest, "rows", swap)
    e3 = lax.ppermute(e3, X, shift(X, 2))
    ends = [(d, (d + nx) % devices) for d in range(devices) if d % nx == 0]
    ends += [(d, (d - nx) % devices) for d in range(devices) if d % nx == nx - 1]
    edge = lax.ppermute(passed, ROWS_WAVES, ends)
    e0, e1, e2 = back(((0, 0), (1, 0), (1, 1)), ft, mine, rest)
    e1 = lax.ppermute(e1, X, shift(X, 1))
    e2 = lax.ppermute(e2, X, shift(X, -1))

    sizes = cells, cell, cells * devices, neighbours.shape[1], nx - 1
    sizes = cells, cell, cells * devices, neighbours.shape[1], nx - 1
    small = floats(slots, 128), floats(slots, 8), floats(16, 128)
    outs = floats(slots, width), *small, *(halves(width, width),) * 6
    base, mask, cols, factors, w0, w1, *w = call(messages(*sizes), outs, 8, smem=(0, 1))(
        neighbours, nbr_count, payload, below, above, w_msg, w_one, w_two
    )
    base = call(end_messages(cells, cell, nx - 1), floats(slots, width), 7, alias={0: 0})(
        base, mask, cols, factors, edge, w0, w1
    )
    (e0,) = call(pairs, (one,), 2)(e0, e3)
    return call(finish(), floats(slots, width), 9)(base, mask, e0, e1, e2, *w)


def solution(mesh):
    torus = Mesh(mesh.devices.reshape(mesh.shape["rows"], 4, 4, 4), ROWS_WAVES)
    return jax.shard_map(
        shards,
        mesh=torus,
        in_specs=(
            P(ROWS_WAVES, None),
            P(None, ROWS_WAVES),
            P(ROWS_WAVES),
            P(ROWS_WAVES, None),
            P(ROWS_WAVES),
            P(None, WAVES),
            P(WAVES, None),
            P(),
            P(),
            P(),
            P(),
        ),
        out_specs=P(ROWS_WAVES, None),
        check_vma=False,
    )
```
